32 devices in a mesh: rep: 2 (over x), head: 8 (over z, y), seq: 2 (over core).
Axes of the slice: x: 2, y: 2, z: 4, core: 2. Of those that a mesh axis runs over, the one named last changes fastest.
Arguments:
- q_span: bfloat16 [512, 4096], P(('rep', 'head', 'seq')), parts along dimension 0, may hold values from -6 to 6
- k_span: bfloat16 [512, 1024], P(('rep', 'head', 'seq')), parts along dimension 0, may hold values from -6 to 6
- v_span: bfloat16 [512, 1024], P(('rep', 'head', 'seq')), parts along dimension 0, may hold values from -6 to 6
- k_cache: bfloat16 [16, 8192, 128], P(('rep', 'head'), 'seq'), parts along dimension 0, may hold values from -6 to 6
- v_cache: bfloat16 [16, 8192, 128], P(('rep', 'head'), 'seq'), parts along dimension 0, may hold values from -6 to 6
- head_list: int32 [16], P('rep'), parts along dimension 0, may hold values from 0 to 7, each once
- retrieval: int32 [16], P('rep'), parts along dimension 0, may hold values from 0 to 1
- windows: int32 [16], P('rep'), parts along dimension 0, may hold values from 2049 to 4096
- sinks: int32 [16], P('rep'), parts along dimension 0, may hold values from 1 to 64
Outputs:
- attn_out: bfloat16 [512, 4096], P(('rep', 'head', 'seq')), parts along dimension 0
The draws below stay inside these ranges and needn't reach their ends.
There are 2 independent parts, one for each index of `rep`. The reference program is written for one: setup_inputs(seed, part) draws one part's arguments, and reference() takes and returns one part's arrays. A program takes and returns all parts, laid end to end along the dimension named above; each array names one. Nothing has to cross between parts.
Inputs may be any that keep to these rules, and one draw needn't show every extreme that they name: `head_list`: each kv head stands in exactly one slot.
All inputs are finite; a program needn't handle non-finite values.
Results may differ from the reference program's by a relative error of at most 0.0055.
Values may be sent and summed in bfloat16 or wider, within the bound.
No kernel may reach another device: no remote copies, remote signals or barrier semaphores. Data moves between devices by JAX's collectives and lax.ppermute only.
A program may use at most 64 MiB of HBM per device.

```python
import jax
import jax.numpy as jnp
from jax import lax

H = 32
KVH = 8
DH = 128
HPG = 4
QUART = 1
Q = 256
CTX_DEV = 4096
SEG = 8192
CTX = 8192
SINK_MAX = 64


def draw_retrieval(key, part):
    inner_key = jax.random.fold_in(key, 7)
    retr_count = jax.random.randint(jax.random.fold_in(inner_key, 1), (), 1, KVH)
    ranking = jax.random.permutation(jax.random.fold_in(inner_key, 2), KVH).astype(jnp.int32)
    rank_of = jnp.argsort(ranking, stable=True).astype(jnp.int32)
    return (rank_of < retr_count).astype(jnp.int32)


def draw_q_span(key, part):
    values = jnp.clip(1.7 * jax.random.normal(jax.random.fold_in(key, 41), (Q, H * DH), jnp.float32), -6.0, 6.0)
    return values.astype(jnp.bfloat16)


def draw_k_cache(key, part):
    values = jnp.clip(1.7 * jax.random.normal(jax.random.fold_in(key, 43), (KVH * QUART, SEG, DH), jnp.float32), -6.0, 6.0)
    return values.astype(jnp.bfloat16)


def plant(drawn, stream_key, low, top_value):
    spot = [jax.random.randint(jax.random.fold_in(stream_key, axis), (), 0, length) for axis, length in enumerate(drawn.shape)]
    main_axis = drawn.shape.index(max(drawn.shape))
    beside = spot[:main_axis] + [(spot[main_axis] + 1) % drawn.shape[main_axis]] + spot[main_axis + 1:]
    return drawn.at[tuple(spot)].set(low).at[tuple(beside)].set(top_value)


def block_levels(key, extent, shards, least, top_value):
    def one(axis_at, blocks):
        heights = jax.random.uniform(jax.random.fold_in(jax.random.fold_in(key, 6), axis_at), (blocks,), jnp.float32, least / len(shards), top_value / len(shards))
        return jnp.repeat(jnp.exp(heights), extent[axis_at] // blocks).reshape((-1,) + (1,) * (len(extent) - axis_at - 1))

    level = one(*shards[0])
    for cut in shards[1:]:
        level = level * one(*cut)
    return level


def gaussian(own_key, extent, width, limit, split=(), kind=jnp.bfloat16):
    factor_of = block_levels(own_key, extent, split, -0.22, 0.18) if split else 1.0
    values = jax.random.normal(own_key, extent, jnp.float32) * width * factor_of
    return jnp.minimum(jnp.maximum(values, -limit), limit).astype(kind)


def setup_inputs(seed: int = 0, part: int = 0) -> dict:
    key_list = jax.random.split(jax.random.key(seed), 10)
    part_splits = jax.random.split(jax.random.fold_in(key_list[9], part), 10)
    q_span = draw_q_span(jax.random.fold_in(jax.random.fold_in(key_list[9], part), 71), part)
    k_span = gaussian(part_splits[1], (Q, KVH * DH), 1.7, 6.0, ((0, 16),))
    v_span = gaussian(part_splits[2], (Q, KVH * DH), 1.0, 6.0, ((0, 16),))
    k_cache = draw_k_cache(jax.random.fold_in(jax.random.fold_in(key_list[9], part), 71), part)
    v_cache = gaussian(part_splits[4], (KVH * QUART, SEG, DH), 1.0, 6.0, ((0, 8), (1, 2)))
    head_list = jax.random.permutation(part_splits[5], KVH).astype(jnp.int32)
    retrieval = draw_retrieval(jax.random.fold_in(jax.random.fold_in(key_list[9], part), 71), part)
    windows = plant(jax.random.randint(part_splits[7], (KVH,), CTX_DEV // 2 + 1, CTX_DEV + 1), jax.random.fold_in(part_splits[7], 1), CTX_DEV // 2 + 1, CTX_DEV).astype(jnp.int32)
    sinks = plant(jax.random.randint(part_splits[8], (KVH,), 1, SINK_MAX + 1), jax.random.fold_in(part_splits[8], 1), 1, SINK_MAX).astype(jnp.int32)
    return {"q_span": q_span, "k_span": k_span, "v_span": v_span, "k_cache": k_cache, "v_cache": v_cache, "head_list": head_list, "retrieval": retrieval, "windows": windows, "sinks": sinks}


def head_output(queries, key_rows, value_rows, is_retrieval, window_len, sink_len):
    score_scale = 1.0 / (DH ** 0.5)
    scores = jnp.dot(queries, key_rows.T, preferred_element_type=jnp.float32) * score_scale
    query_pos = CTX + jnp.arange(Q, dtype=jnp.int32)
    key_pos = jnp.arange(CTX + Q, dtype=jnp.int32)
    allowed = (key_pos[None, :] <= query_pos[:, None]) & ((is_retrieval == 1) | (key_pos[None, :] < sink_len) | (key_pos[None, :] > query_pos[:, None] - window_len))
    top_score = jnp.max(jnp.where(allowed, scores, -1e30), axis=1)
    weights = jnp.where(allowed, jnp.exp(scores - top_score[:, None]), 0.0)
    totals = jnp.sum(weights, axis=1)
    weighted = jnp.dot(weights.astype(jnp.bfloat16), value_rows, preferred_element_type=jnp.float32)
    return weighted / totals[:, None]


def reference(q_span, k_span, v_span, k_cache, v_cache, head_list, retrieval, windows, sinks):
    cache_keys = k_cache.reshape(KVH, CTX, DH)
    cache_values = v_cache.reshape(KVH, CTX, DH)

    def per_slot(packed):
        slot_keys, slot_values, kv_group = packed
        kv_group = kv_group.astype(jnp.int32)
        key_rows = jnp.concatenate([slot_keys, lax.dynamic_slice_in_dim(k_span, kv_group * DH, DH, 1)], axis=0)
        value_rows = jnp.concatenate([slot_values, lax.dynamic_slice_in_dim(v_span, kv_group * DH, DH, 1)], axis=0)
        queries = lax.dynamic_slice_in_dim(q_span, kv_group * (HPG * DH), HPG * DH, 1)
        queries = queries.reshape(Q, HPG, DH).transpose(1, 0, 2)
        is_retrieval = jnp.take(retrieval, kv_group)
        window_len = jnp.take(windows, kv_group)
        sink_len = jnp.take(sinks, kv_group)

        def one_head(head_queries):
            return head_output(head_queries, key_rows, value_rows, is_retrieval, window_len, sink_len)

        return lax.map(one_head, queries)

    slot_out = lax.map(per_slot, (cache_keys, cache_values, head_list))
    matches = (head_list[:, None] == jnp.arange(KVH, dtype=jnp.int32)[None, :]).astype(jnp.int32)
    inverse = jnp.sum(jnp.arange(KVH, dtype=jnp.int32)[:, None] * matches, axis=0).astype(jnp.int32)
    by_group = jnp.take(slot_out, inverse, axis=0)
    return by_group.transpose(2, 0, 1, 3).reshape(Q, H * DH).astype(jnp.bfloat16)
```

```python
import functools
import math

import jax
import jax.numpy as jnp
from jax import lax
from jax.experimental import pallas as pl
from jax.experimental.pallas import tpu as pltpu
from jax.sharding import PartitionSpec as P

KVH = 8


NEG_FILL = -1e30


def absorb(
    running,
    query_rows,
    query_pos,
    key_rows,
    value_rows,
    key_pos,
    is_retrieval,
    window_len,
    sink_len,
    score_scale,
):
    top_score, totals, weighted = running
    scores = jnp.dot(query_rows, key_rows.T, preferred_element_type=jnp.float32) * score_scale
    allowed = (key_pos[None, :] <= query_pos[:, None]) & (
        (is_retrieval == 1)
        | (key_pos[None, :] < sink_len)
        | (key_pos[None, :] > query_pos[:, None] - window_len)
    )
    block_top = jnp.max(jnp.where(allowed, scores, NEG_FILL), axis=1)
    new_top = jnp.maximum(top_score, block_top)
    weights = jnp.where(allowed, jnp.exp(scores - new_top[:, None]), 0.0)
    rescale = jnp.exp(top_score - new_top)
    totals = totals * rescale + jnp.sum(weights, axis=1)
    weighted = weighted * rescale[:, None] + jnp.dot(
        weights.astype(jnp.bfloat16), value_rows, preferred_element_type=jnp.float32
    )
    return (new_top, totals, weighted)


def finish_rows(received, spread, head_list, tok_rows, head_dim):
    top_score, totals, weighted = received
    group_heads = top_score.shape[-1]
    top_score = top_score.reshape(KVH, spread, tok_rows, group_heads)
    totals = totals.reshape(KVH, spread, tok_rows, group_heads)
    weighted = weighted.reshape(KVH, spread, tok_rows, group_heads, head_dim)
    overall = jnp.max(top_score, axis=1, keepdims=True)
    factor = jnp.exp(top_score - overall)
    summed = jnp.sum(totals * factor, axis=1)
    combined = jnp.sum(weighted * factor[..., None], axis=1)
    result = combined / summed[..., None]
    matches = (head_list[:, None] == jnp.arange(KVH, dtype=jnp.int32)[None, :]).astype(jnp.int32)
    inverse = jnp.sum(jnp.arange(KVH, dtype=jnp.int32)[:, None] * matches, axis=0)
    by_group = jnp.take(result, inverse, axis=0)
    return (
        by_group.transpose(1, 0, 2, 3)
        .reshape(tok_rows, KVH * group_heads * head_dim)
        .astype(jnp.bfloat16)
    )


def on_device_quarters(q_span, k_span, v_span, k_cache, v_cache, head_list, retrieval, windows, sinks):
    head_count = lax.axis_size("head")
    pair_count = lax.axis_size("seq")
    quarters = head_count // KVH
    tok_rows = q_span.shape[0]
    group_width = q_span.shape[1] // KVH
    head_dim = k_cache.shape[2]
    group_heads = group_width // head_dim
    ctx_dev = k_cache.shape[1]
    total_q = tok_rows * head_count * pair_count
    context = ctx_dev * pair_count * quarters
    head_at = lax.axis_index("head")
    pair_at = lax.axis_index("seq")
    slot_index = head_at // quarters
    quarter = head_at % quarters
    kv_group = jnp.take(head_list, slot_index)
    q_groups = q_span.reshape(tok_rows, KVH, group_width)
    kv_groups = jnp.concatenate(
        [k_span.reshape(tok_rows, KVH, head_dim), v_span.reshape(tok_rows, KVH, head_dim)], axis=2
    )
    targets = jnp.take(head_list, jnp.arange(head_count * pair_count) // pair_count // quarters)
    q_send = jnp.take(q_groups, targets, axis=1)
    kv_send = jnp.take(kv_groups, targets, axis=1)
    q_recv, kv_recv = (
        lax.all_to_all(q_send, ("head", "seq"), split_axis=1, concat_axis=0, tiled=True),
        lax.all_to_all(kv_send, ("head", "seq"), split_axis=1, concat_axis=0, tiled=True),
    )
    queries = q_recv.reshape(total_q, group_width)
    span_kv = kv_recv.reshape(total_q, 2 * head_dim)
    query_rows = queries.reshape(total_q * group_heads, head_dim)
    query_pos = context + jnp.arange(total_q * group_heads, dtype=jnp.int32) // group_heads
    is_retrieval = jnp.take(retrieval, kv_group)
    window_len = jnp.take(windows, kv_group)
    sink_len = jnp.take(sinks, kv_group)
    score_scale = 1.0 / math.sqrt(head_dim)
    row_total = total_q * group_heads
    running = (
        jnp.full((row_total,), NEG_FILL, jnp.float32),
        jnp.zeros((row_total,), jnp.float32),
        jnp.zeros((row_total, head_dim), jnp.float32),
    )
    key_block = min(512, ctx_dev)
    segment = quarter * pair_count + pair_at
    first_key = segment * ctx_dev
    cache_keys = k_cache[0]
    cache_values = v_cache[0]

    def key_step(step_index, state):
        start = step_index * key_block
        key_rows = lax.dynamic_slice_in_dim(cache_keys, start, key_block, 0)
        value_rows = lax.dynamic_slice_in_dim(cache_values, start, key_block, 0)
        key_pos = first_key + start + jnp.arange(key_block, dtype=jnp.int32)
        return absorb(
            state,
            query_rows,
            query_pos,
            key_rows,
            value_rows,
            key_pos,
            is_retrieval,
            window_len,
            sink_len,
            score_scale,
        )

    running = lax.fori_loop(0, ctx_dev // key_block, key_step, running)
    span_piece = total_q // (quarters * pair_count)
    span_start = segment * span_piece
    span_rows = lax.dynamic_slice_in_dim(span_kv, span_start, span_piece, 0)
    span_pos = context + span_start + jnp.arange(span_piece, dtype=jnp.int32)
    top_score, totals, weighted = absorb(
        running,
        query_rows,
        query_pos,
        span_rows[:, :head_dim],
        span_rows[:, head_dim:],
        span_pos,
        is_retrieval,
        window_len,
        sink_len,
        score_scale,
    )
    received = (
        lax.all_to_all(
            top_score.reshape(head_count * pair_count, tok_rows, group_heads),
            ("head", "seq"),
            split_axis=0,
            concat_axis=0,
            tiled=True,
        ),
        lax.all_to_all(
            totals.reshape(head_count * pair_count, tok_rows, group_heads),
            ("head", "seq"),
            split_axis=0,
            concat_axis=0,
            tiled=True,
        ),
        lax.all_to_all(
            weighted.reshape(head_count * pair_count, tok_rows, group_width),
            ("head", "seq"),
            split_axis=0,
            concat_axis=0,
            tiled=True,
        ),
    )
    spread = quarters * pair_count
    return finish_rows(received, spread, head_list, tok_rows, head_dim)


VMEM_SPEC = pl.BlockSpec(memory_space=pltpu.VMEM)
SMEM_SPEC = pl.BlockSpec(memory_space=pltpu.SMEM)


def pack_kernel(head_ref, q_ref, k_ref, v_ref, out_ref, *, group_width, head_dim):
    for slot in range(out_ref.shape[0]):
        group = head_ref[slot]
        q_start = pl.multiple_of(group * group_width, 128)
        kv_start = pl.multiple_of(group * head_dim, 128)
        out_ref[slot, :, :group_width] = q_ref[:, pl.ds(q_start, group_width)]
        out_ref[slot, :, group_width : group_width + head_dim] = k_ref[:, pl.ds(kv_start, head_dim)]
        out_ref[slot, :, group_width + head_dim :] = v_ref[:, pl.ds(kv_start, head_dim)]


def unpack_kernel(head_ref, in_ref, out_ref):
    width = in_ref.shape[2]
    for slot in range(in_ref.shape[0]):
        start = pl.multiple_of(head_ref[slot] * width, 128)
        out_ref[:, pl.ds(start, width)] = in_ref[slot]


def attend_kernel(
    head_ref,
    retrieval_ref,
    window_ref,
    sink_ref,
    recv_ref,
    peer_ref,
    k_peer,
    v_peer,
    k_source,
    v_source,
    out_ref,
    k_own,
    v_own,
    score_ref,
    top_ref,
    total_ref,
    acc_ref,
    own_sem,
    *,
    tok_rows,
    group_heads,
    head_dim,
    key_block,
    row_block,
):
    k_copy = pltpu.make_async_copy(k_source, k_own, own_sem.at[0])
    v_copy = pltpu.make_async_copy(v_source, v_own, own_sem.at[1])
    k_copy.start()
    v_copy.start()
    pair_at = lax.axis_index("seq")
    kv_group = head_ref[lax.axis_index("head")]
    is_retrieval = retrieval_ref[kv_group]
    window_len = window_ref[kv_group]
    sink_len = sink_ref[kv_group]
    tokens = recv_ref.shape[0]
    rows = tokens * group_heads
    group_width = group_heads * head_dim
    ctx_dev = k_own.shape[0]
    context = 2 * ctx_dev
    f32, bf16 = jnp.float32, jnp.bfloat16
    scale = math.log2(math.e) / math.sqrt(head_dim)

    def token_pos(index, pair):
        return context + ((index // tok_rows) * 2 + pair) * tok_rows + index % tok_rows

    queries = jnp.concatenate(
        [recv_ref[:, k * head_dim : (k + 1) * head_dim] for k in range(group_heads)], axis=0
    )
    scaled = queries.astype(f32) * scale
    high = scaled.astype(bf16)
    low = (scaled - high.astype(f32)).astype(bf16)
    queries = jnp.concatenate([high, low], axis=1)
    row_token = lax.broadcasted_iota(jnp.int32, (1, rows), 1) % tokens
    query_pos = token_pos(row_token, pair_at)

    span_k = pl.ds(group_width, head_dim)
    span_v = pl.ds(group_width + head_dim, head_dim)
    cached, spans = [], []
    for k_ref, v_ref, pair in ((k_peer, v_peer, 1 - pair_at), (k_own, v_own, pair_at)):
        for start in range(0, ctx_dev, key_block):
            cached.append((k_ref, v_ref, start, key_block, pair))
    for ref, pair in ((recv_ref, pair_at), (peer_ref, 1 - pair_at)):
        spans.append((ref, pair))

    def load_keys(index):
        if index < len(cached):
            k_ref, _, start, size, _ = cached[index]
            return k_ref[start : start + size, :]
        return spans[index - len(cached)][0][:, span_k]

    def load_values(index):
        if index < len(cached):
            _, v_ref, start, size, _ = cached[index]
            return v_ref[start : start + size, :]
        return spans[index - len(cached)][0][:, span_v]

    def place(index):
        if index < len(cached):
            return index * key_block, key_block
        return len(cached) * key_block + (index - len(cached)) * tokens, tokens

    def first_pos(index):
        _, _, start, _, pair = cached[index]
        return pair * ctx_dev + start

    def scores(index, row_at, masked):
        keys = load_keys(index)
        keys = jnp.concatenate([keys, keys], axis=1)
        block = lax.dot_general(
            keys,
            queries[row_at : row_at + row_block],
            (((1,), (1,)), ((), ())),
            preferred_element_type=f32,
        )
        size = block.shape[0]
        pos_q = query_pos[:, row_at : row_at + row_block]
        column = lax.broadcasted_iota(jnp.int32, (size, 1), 0)
        allowed = None
        if index >= len(cached):
            pos_k = token_pos(column, spans[index - len(cached)][1])
            allowed = pos_k <= pos_q
        else:
            pos_k = first_pos(index) + column
        if masked:
            near = (pos_k < sink_len) | (pos_k > pos_q - window_len)
            allowed = near if allowed is None else allowed & near
        if allowed is not None:
            block = jnp.where(allowed, block, NEG_FILL)
        start, _ = place(index)
        score_ref[start : start + size, row_at : row_at + row_block] = block
        return jnp.max(block.reshape(size // 8, 8, row_block), axis=0)

    def weighted(index, row_at, top):
        start, size = place(index)
        block = score_ref[start : start + size, row_at : row_at + row_block]
        weights = jnp.exp2(block - top)
        total = jnp.sum(weights.reshape(size // 8, 8, row_block), axis=0)
        acc = lax.dot_general(
            load_values(index),
            weights.astype(bf16),
            (((0,), (0,)), ((), ())),
            preferred_element_type=f32,
        )
        return total, acc

    def finish(row_at, total, acc):
        result = (acc / jnp.sum(total, axis=0, keepdims=True)).T.astype(bf16)
        for start in range(0, row_block, tokens):
            head = (row_at + start) // tokens
            out_ref[:, head * head_dim : (head + 1) * head_dim] = result[start : start + tokens]

    blocks = len(cached) + len(spans)
    row_starts = list(range(0, rows, row_block))

    @pl.when(is_retrieval == 1)
    def _():
        tops = {}
        for step in range(len(row_starts) + 1):
            running, total, acc = None, None, None
            for index in range(blocks):
                if step == 0 and index == len(cached) // 2:
                    k_copy.wait()
                if step < len(row_starts):
                    top = scores(index, row_starts[step], False)
                    running = top if running is None else jnp.maximum(running, top)
                if step == 1 and index == 0:
                    v_copy.wait()
                if step > 0:
                    part_total, part_acc = weighted(index, row_starts[step - 1], tops[step - 1])
                    total = part_total if total is None else total + part_total
                    acc = part_acc if acc is None else acc + part_acc
            if step < len(row_starts):
                tops[step] = jnp.max(running, axis=0, keepdims=True)
            if step > 0:
                finish(row_starts[step - 1], total, acc)

    @pl.when(is_retrieval != 1)
    def _():
        k_copy.wait()
        v_copy.wait()

        def needed(index):
            pos = first_pos(index)
            return (pos < sink_len) | (pos + key_block - 1 > context - window_len)

        top_ref[...] = jnp.full(top_ref.shape, NEG_FILL, f32)
        total_ref[...] = jnp.zeros(total_ref.shape, f32)
        acc_ref[...] = jnp.zeros(acc_ref.shape, f32)

        def first(index):
            for row_at in row_starts:
                cols = slice(row_at, row_at + row_block)
                top_ref[:, cols] = jnp.maximum(top_ref[:, cols], scores(index, row_at, True))

        def second(index):
            for row_at in row_starts:
                cols = slice(row_at, row_at + row_block)
                top = jnp.max(top_ref[:, cols], axis=0, keepdims=True)
                total, acc = weighted(index, row_at, top)
                total_ref[:, cols] += total
                acc_ref[:, cols] += acc

        for work in (first, second):
            for index in range(blocks):
                if index < len(cached):
                    pl.when(needed(index))(functools.partial(work, index))
                else:
                    work(index)
        for row_at in row_starts:
            cols = slice(row_at, row_at + row_block)
            finish(row_at, total_ref[:, cols], acc_ref[:, cols])


def on_device_pairs(q_span, k_span, v_span, k_cache, v_cache, head_list, retrieval, windows, sinks):
    head_count = lax.axis_size("head")
    tok_rows = q_span.shape[0]
    group_width = q_span.shape[1] // KVH
    head_dim = k_cache.shape[2]
    group_heads = group_width // head_dim
    ctx_dev = k_cache.shape[1]
    tokens = tok_rows * head_count
    rows = tokens * group_heads
    swap = [(0, 1), (1, 0)]
    k_own, v_own = k_cache[0], v_cache[0]
    k_peer = lax.ppermute(k_own, "seq", swap)
    v_peer = lax.ppermute(v_own, "seq", swap)
    send = pl.pallas_call(
        functools.partial(pack_kernel, group_width=group_width, head_dim=head_dim),
        out_shape=jax.ShapeDtypeStruct((head_count, tok_rows, group_width + 2 * head_dim), jnp.bfloat16),
        in_specs=[SMEM_SPEC, VMEM_SPEC, VMEM_SPEC, VMEM_SPEC],
        out_specs=VMEM_SPEC,
    )(head_list, q_span, k_span, v_span)
    recv = lax.all_to_all(send, "head", split_axis=0, concat_axis=0, tiled=True)
    recv = recv.reshape(tokens, group_width + 2 * head_dim)
    peer = lax.ppermute(recv, "seq", swap)
    key_block = math.gcd(ctx_dev, 1024)
    row_block = 256
    keys = 2 * ctx_dev + 2 * tokens
    result = pl.pallas_call(
        functools.partial(
            attend_kernel,
            tok_rows=tok_rows,
            group_heads=group_heads,
            head_dim=head_dim,
            key_block=key_block,
            row_block=row_block,
        ),
        out_shape=jax.ShapeDtypeStruct((tokens, group_width), jnp.bfloat16),
        in_specs=[SMEM_SPEC] * 4 + [VMEM_SPEC] * 4 + [pl.BlockSpec(memory_space=pltpu.HBM)] * 2,
        out_specs=VMEM_SPEC,
        scratch_shapes=[
            pltpu.VMEM((ctx_dev, head_dim), jnp.bfloat16),
            pltpu.VMEM((ctx_dev, head_dim), jnp.bfloat16),
            pltpu.VMEM((keys, rows), jnp.float32),
            pltpu.VMEM((8, rows), jnp.float32),
            pltpu.VMEM((8, rows), jnp.float32),
            pltpu.VMEM((head_dim, rows), jnp.float32),
            pltpu.SemaphoreType.DMA((2,)),
        ],
        compiler_params=pltpu.CompilerParams(vmem_limit_bytes=40 * 2**20),
    )(head_list, retrieval, windows, sinks, recv, peer, k_peer, v_peer, k_own, v_own)
    result = result.reshape(head_count, tok_rows, group_width)
    back = lax.all_to_all(result, "head", split_axis=0, concat_axis=0, tiled=True)
    return pl.pallas_call(
        unpack_kernel,
        out_shape=jax.ShapeDtypeStruct((tok_rows, KVH * group_width), jnp.bfloat16),
        in_specs=[SMEM_SPEC, VMEM_SPEC],
        out_specs=VMEM_SPEC,
    )(head_list, back)


def solution(mesh):
    on_device = on_device_pairs if mesh.shape["head"] == KVH else on_device_quarters
    in_specs = (
        P(("rep", "head", "seq"), None),
        P(("rep", "head", "seq"), None),
        P(("rep", "head", "seq"), None),
        P(("rep", "head"), "seq", None),
        P(("rep", "head"), "seq", None),
        P("rep"),
        P("rep"),
        P("rep"),
        P("rep"),
    )
    out_specs = P(("rep", "head", "seq"), None)
    return jax.shard_map(
        on_device, mesh=mesh, in_specs=in_specs, out_specs=out_specs, check_vma=False
    )
```

```python
import functools
import math

import jax
import jax.numpy as jnp
from jax import lax
from jax.experimental import pallas as pl
from jax.experimental.pallas import tpu as pltpu
from jax.sharding import PartitionSpec as P

KVH = 8


NEG_FILL = -1e30


def absorb(
    running,
    query_rows,
    query_pos,
    key_rows,
    value_rows,
    key_pos,
    is_retrieval,
    window_len,
    sink_len,
    score_scale,
):
    top_score, totals, weighted = running
    scores = jnp.dot(query_rows, key_rows.T, preferred_element_type=jnp.float32) * score_scale
    allowed = (key_pos[None, :] <= query_pos[:, None]) & (
        (is_retrieval == 1)
        | (key_pos[None, :] < sink_len)
        | (key_pos[None, :] > query_pos[:, None] - window_len)
    )
    block_top = jnp.max(jnp.where(allowed, scores, NEG_FILL), axis=1)
    new_top = jnp.maximum(top_score, block_top)
    weights = jnp.where(allowed, jnp.exp(scores - new_top[:, None]), 0.0)
    rescale = jnp.exp(top_score - new_top)
    totals = totals * rescale + jnp.sum(weights, axis=1)
    weighted = weighted * rescale[:, None] + jnp.dot(
        weights.astype(jnp.bfloat16), value_rows, preferred_element_type=jnp.float32
    )
    return (new_top, totals, weighted)


def finish_rows(received, spread, head_list, tok_rows, head_dim):
    top_score, totals, weighted = received
    group_heads = top_score.shape[-1]
    top_score = top_score.reshape(KVH, spread, tok_rows, group_heads)
    totals = totals.reshape(KVH, spread, tok_rows, group_heads)
    weighted = weighted.reshape(KVH, spread, tok_rows, group_heads, head_dim)
    overall = jnp.max(top_score, axis=1, keepdims=True)
    factor = jnp.exp(top_score - overall)
    summed = jnp.sum(totals * factor, axis=1)
    combined = jnp.sum(weighted * factor[..., None], axis=1)
    result = combined / summed[..., None]
    matches = (head_list[:, None] == jnp.arange(KVH, dtype=jnp.int32)[None, :]).astype(jnp.int32)
    inverse = jnp.sum(jnp.arange(KVH, dtype=jnp.int32)[:, None] * matches, axis=0)
    by_group = jnp.take(result, inverse, axis=0)
    return (
        by_group.transpose(1, 0, 2, 3)
        .reshape(tok_rows, KVH * group_heads * head_dim)
        .astype(jnp.bfloat16)
    )


def on_device_quarters(q_span, k_span, v_span, k_cache, v_cache, head_list, retrieval, windows, sinks):
    head_count = lax.axis_size("head")
    pair_count = lax.axis_size("seq")
    quarters = head_count // KVH
    tok_rows = q_span.shape[0]
    group_width = q_span.shape[1] // KVH
    head_dim = k_cache.shape[2]
    group_heads = group_width // head_dim
    ctx_dev = k_cache.shape[1]
    total_q = tok_rows * head_count * pair_count
    context = ctx_dev * pair_count * quarters
    head_at = lax.axis_index("head")
    pair_at = lax.axis_index("seq")
    slot_index = head_at // quarters
    quarter = head_at % quarters
    kv_group = jnp.take(head_list, slot_index)
    q_groups = q_span.reshape(tok_rows, KVH, group_width)
    kv_groups = jnp.concatenate(
        [k_span.reshape(tok_rows, KVH, head_dim), v_span.reshape(tok_rows, KVH, head_dim)], axis=2
    )
    targets = jnp.take(head_list, jnp.arange(head_count * pair_count) // pair_count // quarters)
    q_send = jnp.take(q_groups, targets, axis=1)
    kv_send = jnp.take(kv_groups, targets, axis=1)
    q_recv, kv_recv = (
        lax.all_to_all(q_send, ("head", "seq"), split_axis=1, concat_axis=0, tiled=True),
        lax.all_to_all(kv_send, ("head", "seq"), split_axis=1, concat_axis=0, tiled=True),
    )
    queries = q_recv.reshape(total_q, group_width)
    span_kv = kv_recv.reshape(total_q, 2 * head_dim)
    query_rows = queries.reshape(total_q * group_heads, head_dim)
    query_pos = context + jnp.arange(total_q * group_heads, dtype=jnp.int32) // group_heads
    is_retrieval = jnp.take(retrieval, kv_group)
    window_len = jnp.take(windows, kv_group)
    sink_len = jnp.take(sinks, kv_group)
    score_scale = 1.0 / math.sqrt(head_dim)
    row_total = total_q * group_heads
    running = (
        jnp.full((row_total,), NEG_FILL, jnp.float32),
        jnp.zeros((row_total,), jnp.float32),
        jnp.zeros((row_total, head_dim), jnp.float32),
    )
    key_block = min(512, ctx_dev)
    segment = quarter * pair_count + pair_at
    first_key = segment * ctx_dev
    cache_keys = k_cache[0]
    cache_values = v_cache[0]

    def key_step(step_index, state):
        start = step_index * key_block
        key_rows = lax.dynamic_slice_in_dim(cache_keys, start, key_block, 0)
        value_rows = lax.dynamic_slice_in_dim(cache_values, start, key_block, 0)
        key_pos = first_key + start + jnp.arange(key_block, dtype=jnp.int32)
        return absorb(
            state,
            query_rows,
            query_pos,
            key_rows,
            value_rows,
            key_pos,
            is_retrieval,
            window_len,
            sink_len,
            score_scale,
        )

    running = lax.fori_loop(0, ctx_dev // key_block, key_step, running)
    span_piece = total_q // (quarters * pair_count)
    span_start = segment * span_piece
    span_rows = lax.dynamic_slice_in_dim(span_kv, span_start, span_piece, 0)
    span_pos = context + span_start + jnp.arange(span_piece, dtype=jnp.int32)
    top_score, totals, weighted = absorb(
        running,
        query_rows,
        query_pos,
        span_rows[:, :head_dim],
        span_rows[:, head_dim:],
        span_pos,
        is_retrieval,
        window_len,
        sink_len,
        score_scale,
    )
    received = (
        lax.all_to_all(
            top_score.reshape(head_count * pair_count, tok_rows, group_heads),
            ("head", "seq"),
            split_axis=0,
            concat_axis=0,
            tiled=True,
        ),
        lax.all_to_all(
            totals.reshape(head_count * pair_count, tok_rows, group_heads),
            ("head", "seq"),
            split_axis=0,
            concat_axis=0,
            tiled=True,
        ),
        lax.all_to_all(
            weighted.reshape(head_count * pair_count, tok_rows, group_width),
            ("head", "seq"),
            split_axis=0,
            concat_axis=0,
            tiled=True,
        ),
    )
    spread = quarters * pair_count
    return finish_rows(received, spread, head_list, tok_rows, head_dim)


VMEM_SPEC = pl.BlockSpec(memory_space=pltpu.VMEM)
HBM_SPEC = pl.BlockSpec(memory_space=pltpu.HBM)
SMEM_SPEC = pl.BlockSpec(memory_space=pltpu.SMEM)


def pack_kernel(head_ref, q_ref, k_ref, v_ref, out_ref, sems, *, group_width, head_dim):
    copies = []
    for slot in range(out_ref.shape[0]):
        group = head_ref[slot]
        q_start = pl.multiple_of(group * group_width, 128)
        kv_start = pl.multiple_of(group * head_dim, 128)
        for part, (source, start, place, width) in enumerate(
            (
                (q_ref, q_start, 0, group_width),
                (k_ref, kv_start, group_width, head_dim),
                (v_ref, kv_start, group_width + head_dim, head_dim),
            )
        ):
            copies.append(
                pltpu.make_async_copy(
                    source.at[:, pl.ds(start, width)],
                    out_ref.at[slot, :, pl.ds(place, width)],
                    sems.at[slot, part],
                )
            )
    for copy in copies:
        copy.start()
    for copy in copies:
        copy.wait()


def unpack_kernel(head_ref, in_ref, out_ref, sems):
    width = in_ref.shape[2]
    copies = []
    for slot in range(in_ref.shape[0]):
        start = pl.multiple_of(head_ref[slot] * width, 128)
        copies.append(
            pltpu.make_async_copy(in_ref.at[slot], out_ref.at[:, pl.ds(start, width)], sems.at[slot])
        )
    for copy in copies:
        copy.start()
    for copy in copies:
        copy.wait()


def attend_kernel(
    head_ref,
    retrieval_ref,
    window_ref,
    sink_ref,
    recv_ref,
    peer_ref,
    k_peer,
    v_peer,
    k_source,
    v_source,
    out_ref,
    k_own,
    v_own,
    score_ref,
    top_ref,
    total_ref,
    acc_ref,
    own_sem,
    *,
    tok_rows,
    group_heads,
    head_dim,
    key_block,
    row_block,
):
    k_copy = pltpu.make_async_copy(k_source, k_own, own_sem.at[0])
    v_copy = pltpu.make_async_copy(v_source, v_own, own_sem.at[1])
    k_copy.start()
    v_copy.start()
    pair_at = lax.axis_index("seq")
    kv_group = head_ref[lax.axis_index("head")]
    is_retrieval = retrieval_ref[kv_group]
    window_len = window_ref[kv_group]
    sink_len = sink_ref[kv_group]
    tokens = recv_ref.shape[0]
    rows = tokens * group_heads
    group_width = group_heads * head_dim
    ctx_dev = k_own.shape[0]
    context = 2 * ctx_dev
    f32, bf16 = jnp.float32, jnp.bfloat16
    scale = math.log2(math.e) / math.sqrt(head_dim)

    def token_pos(index, pair):
        return context + ((index // tok_rows) * 2 + pair) * tok_rows + index % tok_rows

    queries = jnp.concatenate(
        [recv_ref[:, k * head_dim : (k + 1) * head_dim] for k in range(group_heads)], axis=0
    )
    scaled = queries.astype(f32) * scale
    high = scaled.astype(bf16)
    low = (scaled - high.astype(f32)).astype(bf16)
    queries = jnp.concatenate([high, low], axis=1)
    row_token = lax.broadcasted_iota(jnp.int32, (1, rows), 1) % tokens
    query_pos = token_pos(row_token, pair_at)

    span_k = pl.ds(group_width, head_dim)
    span_v = pl.ds(group_width + head_dim, head_dim)
    cached, spans = [], []
    for k_ref, v_ref, pair in ((k_peer, v_peer, 1 - pair_at), (k_own, v_own, pair_at)):
        for start in range(0, ctx_dev, key_block):
            cached.append((k_ref, v_ref, start, key_block, pair))
    for ref, pair in ((recv_ref, pair_at), (peer_ref, 1 - pair_at)):
        spans.append((ref, pair))

    def load_keys(index):
        if index < len(cached):
            k_ref, _, start, size, _ = cached[index]
            return k_ref[start : start + size, :]
        return spans[index - len(cached)][0][:, span_k]

    def load_values(index):
        if index < len(cached):
            _, v_ref, start, size, _ = cached[index]
            return v_ref[start : start + size, :]
        return spans[index - len(cached)][0][:, span_v]

    def place(index):
        if index < len(cached):
            return index * key_block, key_block
        return len(cached) * key_block + (index - len(cached)) * tokens, tokens

    def first_pos(index):
        _, _, start, _, pair = cached[index]
        return pair * ctx_dev + start

    def scores(index, row_at, masked):
        keys = load_keys(index)
        keys = jnp.concatenate([keys, keys], axis=1)
        block = lax.dot_general(
            keys,
            queries[row_at : row_at + row_block],
            (((1,), (1,)), ((), ())),
            preferred_element_type=f32,
        )
        size = block.shape[0]
        pos_q = query_pos[:, row_at : row_at + row_block]
        column = lax.broadcasted_iota(jnp.int32, (size, 1), 0)
        allowed = None
        if index >= len(cached):
            pos_k = token_pos(column, spans[index - len(cached)][1])
            allowed = pos_k <= pos_q
        else:
            pos_k = first_pos(index) + column
        if masked:
            near = (pos_k < sink_len) | (pos_k > pos_q - window_len)
            allowed = near if allowed is None else allowed & near
        if allowed is not None:
            block = jnp.where(allowed, block, NEG_FILL)
        start, _ = place(index)
        score_ref[start : start + size, row_at : row_at + row_block] = block
        return jnp.max(block.reshape(size // 8, 8, row_block), axis=0)

    def weighted(index, row_at, top):
        start, size = place(index)
        block = score_ref[start : start + size, row_at : row_at + row_block]
        weights = jnp.exp2(block - top)
        total = jnp.sum(weights.reshape(size // 8, 8, row_block), axis=0)
        acc = lax.dot_general(
            load_values(index),
            weights.astype(bf16),
            (((0,), (0,)), ((), ())),
            preferred_element_type=f32,
        )
        return total, acc

    def finish(row_at, total, acc):
        result = (acc / jnp.sum(total, axis=0, keepdims=True)).T.astype(bf16)
        for start in range(0, row_block, tokens):
            head = (row_at + start) // tokens
            out_ref[:, head * head_dim : (head + 1) * head_dim] = result[start : start + tokens]

    blocks = len(cached) + len(spans)
    row_starts = list(range(0, rows, row_block))

    @pl.when(is_retrieval == 1)
    def _():
        tops = {}
        for step in range(len(row_starts) + 1):
            running, total, acc = None, None, None
            for index in range(blocks):
                if step == 0 and index == len(cached) // 2:
                    k_copy.wait()
                if step < len(row_starts):
                    top = scores(index, row_starts[step], False)
                    running = top if running is None else jnp.maximum(running, top)
                if step == 1 and index == 0:
                    v_copy.wait()
                if step > 0:
                    part_total, part_acc = weighted(index, row_starts[step - 1], tops[step - 1])
                    total = part_total if total is None else total + part_total
                    acc = part_acc if acc is None else acc + part_acc
            if step < len(row_starts):
                tops[step] = jnp.max(running, axis=0, keepdims=True)
            if step > 0:
                finish(row_starts[step - 1], total, acc)

    @pl.when(is_retrieval != 1)
    def _():
        k_copy.wait()
        v_copy.wait()

        def needed(index):
            pos = first_pos(index)
            return (pos < sink_len) | (pos + key_block - 1 > context - window_len)

        top_ref[...] = jnp.full(top_ref.shape, NEG_FILL, f32)
        total_ref[...] = jnp.zeros(total_ref.shape, f32)
        acc_ref[...] = jnp.zeros(acc_ref.shape, f32)

        def first(index):
            for row_at in row_starts:
                cols = slice(row_at, row_at + row_block)
                top_ref[:, cols] = jnp.maximum(top_ref[:, cols], scores(index, row_at, True))

        def second(index):
            for row_at in row_starts:
                cols = slice(row_at, row_at + row_block)
                top = jnp.max(top_ref[:, cols], axis=0, keepdims=True)
                total, acc = weighted(index, row_at, top)
                total_ref[:, cols] += total
                acc_ref[:, cols] += acc

        for work in (first, second):
            for index in range(blocks):
                if index < len(cached):
                    pl.when(needed(index))(functools.partial(work, index))
                else:
                    work(index)
        for row_at in row_starts:
            cols = slice(row_at, row_at + row_block)
            finish(row_at, total_ref[:, cols], acc_ref[:, cols])


def on_device_pairs(q_span, k_span, v_span, k_cache, v_cache, head_list, retrieval, windows, sinks):
    head_count = lax.axis_size("head")
    tok_rows = q_span.shape[0]
    group_width = q_span.shape[1] // KVH
    head_dim = k_cache.shape[2]
    group_heads = group_width // head_dim
    ctx_dev = k_cache.shape[1]
    tokens = tok_rows * head_count
    rows = tokens * group_heads
    swap = [(0, 1), (1, 0)]
    k_own, v_own = k_cache[0], v_cache[0]
    k_peer = lax.ppermute(k_own, "seq", swap)
    v_peer = lax.ppermute(v_own, "seq", swap)
    send = pl.pallas_call(
        functools.partial(pack_kernel, group_width=group_width, head_dim=head_dim),
        out_shape=jax.ShapeDtypeStruct((head_count, tok_rows, group_width + 2 * head_dim), jnp.bfloat16),
        in_specs=[SMEM_SPEC, HBM_SPEC, HBM_SPEC, HBM_SPEC],
        out_specs=HBM_SPEC,
        scratch_shapes=[pltpu.SemaphoreType.DMA((head_count, 3))],
    )(head_list, q_span, k_span, v_span)
    recv = lax.all_to_all(send, "head", split_axis=0, concat_axis=0, tiled=True)
    recv = recv.reshape(tokens, group_width + 2 * head_dim)
    peer = lax.ppermute(recv, "seq", swap)
    key_block = math.gcd(ctx_dev, 1024)
    row_block = 256
    keys = 2 * ctx_dev + 2 * tokens
    result = pl.pallas_call(
        functools.partial(
            attend_kernel,
            tok_rows=tok_rows,
            group_heads=group_heads,
            head_dim=head_dim,
            key_block=key_block,
            row_block=row_block,
        ),
        out_shape=jax.ShapeDtypeStruct((tokens, group_width), jnp.bfloat16),
        in_specs=[SMEM_SPEC] * 4 + [VMEM_SPEC] * 4 + [HBM_SPEC] * 2,
        out_specs=VMEM_SPEC,
        scratch_shapes=[
            pltpu.VMEM((ctx_dev, head_dim), jnp.bfloat16),
            pltpu.VMEM((ctx_dev, head_dim), jnp.bfloat16),
            pltpu.VMEM((keys, rows), jnp.float32),
            pltpu.VMEM((8, rows), jnp.float32),
            pltpu.VMEM((8, rows), jnp.float32),
            pltpu.VMEM((head_dim, rows), jnp.float32),
            pltpu.SemaphoreType.DMA((2,)),
        ],
        compiler_params=pltpu.CompilerParams(vmem_limit_bytes=51 * 2**20),
    )(head_list, retrieval, windows, sinks, recv, peer, k_peer, v_peer, k_own, v_own)
    result = result.reshape(head_count, tok_rows, group_width)
    back = lax.all_to_all(result, "head", split_axis=0, concat_axis=0, tiled=True)
    return pl.pallas_call(
        unpack_kernel,
        out_shape=jax.ShapeDtypeStruct((tok_rows, KVH * group_width), jnp.bfloat16),
        in_specs=[SMEM_SPEC, HBM_SPEC],
        out_specs=HBM_SPEC,
        scratch_shapes=[pltpu.SemaphoreType.DMA((head_count,))],
    )(head_list, back)


def solution(mesh):
    on_device = on_device_pairs if mesh.shape["head"] == KVH else on_device_quarters
    in_specs = (
        P(("rep", "head", "seq"), None),
        P(("rep", "head", "seq"), None),
        P(("rep", "head", "seq"), None),
        P(("rep", "head"), "seq", None),
        P(("rep", "head"), "seq", None),
        P("rep"),
        P("rep"),
        P("rep"),
        P("rep"),
    )
    out_specs = P(("rep", "head", "seq"), None)
    return jax.shard_map(
        on_device, mesh=mesh, in_specs=in_specs, out_specs=out_specs, check_vma=False
    )
```

```python
import functools
import math

import jax
import jax.numpy as jnp
from jax import lax
from jax.experimental import pallas as pl
from jax.experimental.pallas import tpu as pltpu
from jax.sharding import PartitionSpec as P

KVH = 8


NEG_FILL = -1e30


def absorb(
    running,
    query_rows,
    query_pos,
    key_rows,
    value_rows,
    key_pos,
    is_retrieval,
    window_len,
    sink_len,
    score_scale,
):
    top_score, totals, weighted = running
    scores = jnp.dot(query_rows, key_rows.T, preferred_element_type=jnp.float32) * score_scale
    allowed = (key_pos[None, :] <= query_pos[:, None]) & (
        (is_retrieval == 1)
        | (key_pos[None, :] < sink_len)
        | (key_pos[None, :] > query_pos[:, None] - window_len)
    )
    block_top = jnp.max(jnp.where(allowed, scores, NEG_FILL), axis=1)
    new_top = jnp.maximum(top_score, block_top)
    weights = jnp.where(allowed, jnp.exp(scores - new_top[:, None]), 0.0)
    rescale = jnp.exp(top_score - new_top)
    totals = totals * rescale + jnp.sum(weights, axis=1)
    weighted = weighted * rescale[:, None] + jnp.dot(
        weights.astype(jnp.bfloat16), value_rows, preferred_element_type=jnp.float32
    )
    return (new_top, totals, weighted)


def finish_rows(received, spread, head_list, tok_rows, head_dim):
    top_score, totals, weighted = received
    group_heads = top_score.shape[-1]
    top_score = top_score.reshape(KVH, spread, tok_rows, group_heads)
    totals = totals.reshape(KVH, spread, tok_rows, group_heads)
    weighted = weighted.reshape(KVH, spread, tok_rows, group_heads, head_dim)
    overall = jnp.max(top_score, axis=1, keepdims=True)
    factor = jnp.exp(top_score - overall)
    summed = jnp.sum(totals * factor, axis=1)
    combined = jnp.sum(weighted * factor[..., None], axis=1)
    result = combined / summed[..., None]
    matches = (head_list[:, None] == jnp.arange(KVH, dtype=jnp.int32)[None, :]).astype(jnp.int32)
    inverse = jnp.sum(jnp.arange(KVH, dtype=jnp.int32)[:, None] * matches, axis=0)
    by_group = jnp.take(result, inverse, axis=0)
    return (
        by_group.transpose(1, 0, 2, 3)
        .reshape(tok_rows, KVH * group_heads * head_dim)
        .astype(jnp.bfloat16)
    )


def on_device_quarters(q_span, k_span, v_span, k_cache, v_cache, head_list, retrieval, windows, sinks):
    head_count = lax.axis_size("head")
    pair_count = lax.axis_size("seq")
    quarters = head_count // KVH
    tok_rows = q_span.shape[0]
    group_width = q_span.shape[1] // KVH
    head_dim = k_cache.shape[2]
    group_heads = group_width // head_dim
    ctx_dev = k_cache.shape[1]
    total_q = tok_rows * head_count * pair_count
    context = ctx_dev * pair_count * quarters
    head_at = lax.axis_index("head")
    pair_at = lax.axis_index("seq")
    slot_index = head_at // quarters
    quarter = head_at % quarters
    kv_group = jnp.take(head_list, slot_index)
    q_groups = q_span.reshape(tok_rows, KVH, group_width)
    kv_groups = jnp.concatenate(
        [k_span.reshape(tok_rows, KVH, head_dim), v_span.reshape(tok_rows, KVH, head_dim)], axis=2
    )
    targets = jnp.take(head_list, jnp.arange(head_count * pair_count) // pair_count // quarters)
    q_send = jnp.take(q_groups, targets, axis=1)
    kv_send = jnp.take(kv_groups, targets, axis=1)
    q_recv, kv_recv = (
        lax.all_to_all(q_send, ("head", "seq"), split_axis=1, concat_axis=0, tiled=True),
        lax.all_to_all(kv_send, ("head", "seq"), split_axis=1, concat_axis=0, tiled=True),
    )
    queries = q_recv.reshape(total_q, group_width)
    span_kv = kv_recv.reshape(total_q, 2 * head_dim)
    query_rows = queries.reshape(total_q * group_heads, head_dim)
    query_pos = context + jnp.arange(total_q * group_heads, dtype=jnp.int32) // group_heads
    is_retrieval = jnp.take(retrieval, kv_group)
    window_len = jnp.take(windows, kv_group)
    sink_len = jnp.take(sinks, kv_group)
    score_scale = 1.0 / math.sqrt(head_dim)
    row_total = total_q * group_heads
    running = (
        jnp.full((row_total,), NEG_FILL, jnp.float32),
        jnp.zeros((row_total,), jnp.float32),
        jnp.zeros((row_total, head_dim), jnp.float32),
    )
    key_block = min(512, ctx_dev)
    segment = quarter * pair_count + pair_at
    first_key = segment * ctx_dev
    cache_keys = k_cache[0]
    cache_values = v_cache[0]

    def key_step(step_index, state):
        start = step_index * key_block
        key_rows = lax.dynamic_slice_in_dim(cache_keys, start, key_block, 0)
        value_rows = lax.dynamic_slice_in_dim(cache_values, start, key_block, 0)
        key_pos = first_key + start + jnp.arange(key_block, dtype=jnp.int32)
        return absorb(
            state,
            query_rows,
            query_pos,
            key_rows,
            value_rows,
            key_pos,
            is_retrieval,
            window_len,
            sink_len,
            score_scale,
        )

    running = lax.fori_loop(0, ctx_dev // key_block, key_step, running)
    span_piece = total_q // (quarters * pair_count)
    span_start = segment * span_piece
    span_rows = lax.dynamic_slice_in_dim(span_kv, span_start, span_piece, 0)
    span_pos = context + span_start + jnp.arange(span_piece, dtype=jnp.int32)
    top_score, totals, weighted = absorb(
        running,
        query_rows,
        query_pos,
        span_rows[:, :head_dim],
        span_rows[:, head_dim:],
        span_pos,
        is_retrieval,
        window_len,
        sink_len,
        score_scale,
    )
    received = (
        lax.all_to_all(
            top_score.reshape(head_count * pair_count, tok_rows, group_heads),
            ("head", "seq"),
            split_axis=0,
            concat_axis=0,
            tiled=True,
        ),
        lax.all_to_all(
            totals.reshape(head_count * pair_count, tok_rows, group_heads),
            ("head", "seq"),
            split_axis=0,
            concat_axis=0,
            tiled=True,
        ),
        lax.all_to_all(
            weighted.reshape(head_count * pair_count, tok_rows, group_width),
            ("head", "seq"),
            split_axis=0,
            concat_axis=0,
            tiled=True,
        ),
    )
    spread = quarters * pair_count
    return finish_rows(received, spread, head_list, tok_rows, head_dim)


VMEM_SPEC = pl.BlockSpec(memory_space=pltpu.VMEM)
HBM_SPEC = pl.BlockSpec(memory_space=pltpu.HBM)
SMEM_SPEC = pl.BlockSpec(memory_space=pltpu.SMEM)


def pack_kernel(head_ref, q_ref, k_ref, v_ref, out_ref, *, group_width, head_dim):
    for slot in range(out_ref.shape[0]):
        group = head_ref[slot]
        q_start = pl.multiple_of(group * group_width, 128)
        kv_start = pl.multiple_of(group * head_dim, 128)
        out_ref[slot, :, :group_width] = q_ref[:, pl.ds(q_start, group_width)]
        out_ref[slot, :, group_width : group_width + head_dim] = k_ref[:, pl.ds(kv_start, head_dim)]
        out_ref[slot, :, group_width + head_dim :] = v_ref[:, pl.ds(kv_start, head_dim)]


def unpack_kernel(head_ref, in_ref, out_ref):
    width = in_ref.shape[2]
    for slot in range(in_ref.shape[0]):
        start = pl.multiple_of(head_ref[slot] * width, 128)
        out_ref[:, pl.ds(start, width)] = in_ref[slot]


def attend_kernel(
    head_ref,
    retrieval_ref,
    window_ref,
    sink_ref,
    recv_ref,
    peer_ref,
    k_peer,
    v_peer,
    k_source,
    v_source,
    out_ref,
    k_own,
    v_own,
    score_ref,
    top_ref,
    total_ref,
    acc_ref,
    own_sem,
    *,
    tok_rows,
    group_heads,
    head_dim,
    key_block,
    row_block,
):
    k_copy = pltpu.make_async_copy(k_source, k_own, own_sem.at[0])
    v_copy = pltpu.make_async_copy(v_source, v_own, own_sem.at[1])
    k_copy.start()
    v_copy.start()
    pair_at = lax.axis_index("seq")
    kv_group = head_ref[lax.axis_index("head")]
    is_retrieval = retrieval_ref[kv_group]
    window_len = window_ref[kv_group]
    sink_len = sink_ref[kv_group]
    tokens = recv_ref.shape[0]
    rows = tokens * group_heads
    group_width = group_heads * head_dim
    ctx_dev = k_own.shape[0]
    context = 2 * ctx_dev
    f32, bf16 = jnp.float32, jnp.bfloat16
    scale = math.log2(math.e) / math.sqrt(head_dim)

    def token_pos(index, pair):
        return context + ((index // tok_rows) * 2 + pair) * tok_rows + index % tok_rows

    queries = jnp.concatenate(
        [recv_ref[:, k * head_dim : (k + 1) * head_dim] for k in range(group_heads)], axis=0
    )
    scaled = queries.astype(f32) * scale
    high = scaled.astype(bf16)
    low = (scaled - high.astype(f32)).astype(bf16)
    queries = jnp.concatenate([high, low], axis=1)
    row_token = lax.broadcasted_iota(jnp.int32, (1, rows), 1) % tokens
    query_pos = token_pos(row_token, pair_at)

    span_k = pl.ds(group_width, head_dim)
    span_v = pl.ds(group_width + head_dim, head_dim)
    cached, spans = [], []
    for k_ref, v_ref, pair in ((k_peer, v_peer, 1 - pair_at), (k_own, v_own, pair_at)):
        for start in range(0, ctx_dev, key_block):
            cached.append((k_ref, v_ref, start, key_block, pair))
    for ref, pair in ((recv_ref, pair_at), (peer_ref, 1 - pair_at)):
        spans.append((ref, pair))

    def load_keys(index):
        if index < len(cached):
            k_ref, _, start, size, _ = cached[index]
            return k_ref[start : start + size, :]
        return spans[index - len(cached)][0][:, span_k]

    def load_values(index):
        if index < len(cached):
            _, v_ref, start, size, _ = cached[index]
            return v_ref[start : start + size, :]
        return spans[index - len(cached)][0][:, span_v]

    def place(index):
        if index < len(cached):
            return index * key_block, key_block
        return len(cached) * key_block + (index - len(cached)) * tokens, tokens

    def first_pos(index):
        _, _, start, _, pair = cached[index]
        return pair * ctx_dev + start

    def scores(index, row_at, masked):
        keys = load_keys(index)
        keys = jnp.concatenate([keys, keys], axis=1)
        block = lax.dot_general(
            keys,
            queries[row_at : row_at + row_block],
            (((1,), (1,)), ((), ())),
            preferred_element_type=f32,
        )
        size = block.shape[0]
        pos_q = query_pos[:, row_at : row_at + row_block]
        column = lax.broadcasted_iota(jnp.int32, (size, 1), 0)
        allowed = None
        if index >= len(cached):
            pos_k = token_pos(column, spans[index - len(cached)][1])
            allowed = pos_k <= pos_q
        else:
            pos_k = first_pos(index) + column
        if masked:
            near = (pos_k < sink_len) | (pos_k > pos_q - window_len)
            allowed = near if allowed is None else allowed & near
        if allowed is not None:
            block = jnp.where(allowed, block, NEG_FILL)
        start, _ = place(index)
        score_ref[start : start + size, row_at : row_at + row_block] = block
        return jnp.max(block.reshape(size // 8, 8, row_block), axis=0)

    def weighted(index, row_at, top):
        start, size = place(index)
        block = score_ref[start : start + size, row_at : row_at + row_block]
        weights = jnp.exp2(block - top)
        total = jnp.sum(weights.reshape(size // 8, 8, row_block), axis=0)
        acc = lax.dot_general(
            load_values(index),
            weights.astype(bf16),
            (((0,), (0,)), ((), ())),
            preferred_element_type=f32,
        )
        return total, acc

    def finish(row_at, total, acc):
        result = (acc / jnp.sum(total, axis=0, keepdims=True)).T.astype(bf16)
        for start in range(0, row_block, tokens):
            head = (row_at + start) // tokens
            out_ref[:, head * head_dim : (head + 1) * head_dim] = result[start : start + tokens]

    blocks = len(cached) + len(spans)
    row_starts = list(range(0, rows, row_block))

    @pl.when(is_retrieval == 1)
    def _():
        tops = {}
        for step in range(len(row_starts) + 1):
            running, total, acc = None, None, None
            for index in range(blocks):
                if step == 0 and index == len(cached) // 2:
                    k_copy.wait()
                if step < len(row_starts):
                    top = scores(index, row_starts[step], False)
                    running = top if running is None else jnp.maximum(running, top)
                if step == 1 and index == 0:
                    v_copy.wait()
                if step > 0:
                    part_total, part_acc = weighted(index, row_starts[step - 1], tops[step - 1])
                    total = part_total if total is None else total + part_total
                    acc = part_acc if acc is None else acc + part_acc
            if step < len(row_starts):
                tops[step] = jnp.max(running, axis=0, keepdims=True)
            if step > 0:
                finish(row_starts[step - 1], total, acc)

    @pl.when(is_retrieval != 1)
    def _():
        k_copy.wait()
        v_copy.wait()

        def needed(index):
            pos = first_pos(index)
            return (pos < sink_len) | (pos + key_block - 1 > context - window_len)

        top_ref[...] = jnp.full(top_ref.shape, NEG_FILL, f32)
        total_ref[...] = jnp.zeros(total_ref.shape, f32)
        acc_ref[...] = jnp.zeros(acc_ref.shape, f32)

        def first(index):
            for row_at in row_starts:
                cols = slice(row_at, row_at + row_block)
                top_ref[:, cols] = jnp.maximum(top_ref[:, cols], scores(index, row_at, True))

        def second(index):
            for row_at in row_starts:
                cols = slice(row_at, row_at + row_block)
                top = jnp.max(top_ref[:, cols], axis=0, keepdims=True)
                total, acc = weighted(index, row_at, top)
                total_ref[:, cols] += total
                acc_ref[:, cols] += acc

        for work in (first, second):
            for index in range(blocks):
                if index < len(cached):
                    pl.when(needed(index))(functools.partial(work, index))
                else:
                    work(index)
        for row_at in row_starts:
            cols = slice(row_at, row_at + row_block)
            finish(row_at, total_ref[:, cols], acc_ref[:, cols])


def on_device_pairs(q_span, k_span, v_span, k_cache, v_cache, head_list, retrieval, windows, sinks):
    head_count = lax.axis_size("head")
    tok_rows = q_span.shape[0]
    group_width = q_span.shape[1] // KVH
    head_dim = k_cache.shape[2]
    group_heads = group_width // head_dim
    ctx_dev = k_cache.shape[1]
    tokens = tok_rows * head_count
    rows = tokens * group_heads
    swap = [(0, 1), (1, 0)]
    k_own, v_own = k_cache[0], v_cache[0]
    k_peer = lax.ppermute(k_own, "seq", swap)
    v_peer = lax.ppermute(v_own, "seq", swap)
    send = pl.pallas_call(
        functools.partial(pack_kernel, group_width=group_width, head_dim=head_dim),
        out_shape=jax.ShapeDtypeStruct((head_count, tok_rows, group_width + 2 * head_dim), jnp.bfloat16),
        in_specs=[SMEM_SPEC, VMEM_SPEC, VMEM_SPEC, VMEM_SPEC],
        out_specs=VMEM_SPEC,
        compiler_params=pltpu.CompilerParams(vmem_limit_bytes=2**20),
    )(head_list, q_span, k_span, v_span)
    recv = lax.all_to_all(send, "head", split_axis=0, concat_axis=0, tiled=True)
    recv = recv.reshape(tokens, group_width + 2 * head_dim)
    peer = lax.ppermute(recv, "seq", swap)
    key_block = math.gcd(ctx_dev, 1024)
    row_block = 256
    keys = 2 * ctx_dev + 2 * tokens
    result = pl.pallas_call(
        functools.partial(
            attend_kernel,
            tok_rows=tok_rows,
            group_heads=group_heads,
            head_dim=head_dim,
            key_block=key_block,
            row_block=row_block,
        ),
        out_shape=jax.ShapeDtypeStruct((tokens, group_width), jnp.bfloat16),
        in_specs=[SMEM_SPEC] * 4 + [VMEM_SPEC] * 4 + [HBM_SPEC] * 2,
        out_specs=VMEM_SPEC,
        scratch_shapes=[
            pltpu.VMEM((ctx_dev, head_dim), jnp.bfloat16),
            pltpu.VMEM((ctx_dev, head_dim), jnp.bfloat16),
            pltpu.VMEM((keys, rows), jnp.float32),
            pltpu.VMEM((8, rows), jnp.float32),
            pltpu.VMEM((8, rows), jnp.float32),
            pltpu.VMEM((head_dim, rows), jnp.float32),
            pltpu.SemaphoreType.DMA((2,)),
        ],
        compiler_params=pltpu.CompilerParams(vmem_limit_bytes=51 * 2**20),
    )(head_list, retrieval, windows, sinks, recv, peer, k_peer, v_peer, k_own, v_own)
    result = result.reshape(head_count, tok_rows, group_width)
    back = lax.all_to_all(result, "head", split_axis=0, concat_axis=0, tiled=True)
    return pl.pallas_call(
        unpack_kernel,
        out_shape=jax.ShapeDtypeStruct((tok_rows, KVH * group_width), jnp.bfloat16),
        in_specs=[SMEM_SPEC, VMEM_SPEC],
        out_specs=VMEM_SPEC,
        compiler_params=pltpu.CompilerParams(vmem_limit_bytes=2**20),
    )(head_list, back)


def solution(mesh):
    on_device = on_device_pairs if mesh.shape["head"] == KVH else on_device_quarters
    in_specs = (
        P(("rep", "head", "seq"), None),
        P(("rep", "head", "seq"), None),
        P(("rep", "head", "seq"), None),
        P(("rep", "head"), "seq", None),
        P(("rep", "head"), "seq", None),
        P("rep"),
        P("rep"),
        P("rep"),
        P("rep"),
    )
    out_specs = P(("rep", "head", "seq"), None)
    return jax.shard_map(
        on_device, mesh=mesh, in_specs=in_specs, out_specs=out_specs, check_vma=False
    )
```

```python
import functools
import math

import jax
import jax.numpy as jnp
from jax import lax
from jax.experimental import pallas as pl
from jax.experimental.pallas import tpu as pltpu
from jax.sharding import PartitionSpec as P

KVH = 8


NEG_FILL = -1e30


def absorb(
    running,
    query_rows,
    query_pos,
    key_rows,
    value_rows,
    key_pos,
    is_retrieval,
    window_len,
    sink_len,
    score_scale,
):
    top_score, totals, weighted = running
    scores = jnp.dot(query_rows, key_rows.T, preferred_element_type=jnp.float32) * score_scale
    allowed = (key_pos[None, :] <= query_pos[:, None]) & (
        (is_retrieval == 1)
        | (key_pos[None, :] < sink_len)
        | (key_pos[None, :] > query_pos[:, None] - window_len)
    )
    block_top = jnp.max(jnp.where(allowed, scores, NEG_FILL), axis=1)
    new_top = jnp.maximum(top_score, block_top)
    weights = jnp.where(allowed, jnp.exp(scores - new_top[:, None]), 0.0)
    rescale = jnp.exp(top_score - new_top)
    totals = totals * rescale + jnp.sum(weights, axis=1)
    weighted = weighted * rescale[:, None] + jnp.dot(
        weights.astype(jnp.bfloat16), value_rows, preferred_element_type=jnp.float32
    )
    return (new_top, totals, weighted)


def finish_rows(received, spread, head_list, tok_rows, head_dim):
    top_score, totals, weighted = received
    group_heads = top_score.shape[-1]
    top_score = top_score.reshape(KVH, spread, tok_rows, group_heads)
    totals = totals.reshape(KVH, spread, tok_rows, group_heads)
    weighted = weighted.reshape(KVH, spread, tok_rows, group_heads, head_dim)
    overall = jnp.max(top_score, axis=1, keepdims=True)
    factor = jnp.exp(top_score - overall)
    summed = jnp.sum(totals * factor, axis=1)
    combined = jnp.sum(weighted * factor[..., None], axis=1)
    result = combined / summed[..., None]
    matches = (head_list[:, None] == jnp.arange(KVH, dtype=jnp.int32)[None, :]).astype(jnp.int32)
    inverse = jnp.sum(jnp.arange(KVH, dtype=jnp.int32)[:, None] * matches, axis=0)
    by_group = jnp.take(result, inverse, axis=0)
    return (
        by_group.transpose(1, 0, 2, 3)
        .reshape(tok_rows, KVH * group_heads * head_dim)
        .astype(jnp.bfloat16)
    )


def on_device_quarters(q_span, k_span, v_span, k_cache, v_cache, head_list, retrieval, windows, sinks):
    head_count = lax.axis_size("head")
    pair_count = lax.axis_size("seq")
    quarters = head_count // KVH
    tok_rows = q_span.shape[0]
    group_width = q_span.shape[1] // KVH
    head_dim = k_cache.shape[2]
    group_heads = group_width // head_dim
    ctx_dev = k_cache.shape[1]
    total_q = tok_rows * head_count * pair_count
    context = ctx_dev * pair_count * quarters
    head_at = lax.axis_index("head")
    pair_at = lax.axis_index("seq")
    slot_index = head_at // quarters
    quarter = head_at % quarters
    kv_group = jnp.take(head_list, slot_index)
    q_groups = q_span.reshape(tok_rows, KVH, group_width)
    kv_groups = jnp.concatenate(
        [k_span.reshape(tok_rows, KVH, head_dim), v_span.reshape(tok_rows, KVH, head_dim)], axis=2
    )
    targets = jnp.take(head_list, jnp.arange(head_count * pair_count) // pair_count // quarters)
    q_send = jnp.take(q_groups, targets, axis=1)
    kv_send = jnp.take(kv_groups, targets, axis=1)
    q_recv, kv_recv = (
        lax.all_to_all(q_send, ("head", "seq"), split_axis=1, concat_axis=0, tiled=True),
        lax.all_to_all(kv_send, ("head", "seq"), split_axis=1, concat_axis=0, tiled=True),
    )
    queries = q_recv.reshape(total_q, group_width)
    span_kv = kv_recv.reshape(total_q, 2 * head_dim)
    query_rows = queries.reshape(total_q * group_heads, head_dim)
    query_pos = context + jnp.arange(total_q * group_heads, dtype=jnp.int32) // group_heads
    is_retrieval = jnp.take(retrieval, kv_group)
    window_len = jnp.take(windows, kv_group)
    sink_len = jnp.take(sinks, kv_group)
    score_scale = 1.0 / math.sqrt(head_dim)
    row_total = total_q * group_heads
    running = (
        jnp.full((row_total,), NEG_FILL, jnp.float32),
        jnp.zeros((row_total,), jnp.float32),
        jnp.zeros((row_total, head_dim), jnp.float32),
    )
    key_block = min(512, ctx_dev)
    segment = quarter * pair_count + pair_at
    first_key = segment * ctx_dev
    cache_keys = k_cache[0]
    cache_values = v_cache[0]

    def key_step(step_index, state):
        start = step_index * key_block
        key_rows = lax.dynamic_slice_in_dim(cache_keys, start, key_block, 0)
        value_rows = lax.dynamic_slice_in_dim(cache_values, start, key_block, 0)
        key_pos = first_key + start + jnp.arange(key_block, dtype=jnp.int32)
        return absorb(
            state,
            query_rows,
            query_pos,
            key_rows,
            value_rows,
            key_pos,
            is_retrieval,
            window_len,
            sink_len,
            score_scale,
        )

    running = lax.fori_loop(0, ctx_dev // key_block, key_step, running)
    span_piece = total_q // (quarters * pair_count)
    span_start = segment * span_piece
    span_rows = lax.dynamic_slice_in_dim(span_kv, span_start, span_piece, 0)
    span_pos = context + span_start + jnp.arange(span_piece, dtype=jnp.int32)
    top_score, totals, weighted = absorb(
        running,
        query_rows,
        query_pos,
        span_rows[:, :head_dim],
        span_rows[:, head_dim:],
        span_pos,
        is_retrieval,
        window_len,
        sink_len,
        score_scale,
    )
    received = (
        lax.all_to_all(
            top_score.reshape(head_count * pair_count, tok_rows, group_heads),
            ("head", "seq"),
            split_axis=0,
            concat_axis=0,
            tiled=True,
        ),
        lax.all_to_all(
            totals.reshape(head_count * pair_count, tok_rows, group_heads),
            ("head", "seq"),
            split_axis=0,
            concat_axis=0,
            tiled=True,
        ),
        lax.all_to_all(
            weighted.reshape(head_count * pair_count, tok_rows, group_width),
            ("head", "seq"),
            split_axis=0,
            concat_axis=0,
            tiled=True,
        ),
    )
    spread = quarters * pair_count
    return finish_rows(received, spread, head_list, tok_rows, head_dim)


VMEM_SPEC = pl.BlockSpec(memory_space=pltpu.VMEM)
HBM_SPEC = pl.BlockSpec(memory_space=pltpu.HBM)
SMEM_SPEC = pl.BlockSpec(memory_space=pltpu.SMEM)


def pack_kernel(head_ref, in_ref, out_ref, *, group_width, head_dim):
    q_width = KVH * group_width
    q_ref = in_ref.at[:, :q_width]
    k_ref = in_ref.at[:, q_width : q_width + KVH * head_dim]
    v_ref = in_ref.at[:, q_width + KVH * head_dim :]
    for slot in range(out_ref.shape[0]):
        group = head_ref[slot]
        q_start = pl.multiple_of(group * group_width, 128)
        kv_start = pl.multiple_of(group * head_dim, 128)
        out_ref[slot, :, :group_width] = q_ref[:, pl.ds(q_start, group_width)]
        out_ref[slot, :, group_width : group_width + head_dim] = k_ref[:, pl.ds(kv_start, head_dim)]
        out_ref[slot, :, group_width + head_dim :] = v_ref[:, pl.ds(kv_start, head_dim)]


def unpack_kernel(head_ref, in_ref, out_ref, sems):
    width = in_ref.shape[2]
    copies = []
    for slot in range(in_ref.shape[0]):
        start = pl.multiple_of(head_ref[slot] * width, 128)
        copies.append(
            pltpu.make_async_copy(in_ref.at[slot], out_ref.at[:, pl.ds(start, width)], sems.at[slot])
        )
    for copy in copies:
        copy.start()
    for copy in copies:
        copy.wait()


def attend_kernel(
    head_ref,
    retrieval_ref,
    window_ref,
    sink_ref,
    recv_ref,
    peer_ref,
    k_peer,
    v_peer,
    k_source,
    v_source,
    out_ref,
    k_own,
    v_own,
    score_ref,
    top_ref,
    total_ref,
    acc_ref,
    own_sem,
    *,
    tok_rows,
    group_heads,
    head_dim,
    key_block,
    row_block,
):
    k_copy = pltpu.make_async_copy(k_source, k_own, own_sem.at[0])
    v_copy = pltpu.make_async_copy(v_source, v_own, own_sem.at[1])
    k_copy.start()
    v_copy.start()
    pair_at = lax.axis_index("seq")
    kv_group = head_ref[lax.axis_index("head")]
    is_retrieval = retrieval_ref[kv_group]
    window_len = window_ref[kv_group]
    sink_len = sink_ref[kv_group]
    tokens = recv_ref.shape[0]
    rows = tokens * group_heads
    group_width = group_heads * head_dim
    ctx_dev = k_own.shape[0]
    context = 2 * ctx_dev
    f32, bf16 = jnp.float32, jnp.bfloat16
    scale = math.log2(math.e) / math.sqrt(head_dim)

    def token_pos(index, pair):
        return context + ((index // tok_rows) * 2 + pair) * tok_rows + index % tok_rows

    queries = jnp.concatenate(
        [recv_ref[:, k * head_dim : (k + 1) * head_dim] for k in range(group_heads)], axis=0
    )
    scaled = queries.astype(f32) * scale
    high = scaled.astype(bf16)
    low = (scaled - high.astype(f32)).astype(bf16)
    queries = jnp.concatenate([high, low], axis=1)
    row_token = lax.broadcasted_iota(jnp.int32, (1, rows), 1) % tokens
    query_pos = token_pos(row_token, pair_at)

    span_k = pl.ds(group_width, head_dim)
    span_v = pl.ds(group_width + head_dim, head_dim)
    cached, spans = [], []
    for k_ref, v_ref, pair in ((k_peer, v_peer, 1 - pair_at), (k_own, v_own, pair_at)):
        for start in range(0, ctx_dev, key_block):
            cached.append((k_ref, v_ref, start, key_block, pair))
    for ref, pair in ((recv_ref, pair_at), (peer_ref, 1 - pair_at)):
        spans.append((ref, pair))

    def load_keys(index):
        if index < len(cached):
            k_ref, _, start, size, _ = cached[index]
            return k_ref[start : start + size, :]
        return spans[index - len(cached)][0][:, span_k]

    def load_values(index):
        if index < len(cached):
            _, v_ref, start, size, _ = cached[index]
            return v_ref[start : start + size, :]
        return spans[index - len(cached)][0][:, span_v]

    def place(index):
        if index < len(cached):
            return index * key_block, key_block
        return len(cached) * key_block + (index - len(cached)) * tokens, tokens

    def first_pos(index):
        _, _, start, _, pair = cached[index]
        return pair * ctx_dev + start

    def scores(index, row_at, masked):
        keys = load_keys(index)
        keys = jnp.concatenate([keys, keys], axis=1)
        block = lax.dot_general(
            keys,
            queries[row_at : row_at + row_block],
            (((1,), (1,)), ((), ())),
            preferred_element_type=f32,
        )
        size = block.shape[0]
        pos_q = query_pos[:, row_at : row_at + row_block]
        column = lax.broadcasted_iota(jnp.int32, (size, 1), 0)
        allowed = None
        if index >= len(cached):
            pos_k = token_pos(column, spans[index - len(cached)][1])
            allowed = pos_k <= pos_q
        else:
            pos_k = first_pos(index) + column
        if masked:
            near = (pos_k < sink_len) | (pos_k > pos_q - window_len)
            allowed = near if allowed is None else allowed & near
        if allowed is not None:
            block = jnp.where(allowed, block, NEG_FILL)
        start, _ = place(index)
        score_ref[start : start + size, row_at : row_at + row_block] = block
        return jnp.max(block.reshape(size // 8, 8, row_block), axis=0)

    def weighted(index, row_at, top):
        start, size = place(index)
        block = score_ref[start : start + size, row_at : row_at + row_block]
        weights = jnp.exp2(block - top)
        total = jnp.sum(weights.reshape(size // 8, 8, row_block), axis=0)
        acc = lax.dot_general(
            load_values(index),
            weights.astype(bf16),
            (((0,), (0,)), ((), ())),
            preferred_element_type=f32,
        )
        return total, acc

    def finish(row_at, total, acc):
        result = (acc / jnp.sum(total, axis=0, keepdims=True)).T.astype(bf16)
        for start in range(0, row_block, tokens):
            head = (row_at + start) // tokens
            out_ref[:, head * head_dim : (head + 1) * head_dim] = result[start : start + tokens]

    blocks = len(cached) + len(spans)
    row_starts = list(range(0, rows, row_block))

    @pl.when(is_retrieval == 1)
    def _():
        tops = {}
        for step in range(len(row_starts) + 1):
            running, total, acc = None, None, None
            for index in range(blocks):
                if step == 0 and index == len(cached) // 2:
                    k_copy.wait()
                if step < len(row_starts):
                    top = scores(index, row_starts[step], False)
                    running = top if running is None else jnp.maximum(running, top)
                if step == 1 and index == 0:
                    v_copy.wait()
                if step > 0:
                    part_total, part_acc = weighted(index, row_starts[step - 1], tops[step - 1])
                    total = part_total if total is None else total + part_total
                    acc = part_acc if acc is None else acc + part_acc
            if step < len(row_starts):
                tops[step] = jnp.max(running, axis=0, keepdims=True)
            if step > 0:
                finish(row_starts[step - 1], total, acc)

    @pl.when(is_retrieval != 1)
    def _():
        k_copy.wait()
        v_copy.wait()

        def needed(index):
            pos = first_pos(index)
            return (pos < sink_len) | (pos + key_block - 1 > context - window_len)

        top_ref[...] = jnp.full(top_ref.shape, NEG_FILL, f32)
        total_ref[...] = jnp.zeros(total_ref.shape, f32)
        acc_ref[...] = jnp.zeros(acc_ref.shape, f32)

        def first(index):
            for row_at in row_starts:
                cols = slice(row_at, row_at + row_block)
                top_ref[:, cols] = jnp.maximum(top_ref[:, cols], scores(index, row_at, True))

        def second(index):
            for row_at in row_starts:
                cols = slice(row_at, row_at + row_block)
                top = jnp.max(top_ref[:, cols], axis=0, keepdims=True)
                total, acc = weighted(index, row_at, top)
                total_ref[:, cols] += total
                acc_ref[:, cols] += acc

        for work in (first, second):
            for index in range(blocks):
                if index < len(cached):
                    pl.when(needed(index))(functools.partial(work, index))
                else:
                    work(index)
        for row_at in row_starts:
            cols = slice(row_at, row_at + row_block)
            finish(row_at, total_ref[:, cols], acc_ref[:, cols])


def on_device_pairs(q_span, k_span, v_span, k_cache, v_cache, head_list, retrieval, windows, sinks):
    head_count = lax.axis_size("head")
    tok_rows = q_span.shape[0]
    group_width = q_span.shape[1] // KVH
    head_dim = k_cache.shape[2]
    group_heads = group_width // head_dim
    ctx_dev = k_cache.shape[1]
    tokens = tok_rows * head_count
    rows = tokens * group_heads
    swap = [(0, 1), (1, 0)]
    k_own, v_own = k_cache[0], v_cache[0]
    k_peer = lax.ppermute(k_own, "seq", swap)
    v_peer = lax.ppermute(v_own, "seq", swap)
    joined = jnp.concatenate([q_span, k_span, v_span], axis=1)
    send = pl.pallas_call(
        functools.partial(pack_kernel, group_width=group_width, head_dim=head_dim),
        out_shape=jax.ShapeDtypeStruct((head_count, tok_rows, group_width + 2 * head_dim), jnp.bfloat16),
        in_specs=[SMEM_SPEC, VMEM_SPEC],
        out_specs=VMEM_SPEC,
        compiler_params=pltpu.CompilerParams(vmem_limit_bytes=2**20),
    )(head_list, lax.optimization_barrier(joined))
    recv = lax.all_to_all(send, "head", split_axis=0, concat_axis=0, tiled=True)
    recv = recv.reshape(tokens, group_width + 2 * head_dim)
    peer = lax.ppermute(recv, "seq", swap)
    key_block = math.gcd(ctx_dev, 1024)
    row_block = 256
    keys = 2 * ctx_dev + 2 * tokens
    result = pl.pallas_call(
        functools.partial(
            attend_kernel,
            tok_rows=tok_rows,
            group_heads=group_heads,
            head_dim=head_dim,
            key_block=key_block,
            row_block=row_block,
        ),
        out_shape=jax.ShapeDtypeStruct((tokens, group_width), jnp.bfloat16),
        in_specs=[SMEM_SPEC] * 4 + [VMEM_SPEC] * 4 + [HBM_SPEC] * 2,
        out_specs=VMEM_SPEC,
        scratch_shapes=[
            pltpu.VMEM((ctx_dev, head_dim), jnp.bfloat16),
            pltpu.VMEM((ctx_dev, head_dim), jnp.bfloat16),
            pltpu.VMEM((keys, rows), jnp.float32),
            pltpu.VMEM((8, rows), jnp.float32),
            pltpu.VMEM((8, rows), jnp.float32),
            pltpu.VMEM((head_dim, rows), jnp.float32),
            pltpu.SemaphoreType.DMA((2,)),
        ],
        compiler_params=pltpu.CompilerParams(vmem_limit_bytes=51 * 2**20),
    )(head_list, retrieval, windows, sinks, recv, peer, k_peer, v_peer, k_own, v_own)
    result = result.reshape(head_count, tok_rows, group_width)
    back = lax.all_to_all(result, "head", split_axis=0, concat_axis=0, tiled=True)
    return pl.pallas_call(
        unpack_kernel,
        out_shape=jax.ShapeDtypeStruct((tok_rows, KVH * group_width), jnp.bfloat16),
        in_specs=[SMEM_SPEC, VMEM_SPEC],
        out_specs=HBM_SPEC,
        scratch_shapes=[pltpu.SemaphoreType.DMA((head_count,))],
        compiler_params=pltpu.CompilerParams(vmem_limit_bytes=2**20),
    )(head_list, back)


def solution(mesh):
    on_device = on_device_pairs if mesh.shape["head"] == KVH else on_device_quarters
    in_specs = (
        P(("rep", "head", "seq"), None),
        P(("rep", "head", "seq"), None),
        P(("rep", "head", "seq"), None),
        P(("rep", "head"), "seq", None),
        P(("rep", "head"), "seq", None),
        P("rep"),
        P("rep"),
        P("rep"),
        P("rep"),
    )
    out_specs = P(("rep", "head", "seq"), None)
    return jax.shard_map(
        on_device, mesh=mesh, in_specs=in_specs, out_specs=out_specs, check_vma=False
    )
```

```python
import functools
import math

import jax
import jax.numpy as jnp
from jax import lax
from jax.experimental import pallas as pl
from jax.experimental.pallas import tpu as pltpu
from jax.sharding import PartitionSpec as P

KVH = 8


NEG_FILL = -1e30


def absorb(
    running,
    query_rows,
    query_pos,
    key_rows,
    value_rows,
    key_pos,
    is_retrieval,
    window_len,
    sink_len,
    score_scale,
):
    top_score, totals, weighted = running
    scores = jnp.dot(query_rows, key_rows.T, preferred_element_type=jnp.float32) * score_scale
    allowed = (key_pos[None, :] <= query_pos[:, None]) & (
        (is_retrieval == 1)
        | (key_pos[None, :] < sink_len)
        | (key_pos[None, :] > query_pos[:, None] - window_len)
    )
    block_top = jnp.max(jnp.where(allowed, scores, NEG_FILL), axis=1)
    new_top = jnp.maximum(top_score, block_top)
    weights = jnp.where(allowed, jnp.exp(scores - new_top[:, None]), 0.0)
    rescale = jnp.exp(top_score - new_top)
    totals = totals * rescale + jnp.sum(weights, axis=1)
    weighted = weighted * rescale[:, None] + jnp.dot(
        weights.astype(jnp.bfloat16), value_rows, preferred_element_type=jnp.float32
    )
    return (new_top, totals, weighted)


def finish_rows(received, spread, head_list, tok_rows, head_dim):
    top_score, totals, weighted = received
    group_heads = top_score.shape[-1]
    top_score = top_score.reshape(KVH, spread, tok_rows, group_heads)
    totals = totals.reshape(KVH, spread, tok_rows, group_heads)
    weighted = weighted.reshape(KVH, spread, tok_rows, group_heads, head_dim)
    overall = jnp.max(top_score, axis=1, keepdims=True)
    factor = jnp.exp(top_score - overall)
    summed = jnp.sum(totals * factor, axis=1)
    combined = jnp.sum(weighted * factor[..., None], axis=1)
    result = combined / summed[..., None]
    matches = (head_list[:, None] == jnp.arange(KVH, dtype=jnp.int32)[None, :]).astype(jnp.int32)
    inverse = jnp.sum(jnp.arange(KVH, dtype=jnp.int32)[:, None] * matches, axis=0)
    by_group = jnp.take(result, inverse, axis=0)
    return (
        by_group.transpose(1, 0, 2, 3)
        .reshape(tok_rows, KVH * group_heads * head_dim)
        .astype(jnp.bfloat16)
    )


def on_device_quarters(q_span, k_span, v_span, k_cache, v_cache, head_list, retrieval, windows, sinks):
    head_count = lax.axis_size("head")
    pair_count = lax.axis_size("seq")
    quarters = head_count // KVH
    tok_rows = q_span.shape[0]
    group_width = q_span.shape[1] // KVH
    head_dim = k_cache.shape[2]
    group_heads = group_width // head_dim
    ctx_dev = k_cache.shape[1]
    total_q = tok_rows * head_count * pair_count
    context = ctx_dev * pair_count * quarters
    head_at = lax.axis_index("head")
    pair_at = lax.axis_index("seq")
    slot_index = head_at // quarters
    quarter = head_at % quarters
    kv_group = jnp.take(head_list, slot_index)
    q_groups = q_span.reshape(tok_rows, KVH, group_width)
    kv_groups = jnp.concatenate(
        [k_span.reshape(tok_rows, KVH, head_dim), v_span.reshape(tok_rows, KVH, head_dim)], axis=2
    )
    targets = jnp.take(head_list, jnp.arange(head_count * pair_count) // pair_count // quarters)
    q_send = jnp.take(q_groups, targets, axis=1)
    kv_send = jnp.take(kv_groups, targets, axis=1)
    q_recv, kv_recv = (
        lax.all_to_all(q_send, ("head", "seq"), split_axis=1, concat_axis=0, tiled=True),
        lax.all_to_all(kv_send, ("head", "seq"), split_axis=1, concat_axis=0, tiled=True),
    )
    queries = q_recv.reshape(total_q, group_width)
    span_kv = kv_recv.reshape(total_q, 2 * head_dim)
    query_rows = queries.reshape(total_q * group_heads, head_dim)
    query_pos = context + jnp.arange(total_q * group_heads, dtype=jnp.int32) // group_heads
    is_retrieval = jnp.take(retrieval, kv_group)
    window_len = jnp.take(windows, kv_group)
    sink_len = jnp.take(sinks, kv_group)
    score_scale = 1.0 / math.sqrt(head_dim)
    row_total = total_q * group_heads
    running = (
        jnp.full((row_total,), NEG_FILL, jnp.float32),
        jnp.zeros((row_total,), jnp.float32),
        jnp.zeros((row_total, head_dim), jnp.float32),
    )
    key_block = min(512, ctx_dev)
    segment = quarter * pair_count + pair_at
    first_key = segment * ctx_dev
    cache_keys = k_cache[0]
    cache_values = v_cache[0]

    def key_step(step_index, state):
        start = step_index * key_block
        key_rows = lax.dynamic_slice_in_dim(cache_keys, start, key_block, 0)
        value_rows = lax.dynamic_slice_in_dim(cache_values, start, key_block, 0)
        key_pos = first_key + start + jnp.arange(key_block, dtype=jnp.int32)
        return absorb(
            state,
            query_rows,
            query_pos,
            key_rows,
            value_rows,
            key_pos,
            is_retrieval,
            window_len,
            sink_len,
            score_scale,
        )

    running = lax.fori_loop(0, ctx_dev // key_block, key_step, running)
    span_piece = total_q // (quarters * pair_count)
    span_start = segment * span_piece
    span_rows = lax.dynamic_slice_in_dim(span_kv, span_start, span_piece, 0)
    span_pos = context + span_start + jnp.arange(span_piece, dtype=jnp.int32)
    top_score, totals, weighted = absorb(
        running,
        query_rows,
        query_pos,
        span_rows[:, :head_dim],
        span_rows[:, head_dim:],
        span_pos,
        is_retrieval,
        window_len,
        sink_len,
        score_scale,
    )
    received = (
        lax.all_to_all(
            top_score.reshape(head_count * pair_count, tok_rows, group_heads),
            ("head", "seq"),
            split_axis=0,
            concat_axis=0,
            tiled=True,
        ),
        lax.all_to_all(
            totals.reshape(head_count * pair_count, tok_rows, group_heads),
            ("head", "seq"),
            split_axis=0,
            concat_axis=0,
            tiled=True,
        ),
        lax.all_to_all(
            weighted.reshape(head_count * pair_count, tok_rows, group_width),
            ("head", "seq"),
            split_axis=0,
            concat_axis=0,
            tiled=True,
        ),
    )
    spread = quarters * pair_count
    return finish_rows(received, spread, head_list, tok_rows, head_dim)


VMEM_SPEC = pl.BlockSpec(memory_space=pltpu.VMEM)
HBM_SPEC = pl.BlockSpec(memory_space=pltpu.HBM)
SMEM_SPEC = pl.BlockSpec(memory_space=pltpu.SMEM)


def pack_kernel(head_ref, in_ref, k_ref, v_ref, out_ref, *, group_width, head_dim):
    q_width = KVH * group_width
    kv_width = KVH * head_dim
    for slot in range(out_ref.shape[0]):
        group = head_ref[slot]
        start = pl.multiple_of(group * group_width, 128)
        out_ref[slot, :, :group_width] = in_ref[:, pl.ds(start, group_width)]
        kv_start = pl.multiple_of(group * head_dim, 128)
        parts = (
            in_ref[:, pl.ds(q_width + kv_start, head_dim)],
            in_ref[:, pl.ds(q_width + kv_width + kv_start, head_dim)],
            k_ref[:, pl.ds(kv_start, head_dim)],
            v_ref[:, pl.ds(kv_start, head_dim)],
        )
        for part, value in enumerate(parts):
            place = group_width + part * head_dim
            out_ref[slot, :, place : place + head_dim] = value


def unpack_kernel(head_ref, in_ref, out_ref, sems):
    width = in_ref.shape[2]
    copies = []
    for slot in range(in_ref.shape[0]):
        start = pl.multiple_of(head_ref[slot] * width, 128)
        copies.append(
            pltpu.make_async_copy(in_ref.at[slot], out_ref.at[:, pl.ds(start, width)], sems.at[slot])
        )
    for copy in copies:
        copy.start()
    for copy in copies:
        copy.wait()


def attend_kernel(
    head_ref,
    retrieval_ref,
    window_ref,
    sink_ref,
    recv_ref,
    k_peer,
    v_peer,
    k_source,
    v_source,
    out_ref,
    k_own,
    v_own,
    score_ref,
    top_ref,
    total_ref,
    acc_ref,
    own_sem,
    *,
    tok_rows,
    group_heads,
    head_dim,
    key_block,
    row_block,
):
    k_copy = pltpu.make_async_copy(k_source, k_own, own_sem.at[0])
    v_copy = pltpu.make_async_copy(v_source, v_own, own_sem.at[1])
    k_copy.start()
    v_copy.start()
    pair_at = lax.axis_index("seq")
    kv_group = head_ref[lax.axis_index("head")]
    is_retrieval = retrieval_ref[kv_group]
    window_len = window_ref[kv_group]
    sink_len = sink_ref[kv_group]
    tokens = recv_ref.shape[0]
    rows = tokens * group_heads
    group_width = group_heads * head_dim
    ctx_dev = k_own.shape[0]
    context = 2 * ctx_dev
    f32, bf16 = jnp.float32, jnp.bfloat16
    scale = math.log2(math.e) / math.sqrt(head_dim)

    def token_pos(index, pair):
        return context + ((index // tok_rows) * 2 + pair) * tok_rows + index % tok_rows

    queries = jnp.concatenate(
        [recv_ref[:, k * head_dim : (k + 1) * head_dim] for k in range(group_heads)], axis=0
    )
    scaled = queries.astype(f32) * scale
    high = scaled.astype(bf16)
    low = (scaled - high.astype(f32)).astype(bf16)
    queries = jnp.concatenate([high, low], axis=1)
    row_token = lax.broadcasted_iota(jnp.int32, (1, rows), 1) % tokens
    query_pos = token_pos(row_token, pair_at)

    cached, spans = [], []
    for k_ref, v_ref, pair in ((k_peer, v_peer, 1 - pair_at), (k_own, v_own, pair_at)):
        for start in range(0, ctx_dev, key_block):
            cached.append((k_ref, v_ref, start, key_block, pair))
    for part, pair in enumerate((pair_at, 1 - pair_at)):
        spans.append((group_width + 2 * part * head_dim, pair))

    def load_keys(index):
        if index < len(cached):
            k_ref, _, start, size, _ = cached[index]
            return k_ref[start : start + size, :]
        column = spans[index - len(cached)][0]
        return recv_ref[:, column : column + head_dim]

    def load_values(index):
        if index < len(cached):
            _, v_ref, start, size, _ = cached[index]
            return v_ref[start : start + size, :]
        column = spans[index - len(cached)][0] + head_dim
        return recv_ref[:, column : column + head_dim]

    def place(index):
        if index < len(cached):
            return index * key_block, key_block
        return len(cached) * key_block + (index - len(cached)) * tokens, tokens

    def first_pos(index):
        _, _, start, _, pair = cached[index]
        return pair * ctx_dev + start

    def scores(index, row_at, masked):
        keys = load_keys(index)
        keys = jnp.concatenate([keys, keys], axis=1)
        block = lax.dot_general(
            keys,
            queries[row_at : row_at + row_block],
            (((1,), (1,)), ((), ())),
            preferred_element_type=f32,
        )
        size = block.shape[0]
        pos_q = query_pos[:, row_at : row_at + row_block]
        column = lax.broadcasted_iota(jnp.int32, (size, 1), 0)
        allowed = None
        if index >= len(cached):
            pos_k = token_pos(column, spans[index - len(cached)][1])
            allowed = pos_k <= pos_q
        else:
            pos_k = first_pos(index) + column
        if masked:
            near = (pos_k < sink_len) | (pos_k > pos_q - window_len)
            allowed = near if allowed is None else allowed & near
        if allowed is not None:
            block = jnp.where(allowed, block, NEG_FILL)
        start, _ = place(index)
        score_ref[start : start + size, row_at : row_at + row_block] = block
        return jnp.max(block.reshape(size // 8, 8, row_block), axis=0)

    def weighted(index, row_at, top):
        start, size = place(index)
        block = score_ref[start : start + size, row_at : row_at + row_block]
        weights = jnp.exp2(block - top)
        total = jnp.sum(weights.reshape(size // 8, 8, row_block), axis=0)
        acc = lax.dot_general(
            load_values(index),
            weights.astype(bf16),
            (((0,), (0,)), ((), ())),
            preferred_element_type=f32,
        )
        return total, acc

    def finish(row_at, total, acc):
        result = (acc / jnp.sum(total, axis=0, keepdims=True)).T.astype(bf16)
        for start in range(0, row_block, tokens):
            head = (row_at + start) // tokens
            out_ref[:, head * head_dim : (head + 1) * head_dim] = result[start : start + tokens]

    blocks = len(cached) + len(spans)
    row_starts = list(range(0, rows, row_block))

    @pl.when(is_retrieval == 1)
    def _():
        tops = {}
        for step in range(len(row_starts) + 1):
            running, total, acc = None, None, None
            for index in range(blocks):
                if step == 0 and index == len(cached) // 2:
                    k_copy.wait()
                if step < len(row_starts):
                    top = scores(index, row_starts[step], False)
                    running = top if running is None else jnp.maximum(running, top)
                if step == 1 and index == 0:
                    v_copy.wait()
                if step > 0:
                    part_total, part_acc = weighted(index, row_starts[step - 1], tops[step - 1])
                    total = part_total if total is None else total + part_total
                    acc = part_acc if acc is None else acc + part_acc
            if step < len(row_starts):
                tops[step] = jnp.max(running, axis=0, keepdims=True)
            if step > 0:
                finish(row_starts[step - 1], total, acc)

    @pl.when(is_retrieval != 1)
    def _():
        k_copy.wait()
        v_copy.wait()

        def needed(index):
            pos = first_pos(index)
            return (pos < sink_len) | (pos + key_block - 1 > context - window_len)

        top_ref[...] = jnp.full(top_ref.shape, NEG_FILL, f32)
        total_ref[...] = jnp.zeros(total_ref.shape, f32)
        acc_ref[...] = jnp.zeros(acc_ref.shape, f32)

        def first(index):
            for row_at in row_starts:
                cols = slice(row_at, row_at + row_block)
                top_ref[:, cols] = jnp.maximum(top_ref[:, cols], scores(index, row_at, True))

        def second(index):
            for row_at in row_starts:
                cols = slice(row_at, row_at + row_block)
                top = jnp.max(top_ref[:, cols], axis=0, keepdims=True)
                total, acc = weighted(index, row_at, top)
                total_ref[:, cols] += total
                acc_ref[:, cols] += acc

        for work in (first, second):
            for index in range(blocks):
                if index < len(cached):
                    pl.when(needed(index))(functools.partial(work, index))
                else:
                    work(index)
        for row_at in row_starts:
            cols = slice(row_at, row_at + row_block)
            finish(row_at, total_ref[:, cols], acc_ref[:, cols])


def on_device_pairs(q_span, k_span, v_span, k_cache, v_cache, head_list, retrieval, windows, sinks):
    head_count = lax.axis_size("head")
    tok_rows = q_span.shape[0]
    group_width = q_span.shape[1] // KVH
    head_dim = k_cache.shape[2]
    group_heads = group_width // head_dim
    ctx_dev = k_cache.shape[1]
    tokens = tok_rows * head_count
    rows = tokens * group_heads
    swap = [(0, 1), (1, 0)]
    k_other = lax.ppermute(k_span, "seq", swap)
    v_other = lax.ppermute(v_span, "seq", swap)
    k_own, v_own = k_cache[0], v_cache[0]
    k_peer = lax.ppermute(k_own, "seq", swap)
    v_peer = lax.ppermute(v_own, "seq", swap)
    joined = jnp.concatenate([q_span, k_span, v_span], axis=1)
    send = pl.pallas_call(
        functools.partial(pack_kernel, group_width=group_width, head_dim=head_dim),
        out_shape=jax.ShapeDtypeStruct((head_count, tok_rows, group_width + 4 * head_dim), jnp.bfloat16),
        in_specs=[SMEM_SPEC] + [VMEM_SPEC] * 3,
        out_specs=VMEM_SPEC,
        compiler_params=pltpu.CompilerParams(vmem_limit_bytes=2**20),
    )(head_list, lax.optimization_barrier(joined), k_other, v_other)
    recv = lax.all_to_all(send, "head", split_axis=0, concat_axis=0, tiled=True)
    recv = recv.reshape(tokens, group_width + 4 * head_dim)
    key_block = math.gcd(ctx_dev, 1024)
    row_block = 256
    keys = 2 * ctx_dev + 2 * tokens
    result = pl.pallas_call(
        functools.partial(
            attend_kernel,
            tok_rows=tok_rows,
            group_heads=group_heads,
            head_dim=head_dim,
            key_block=key_block,
            row_block=row_block,
        ),
        out_shape=jax.ShapeDtypeStruct((tokens, group_width), jnp.bfloat16),
        in_specs=[SMEM_SPEC] * 4 + [VMEM_SPEC] * 3 + [HBM_SPEC] * 2,
        out_specs=VMEM_SPEC,
        scratch_shapes=[
            pltpu.VMEM((ctx_dev, head_dim), jnp.bfloat16),
            pltpu.VMEM((ctx_dev, head_dim), jnp.bfloat16),
            pltpu.VMEM((keys, rows), jnp.float32),
            pltpu.VMEM((8, rows), jnp.float32),
            pltpu.VMEM((8, rows), jnp.float32),
            pltpu.VMEM((head_dim, rows), jnp.float32),
            pltpu.SemaphoreType.DMA((2,)),
        ],
        compiler_params=pltpu.CompilerParams(vmem_limit_bytes=51 * 2**20),
    )(head_list, retrieval, windows, sinks, recv, k_peer, v_peer, k_own, v_own)
    result = result.reshape(head_count, tok_rows, group_width)
    back = lax.all_to_all(result, "head", split_axis=0, concat_axis=0, tiled=True)
    return pl.pallas_call(
        unpack_kernel,
        out_shape=jax.ShapeDtypeStruct((tok_rows, KVH * group_width), jnp.bfloat16),
        in_specs=[SMEM_SPEC, VMEM_SPEC],
        out_specs=HBM_SPEC,
        scratch_shapes=[pltpu.SemaphoreType.DMA((head_count,))],
        compiler_params=pltpu.CompilerParams(vmem_limit_bytes=2**20),
    )(head_list, back)


def solution(mesh):
    on_device = on_device_pairs if mesh.shape["head"] == KVH else on_device_quarters
    in_specs = (
        P(("rep", "head", "seq"), None),
        P(("rep", "head", "seq"), None),
        P(("rep", "head", "seq"), None),
        P(("rep", "head"), "seq", None),
        P(("rep", "head"), "seq", None),
        P("rep"),
        P("rep"),
        P("rep"),
        P("rep"),
    )
    out_specs = P(("rep", "head", "seq"), None)
    return jax.shard_map(
        on_device, mesh=mesh, in_specs=in_specs, out_specs=out_specs, check_vma=False
    )
```

```python
import functools
import math

import jax
import jax.numpy as jnp
from jax import lax
from jax.experimental import pallas as pl
from jax.experimental.pallas import tpu as pltpu
from jax.sharding import PartitionSpec as P

KVH = 8


NEG_FILL = -1e30


def absorb(
    running,
    query_rows,
    query_pos,
    key_rows,
    value_rows,
    key_pos,
    is_retrieval,
    window_len,
    sink_len,
    score_scale,
):
    top_score, totals, weighted = running
    scores = jnp.dot(query_rows, key_rows.T, preferred_element_type=jnp.float32) * score_scale
    allowed = (key_pos[None, :] <= query_pos[:, None]) & (
        (is_retrieval == 1)
        | (key_pos[None, :] < sink_len)
        | (key_pos[None, :] > query_pos[:, None] - window_len)
    )
    block_top = jnp.max(jnp.where(allowed, scores, NEG_FILL), axis=1)
    new_top = jnp.maximum(top_score, block_top)
    weights = jnp.where(allowed, jnp.exp(scores - new_top[:, None]), 0.0)
    rescale = jnp.exp(top_score - new_top)
    totals = totals * rescale + jnp.sum(weights, axis=1)
    weighted = weighted * rescale[:, None] + jnp.dot(
        weights.astype(jnp.bfloat16), value_rows, preferred_element_type=jnp.float32
    )
    return (new_top, totals, weighted)


def finish_rows(received, spread, head_list, tok_rows, head_dim):
    top_score, totals, weighted = received
    group_heads = top_score.shape[-1]
    top_score = top_score.reshape(KVH, spread, tok_rows, group_heads)
    totals = totals.reshape(KVH, spread, tok_rows, group_heads)
    weighted = weighted.reshape(KVH, spread, tok_rows, group_heads, head_dim)
    overall = jnp.max(top_score, axis=1, keepdims=True)
    factor = jnp.exp(top_score - overall)
    summed = jnp.sum(totals * factor, axis=1)
    combined = jnp.sum(weighted * factor[..., None], axis=1)
    result = combined / summed[..., None]
    matches = (head_list[:, None] == jnp.arange(KVH, dtype=jnp.int32)[None, :]).astype(jnp.int32)
    inverse = jnp.sum(jnp.arange(KVH, dtype=jnp.int32)[:, None] * matches, axis=0)
    by_group = jnp.take(result, inverse, axis=0)
    return (
        by_group.transpose(1, 0, 2, 3)
        .reshape(tok_rows, KVH * group_heads * head_dim)
        .astype(jnp.bfloat16)
    )


def on_device_quarters(q_span, k_span, v_span, k_cache, v_cache, head_list, retrieval, windows, sinks):
    head_count = lax.axis_size("head")
    pair_count = lax.axis_size("seq")
    quarters = head_count // KVH
    tok_rows = q_span.shape[0]
    group_width = q_span.shape[1] // KVH
    head_dim = k_cache.shape[2]
    group_heads = group_width // head_dim
    ctx_dev = k_cache.shape[1]
    total_q = tok_rows * head_count * pair_count
    context = ctx_dev * pair_count * quarters
    head_at = lax.axis_index("head")
    pair_at = lax.axis_index("seq")
    slot_index = head_at // quarters
    quarter = head_at % quarters
    kv_group = jnp.take(head_list, slot_index)
    q_groups = q_span.reshape(tok_rows, KVH, group_width)
    kv_groups = jnp.concatenate(
        [k_span.reshape(tok_rows, KVH, head_dim), v_span.reshape(tok_rows, KVH, head_dim)], axis=2
    )
    targets = jnp.take(head_list, jnp.arange(head_count * pair_count) // pair_count // quarters)
    q_send = jnp.take(q_groups, targets, axis=1)
    kv_send = jnp.take(kv_groups, targets, axis=1)
    q_recv, kv_recv = (
        lax.all_to_all(q_send, ("head", "seq"), split_axis=1, concat_axis=0, tiled=True),
        lax.all_to_all(kv_send, ("head", "seq"), split_axis=1, concat_axis=0, tiled=True),
    )
    queries = q_recv.reshape(total_q, group_width)
    span_kv = kv_recv.reshape(total_q, 2 * head_dim)
    query_rows = queries.reshape(total_q * group_heads, head_dim)
    query_pos = context + jnp.arange(total_q * group_heads, dtype=jnp.int32) // group_heads
    is_retrieval = jnp.take(retrieval, kv_group)
    window_len = jnp.take(windows, kv_group)
    sink_len = jnp.take(sinks, kv_group)
    score_scale = 1.0 / math.sqrt(head_dim)
    row_total = total_q * group_heads
    running = (
        jnp.full((row_total,), NEG_FILL, jnp.float32),
        jnp.zeros((row_total,), jnp.float32),
        jnp.zeros((row_total, head_dim), jnp.float32),
    )
    key_block = min(512, ctx_dev)
    segment = quarter * pair_count + pair_at
    first_key = segment * ctx_dev
    cache_keys = k_cache[0]
    cache_values = v_cache[0]

    def key_step(step_index, state):
        start = step_index * key_block
        key_rows = lax.dynamic_slice_in_dim(cache_keys, start, key_block, 0)
        value_rows = lax.dynamic_slice_in_dim(cache_values, start, key_block, 0)
        key_pos = first_key + start + jnp.arange(key_block, dtype=jnp.int32)
        return absorb(
            state,
            query_rows,
            query_pos,
            key_rows,
            value_rows,
            key_pos,
            is_retrieval,
            window_len,
            sink_len,
            score_scale,
        )

    running = lax.fori_loop(0, ctx_dev // key_block, key_step, running)
    span_piece = total_q // (quarters * pair_count)
    span_start = segment * span_piece
    span_rows = lax.dynamic_slice_in_dim(span_kv, span_start, span_piece, 0)
    span_pos = context + span_start + jnp.arange(span_piece, dtype=jnp.int32)
    top_score, totals, weighted = absorb(
        running,
        query_rows,
        query_pos,
        span_rows[:, :head_dim],
        span_rows[:, head_dim:],
        span_pos,
        is_retrieval,
        window_len,
        sink_len,
        score_scale,
    )
    received = (
        lax.all_to_all(
            top_score.reshape(head_count * pair_count, tok_rows, group_heads),
            ("head", "seq"),
            split_axis=0,
            concat_axis=0,
            tiled=True,
        ),
        lax.all_to_all(
            totals.reshape(head_count * pair_count, tok_rows, group_heads),
            ("head", "seq"),
            split_axis=0,
            concat_axis=0,
            tiled=True,
        ),
        lax.all_to_all(
            weighted.reshape(head_count * pair_count, tok_rows, group_width),
            ("head", "seq"),
            split_axis=0,
            concat_axis=0,
            tiled=True,
        ),
    )
    spread = quarters * pair_count
    return finish_rows(received, spread, head_list, tok_rows, head_dim)


VMEM_SPEC = pl.BlockSpec(memory_space=pltpu.VMEM)
HBM_SPEC = pl.BlockSpec(memory_space=pltpu.HBM)
SMEM_SPEC = pl.BlockSpec(memory_space=pltpu.SMEM)


def pack_kernel(head_ref, in_ref, out_ref, *, group_width, head_dim):
    q_width = KVH * group_width
    q_ref = in_ref.at[:, :q_width]
    k_ref = in_ref.at[:, q_width : q_width + KVH * head_dim]
    v_ref = in_ref.at[:, q_width + KVH * head_dim :]
    for slot in range(out_ref.shape[0]):
        group = head_ref[slot]
        q_start = pl.multiple_of(group * group_width, 128)
        kv_start = pl.multiple_of(group * head_dim, 128)
        out_ref[slot, :, :group_width] = q_ref[:, pl.ds(q_start, group_width)]
        out_ref[slot, :, group_width : group_width + head_dim] = k_ref[:, pl.ds(kv_start, head_dim)]
        out_ref[slot, :, group_width + head_dim :] = v_ref[:, pl.ds(kv_start, head_dim)]


def unpack_kernel(head_ref, in_ref, out_ref, sems):
    width = in_ref.shape[2]
    copies = []
    for slot in range(in_ref.shape[0]):
        start = pl.multiple_of(head_ref[slot] * width, 128)
        copies.append(
            pltpu.make_async_copy(in_ref.at[slot], out_ref.at[:, pl.ds(start, width)], sems.at[slot])
        )
    for copy in copies:
        copy.start()
    for copy in copies:
        copy.wait()


def attend_kernel(
    head_ref,
    retrieval_ref,
    window_ref,
    sink_ref,
    recv_ref,
    peer_ref,
    k_peer,
    v_peer,
    k_source,
    v_source,
    out_ref,
    k_own,
    v_own,
    score_ref,
    top_ref,
    total_ref,
    acc_ref,
    own_sem,
    *,
    tok_rows,
    group_heads,
    head_dim,
    key_block,
    row_block,
):
    k_copy = pltpu.make_async_copy(k_source, k_own, own_sem.at[0])
    v_copy = pltpu.make_async_copy(v_source, v_own, own_sem.at[1])
    k_copy.start()
    pair_at = lax.axis_index("seq")
    kv_group = head_ref[lax.axis_index("head")]
    is_retrieval = retrieval_ref[kv_group]
    window_len = window_ref[kv_group]
    sink_len = sink_ref[kv_group]
    tokens = recv_ref.shape[0]
    rows = tokens * group_heads
    group_width = group_heads * head_dim
    ctx_dev = k_own.shape[0]
    context = 2 * ctx_dev
    f32, bf16 = jnp.float32, jnp.bfloat16
    scale = math.log2(math.e) / math.sqrt(head_dim)

    def token_pos(index, pair):
        return context + ((index // tok_rows) * 2 + pair) * tok_rows + index % tok_rows

    queries = jnp.concatenate(
        [recv_ref[:, k * head_dim : (k + 1) * head_dim] for k in range(group_heads)], axis=0
    )
    scaled = queries.astype(f32) * scale
    high = scaled.astype(bf16)
    low = (scaled - high.astype(f32)).astype(bf16)
    queries = jnp.concatenate([high, low], axis=1)
    row_token = lax.broadcasted_iota(jnp.int32, (1, rows), 1) % tokens
    query_pos = token_pos(row_token, pair_at)

    span_k = pl.ds(group_width, head_dim)
    span_v = pl.ds(group_width + head_dim, head_dim)
    cached, spans = [], []
    for k_ref, v_ref, pair in ((k_peer, v_peer, 1 - pair_at), (k_own, v_own, pair_at)):
        for start in range(0, ctx_dev, key_block):
            cached.append((k_ref, v_ref, start, key_block, pair))
    for ref, pair in ((recv_ref, pair_at), (peer_ref, 1 - pair_at)):
        spans.append((ref, pair))

    def load_keys(index):
        if index < len(cached):
            k_ref, _, start, size, _ = cached[index]
            return k_ref[start : start + size, :]
        return spans[index - len(cached)][0][:, span_k]

    def load_values(index):
        if index < len(cached):
            _, v_ref, start, size, _ = cached[index]
            return v_ref[start : start + size, :]
        return spans[index - len(cached)][0][:, span_v]

    def place(index):
        if index < len(cached):
            return index * key_block, key_block
        return len(cached) * key_block + (index - len(cached)) * tokens, tokens

    def first_pos(index):
        _, _, start, _, pair = cached[index]
        return pair * ctx_dev + start

    def scores(index, row_at, masked):
        keys = load_keys(index)
        keys = jnp.concatenate([keys, keys], axis=1)
        block = lax.dot_general(
            keys,
            queries[row_at : row_at + row_block],
            (((1,), (1,)), ((), ())),
            preferred_element_type=f32,
        )
        size = block.shape[0]
        pos_q = query_pos[:, row_at : row_at + row_block]
        column = lax.broadcasted_iota(jnp.int32, (size, 1), 0)
        allowed = None
        if index >= len(cached):
            pos_k = token_pos(column, spans[index - len(cached)][1])
            allowed = pos_k <= pos_q
        else:
            pos_k = first_pos(index) + column
        if masked:
            near = (pos_k < sink_len) | (pos_k > pos_q - window_len)
            allowed = near if allowed is None else allowed & near
        if allowed is not None:
            block = jnp.where(allowed, block, NEG_FILL)
        start, _ = place(index)
        score_ref[start : start + size, row_at : row_at + row_block] = block
        return jnp.max(block.reshape(size // 8, 8, row_block), axis=0)

    def weighted(index, row_at, top):
        start, size = place(index)
        block = score_ref[start : start + size, row_at : row_at + row_block]
        weights = jnp.exp2(block - top)
        total = jnp.sum(weights.reshape(size // 8, 8, row_block), axis=0)
        acc = lax.dot_general(
            load_values(index),
            weights.astype(bf16),
            (((0,), (0,)), ((), ())),
            preferred_element_type=f32,
        )
        return total, acc

    def finish(row_at, total, acc):
        result = (acc / jnp.sum(total, axis=0, keepdims=True)).T.astype(bf16)
        for start in range(0, row_block, tokens):
            head = (row_at + start) // tokens
            out_ref[:, head * head_dim : (head + 1) * head_dim] = result[start : start + tokens]

    blocks = len(cached) + len(spans)
    row_starts = list(range(0, rows, row_block))

    half = len(cached) // 2
    peer_blocks = list(range(half))
    own_blocks = list(range(half, blocks))

    @pl.when(is_retrieval == 1)
    def _():
        running, total, acc = {}, {}, {}

        def first(indices):
            for row_at in row_starts:
                for index in indices:
                    top = scores(index, row_at, False)
                    running[row_at] = jnp.maximum(running[row_at], top) if row_at in running else top

        def second(indices):
            for row_at in row_starts:
                top = jnp.max(running[row_at], axis=0, keepdims=True)
                for index in indices:
                    part_total, part_acc = weighted(index, row_at, top)
                    total[row_at] = total[row_at] + part_total if row_at in total else part_total
                    acc[row_at] = acc[row_at] + part_acc if row_at in acc else part_acc

        first(peer_blocks)
        k_copy.wait()
        v_copy.start()
        first(own_blocks)
        second(peer_blocks)
        v_copy.wait()
        second(own_blocks)
        for row_at in row_starts:
            finish(row_at, total[row_at], acc[row_at])

    @pl.when(is_retrieval != 1)
    def _():
        def needed(index):
            pos = first_pos(index)
            return (pos < sink_len) | (pos + key_block - 1 > context - window_len)

        top_ref[...] = jnp.full(top_ref.shape, NEG_FILL, f32)
        total_ref[...] = jnp.zeros(total_ref.shape, f32)
        acc_ref[...] = jnp.zeros(acc_ref.shape, f32)

        def first(index):
            for row_at in row_starts:
                cols = slice(row_at, row_at + row_block)
                top_ref[:, cols] = jnp.maximum(top_ref[:, cols], scores(index, row_at, True))

        def second(index):
            for row_at in row_starts:
                cols = slice(row_at, row_at + row_block)
                top = jnp.max(top_ref[:, cols], axis=0, keepdims=True)
                total, acc = weighted(index, row_at, top)
                total_ref[:, cols] += total
                acc_ref[:, cols] += acc

        def each(work, indices):
            for index in indices:
                if index < len(cached):
                    pl.when(needed(index))(functools.partial(work, index))
                else:
                    work(index)

        each(first, peer_blocks)
        k_copy.wait()
        v_copy.start()
        each(first, own_blocks)
        each(second, peer_blocks)
        v_copy.wait()
        each(second, own_blocks)
        for row_at in row_starts:
            cols = slice(row_at, row_at + row_block)
            finish(row_at, total_ref[:, cols], acc_ref[:, cols])


def on_device_pairs(q_span, k_span, v_span, k_cache, v_cache, head_list, retrieval, windows, sinks):
    head_count = lax.axis_size("head")
    tok_rows = q_span.shape[0]
    group_width = q_span.shape[1] // KVH
    head_dim = k_cache.shape[2]
    group_heads = group_width // head_dim
    ctx_dev = k_cache.shape[1]
    tokens = tok_rows * head_count
    rows = tokens * group_heads
    swap = [(0, 1), (1, 0)]
    k_own, v_own = k_cache[0], v_cache[0]
    k_peer = lax.ppermute(k_own, "seq", swap)
    v_peer = lax.ppermute(v_own, "seq", swap)
    joined = jnp.concatenate([q_span, k_span, v_span], axis=1)
    send = pl.pallas_call(
        functools.partial(pack_kernel, group_width=group_width, head_dim=head_dim),
        out_shape=jax.ShapeDtypeStruct((head_count, tok_rows, group_width + 2 * head_dim), jnp.bfloat16),
        in_specs=[SMEM_SPEC, VMEM_SPEC],
        out_specs=VMEM_SPEC,
        compiler_params=pltpu.CompilerParams(vmem_limit_bytes=2**20),
    )(head_list, lax.optimization_barrier(joined))
    recv = lax.all_to_all(send, "head", split_axis=0, concat_axis=0, tiled=True)
    recv = recv.reshape(tokens, group_width + 2 * head_dim)
    peer = lax.ppermute(recv, "seq", swap)
    key_block = math.gcd(ctx_dev, 1024)
    row_block = 256
    keys = 2 * ctx_dev + 2 * tokens
    result = pl.pallas_call(
        functools.partial(
            attend_kernel,
            tok_rows=tok_rows,
            group_heads=group_heads,
            head_dim=head_dim,
            key_block=key_block,
            row_block=row_block,
        ),
        out_shape=jax.ShapeDtypeStruct((tokens, group_width), jnp.bfloat16),
        in_specs=[SMEM_SPEC] * 4 + [VMEM_SPEC] * 4 + [HBM_SPEC] * 2,
        out_specs=VMEM_SPEC,
        scratch_shapes=[
            pltpu.VMEM((ctx_dev, head_dim), jnp.bfloat16),
            pltpu.VMEM((ctx_dev, head_dim), jnp.bfloat16),
            pltpu.VMEM((keys, rows), jnp.float32),
            pltpu.VMEM((8, rows), jnp.float32),
            pltpu.VMEM((8, rows), jnp.float32),
            pltpu.VMEM((head_dim, rows), jnp.float32),
            pltpu.SemaphoreType.DMA((2,)),
        ],
        compiler_params=pltpu.CompilerParams(vmem_limit_bytes=51 * 2**20),
    )(head_list, retrieval, windows, sinks, recv, peer, k_peer, v_peer, k_own, v_own)
    result = result.reshape(head_count, tok_rows, group_width)
    back = lax.all_to_all(result, "head", split_axis=0, concat_axis=0, tiled=True)
    return pl.pallas_call(
        unpack_kernel,
        out_shape=jax.ShapeDtypeStruct((tok_rows, KVH * group_width), jnp.bfloat16),
        in_specs=[SMEM_SPEC, VMEM_SPEC],
        out_specs=HBM_SPEC,
        scratch_shapes=[pltpu.SemaphoreType.DMA((head_count,))],
        compiler_params=pltpu.CompilerParams(vmem_limit_bytes=2**20),
    )(head_list, back)


def solution(mesh):
    on_device = on_device_pairs if mesh.shape["head"] == KVH else on_device_quarters
    in_specs = (
        P(("rep", "head", "seq"), None),
        P(("rep", "head", "seq"), None),
        P(("rep", "head", "seq"), None),
        P(("rep", "head"), "seq", None),
        P(("rep", "head"), "seq", None),
        P("rep"),
        P("rep"),
        P("rep"),
        P("rep"),
    )
    out_specs = P(("rep", "head", "seq"), None)
    return jax.shard_map(
        on_device, mesh=mesh, in_specs=in_specs, out_specs=out_specs, check_vma=False
    )
```

```python
import functools
import math

import jax
import jax.numpy as jnp
from jax import lax
from jax.experimental import pallas as pl
from jax.experimental.pallas import tpu as pltpu
from jax.sharding import PartitionSpec as P

KVH = 8


NEG_FILL = -1e30


def absorb(
    running,
    query_rows,
    query_pos,
    key_rows,
    value_rows,
    key_pos,
    is_retrieval,
    window_len,
    sink_len,
    score_scale,
):
    top_score, totals, weighted = running
    scores = jnp.dot(query_rows, key_rows.T, preferred_element_type=jnp.float32) * score_scale
    allowed = (key_pos[None, :] <= query_pos[:, None]) & (
        (is_retrieval == 1)
        | (key_pos[None, :] < sink_len)
        | (key_pos[None, :] > query_pos[:, None] - window_len)
    )
    block_top = jnp.max(jnp.where(allowed, scores, NEG_FILL), axis=1)
    new_top = jnp.maximum(top_score, block_top)
    weights = jnp.where(allowed, jnp.exp(scores - new_top[:, None]), 0.0)
    rescale = jnp.exp(top_score - new_top)
    totals = totals * rescale + jnp.sum(weights, axis=1)
    weighted = weighted * rescale[:, None] + jnp.dot(
        weights.astype(jnp.bfloat16), value_rows, preferred_element_type=jnp.float32
    )
    return (new_top, totals, weighted)


def finish_rows(received, spread, head_list, tok_rows, head_dim):
    top_score, totals, weighted = received
    group_heads = top_score.shape[-1]
    top_score = top_score.reshape(KVH, spread, tok_rows, group_heads)
    totals = totals.reshape(KVH, spread, tok_rows, group_heads)
    weighted = weighted.reshape(KVH, spread, tok_rows, group_heads, head_dim)
    overall = jnp.max(top_score, axis=1, keepdims=True)
    factor = jnp.exp(top_score - overall)
    summed = jnp.sum(totals * factor, axis=1)
    combined = jnp.sum(weighted * factor[..., None], axis=1)
    result = combined / summed[..., None]
    matches = (head_list[:, None] == jnp.arange(KVH, dtype=jnp.int32)[None, :]).astype(jnp.int32)
    inverse = jnp.sum(jnp.arange(KVH, dtype=jnp.int32)[:, None] * matches, axis=0)
    by_group = jnp.take(result, inverse, axis=0)
    return (
        by_group.transpose(1, 0, 2, 3)
        .reshape(tok_rows, KVH * group_heads * head_dim)
        .astype(jnp.bfloat16)
    )


def on_device_quarters(q_span, k_span, v_span, k_cache, v_cache, head_list, retrieval, windows, sinks):
    head_count = lax.axis_size("head")
    pair_count = lax.axis_size("seq")
    quarters = head_count // KVH
    tok_rows = q_span.shape[0]
    group_width = q_span.shape[1] // KVH
    head_dim = k_cache.shape[2]
    group_heads = group_width // head_dim
    ctx_dev = k_cache.shape[1]
    total_q = tok_rows * head_count * pair_count
    context = ctx_dev * pair_count * quarters
    head_at = lax.axis_index("head")
    pair_at = lax.axis_index("seq")
    slot_index = head_at // quarters
    quarter = head_at % quarters
    kv_group = jnp.take(head_list, slot_index)
    q_groups = q_span.reshape(tok_rows, KVH, group_width)
    kv_groups = jnp.concatenate(
        [k_span.reshape(tok_rows, KVH, head_dim), v_span.reshape(tok_rows, KVH, head_dim)], axis=2
    )
    targets = jnp.take(head_list, jnp.arange(head_count * pair_count) // pair_count // quarters)
    q_send = jnp.take(q_groups, targets, axis=1)
    kv_send = jnp.take(kv_groups, targets, axis=1)
    q_recv, kv_recv = (
        lax.all_to_all(q_send, ("head", "seq"), split_axis=1, concat_axis=0, tiled=True),
        lax.all_to_all(kv_send, ("head", "seq"), split_axis=1, concat_axis=0, tiled=True),
    )
    queries = q_recv.reshape(total_q, group_width)
    span_kv = kv_recv.reshape(total_q, 2 * head_dim)
    query_rows = queries.reshape(total_q * group_heads, head_dim)
    query_pos = context + jnp.arange(total_q * group_heads, dtype=jnp.int32) // group_heads
    is_retrieval = jnp.take(retrieval, kv_group)
    window_len = jnp.take(windows, kv_group)
    sink_len = jnp.take(sinks, kv_group)
    score_scale = 1.0 / math.sqrt(head_dim)
    row_total = total_q * group_heads
    running = (
        jnp.full((row_total,), NEG_FILL, jnp.float32),
        jnp.zeros((row_total,), jnp.float32),
        jnp.zeros((row_total, head_dim), jnp.float32),
    )
    key_block = min(512, ctx_dev)
    segment = quarter * pair_count + pair_at
    first_key = segment * ctx_dev
    cache_keys = k_cache[0]
    cache_values = v_cache[0]

    def key_step(step_index, state):
        start = step_index * key_block
        key_rows = lax.dynamic_slice_in_dim(cache_keys, start, key_block, 0)
        value_rows = lax.dynamic_slice_in_dim(cache_values, start, key_block, 0)
        key_pos = first_key + start + jnp.arange(key_block, dtype=jnp.int32)
        return absorb(
            state,
            query_rows,
            query_pos,
            key_rows,
            value_rows,
            key_pos,
            is_retrieval,
            window_len,
            sink_len,
            score_scale,
        )

    running = lax.fori_loop(0, ctx_dev // key_block, key_step, running)
    span_piece = total_q // (quarters * pair_count)
    span_start = segment * span_piece
    span_rows = lax.dynamic_slice_in_dim(span_kv, span_start, span_piece, 0)
    span_pos = context + span_start + jnp.arange(span_piece, dtype=jnp.int32)
    top_score, totals, weighted = absorb(
        running,
        query_rows,
        query_pos,
        span_rows[:, :head_dim],
        span_rows[:, head_dim:],
        span_pos,
        is_retrieval,
        window_len,
        sink_len,
        score_scale,
    )
    received = (
        lax.all_to_all(
            top_score.reshape(head_count * pair_count, tok_rows, group_heads),
            ("head", "seq"),
            split_axis=0,
            concat_axis=0,
            tiled=True,
        ),
        lax.all_to_all(
            totals.reshape(head_count * pair_count, tok_rows, group_heads),
            ("head", "seq"),
            split_axis=0,
            concat_axis=0,
            tiled=True,
        ),
        lax.all_to_all(
            weighted.reshape(head_count * pair_count, tok_rows, group_width),
            ("head", "seq"),
            split_axis=0,
            concat_axis=0,
            tiled=True,
        ),
    )
    spread = quarters * pair_count
    return finish_rows(received, spread, head_list, tok_rows, head_dim)


VMEM_SPEC = pl.BlockSpec(memory_space=pltpu.VMEM)
HBM_SPEC = pl.BlockSpec(memory_space=pltpu.HBM)
SMEM_SPEC = pl.BlockSpec(memory_space=pltpu.SMEM)


def pack_kernel(head_ref, in_ref, out_ref, *, group_width, head_dim):
    q_width = KVH * group_width
    q_ref = in_ref.at[:, :q_width]
    k_ref = in_ref.at[:, q_width : q_width + KVH * head_dim]
    v_ref = in_ref.at[:, q_width + KVH * head_dim :]
    for slot in range(out_ref.shape[0]):
        group = head_ref[slot]
        q_start = pl.multiple_of(group * group_width, 128)
        kv_start = pl.multiple_of(group * head_dim, 128)
        out_ref[slot, :, :group_width] = q_ref[:, pl.ds(q_start, group_width)]
        out_ref[slot, :, group_width : group_width + head_dim] = k_ref[:, pl.ds(kv_start, head_dim)]
        out_ref[slot, :, group_width + head_dim :] = v_ref[:, pl.ds(kv_start, head_dim)]


def unpack_kernel(head_ref, in_ref, out_ref, sems):
    width = in_ref.shape[2]
    copies = []
    for slot in range(in_ref.shape[0]):
        start = pl.multiple_of(head_ref[slot] * width, 128)
        copies.append(
            pltpu.make_async_copy(in_ref.at[slot], out_ref.at[:, pl.ds(start, width)], sems.at[slot])
        )
    for copy in copies:
        copy.start()
    for copy in copies:
        copy.wait()


def stack_queries(recv_ref, group_heads, head_dim):
    scale = math.log2(math.e) / math.sqrt(head_dim)
    queries = jnp.concatenate(
        [recv_ref[:, k * head_dim : (k + 1) * head_dim] for k in range(group_heads)], axis=0
    )
    scaled = queries.astype(jnp.float32) * scale
    high = scaled.astype(jnp.bfloat16)
    low = (scaled - high.astype(jnp.float32)).astype(jnp.bfloat16)
    return jnp.concatenate([high, low], axis=1)


def span_kernel(
    head_ref,
    retrieval_ref,
    window_ref,
    sink_ref,
    recv_ref,
    peer_ref,
    acc_ref,
    stat_ref,
    out_ref,
    *,
    tok_rows,
    group_heads,
    head_dim,
    context,
):
    f32, bf16 = jnp.float32, jnp.bfloat16
    pair_at = lax.axis_index("seq")
    kv_group = head_ref[lax.axis_index("head")]
    is_retrieval = retrieval_ref[kv_group]
    window_len = jnp.where(is_retrieval == 1, 2**30, window_ref[kv_group])
    sink_len = sink_ref[kv_group]
    tokens = recv_ref.shape[0]
    rows = tokens * group_heads
    group_width = group_heads * head_dim
    queries = stack_queries(recv_ref, group_heads, head_dim)

    def token_pos(index, pair):
        return context + ((index // tok_rows) * 2 + pair) * tok_rows + index % tok_rows

    query_pos = token_pos(lax.broadcasted_iota(jnp.int32, (1, rows), 1) % tokens, pair_at)
    key_pos = token_pos(lax.broadcasted_iota(jnp.int32, (tokens, 1), 0), 1 - pair_at)
    keys = peer_ref[:, group_width : group_width + head_dim]
    values = peer_ref[:, group_width + head_dim : group_width + 2 * head_dim]
    block = lax.dot_general(
        jnp.concatenate([keys, keys], axis=1),
        queries,
        (((1,), (1,)), ((), ())),
        preferred_element_type=f32,
    )
    allowed = (key_pos <= query_pos) & ((key_pos < sink_len) | (key_pos > query_pos - window_len))
    block = jnp.where(allowed, block, NEG_FILL)
    old_top = stat_ref[0:1, :]
    top = jnp.maximum(old_top, jnp.max(block, axis=0, keepdims=True))
    factor = jnp.exp2(old_top - top)
    weights = jnp.exp2(block - top)
    total = jnp.sum(stat_ref[8:16, :], axis=0, keepdims=True) * factor
    total = total + jnp.sum(weights, axis=0, keepdims=True)
    acc = acc_ref[...] * factor + lax.dot_general(
        values, weights.astype(bf16), (((0,), (0,)), ((), ())), preferred_element_type=f32
    )
    result = (acc / total).T.astype(bf16)
    for head in range(group_heads):
        out_ref[:, head * head_dim : (head + 1) * head_dim] = result[head * tokens : (head + 1) * tokens]


def attend_kernel(
    head_ref,
    retrieval_ref,
    window_ref,
    sink_ref,
    recv_ref,
    k_peer,
    v_peer,
    k_source,
    v_source,
    acc_ref,
    stat_ref,
    k_own,
    v_own,
    score_ref,
    own_sem,
    *,
    tok_rows,
    group_heads,
    head_dim,
    key_block,
    row_block,
):
    k_copy = pltpu.make_async_copy(k_source, k_own, own_sem.at[0])
    v_copy = pltpu.make_async_copy(v_source, v_own, own_sem.at[1])
    k_copy.start()
    pair_at = lax.axis_index("seq")
    kv_group = head_ref[lax.axis_index("head")]
    is_retrieval = retrieval_ref[kv_group]
    window_len = window_ref[kv_group]
    sink_len = sink_ref[kv_group]
    tokens = recv_ref.shape[0]
    rows = tokens * group_heads
    group_width = group_heads * head_dim
    ctx_dev = k_own.shape[0]
    context = 2 * ctx_dev
    f32, bf16 = jnp.float32, jnp.bfloat16
    def token_pos(index, pair):
        return context + ((index // tok_rows) * 2 + pair) * tok_rows + index % tok_rows

    queries = stack_queries(recv_ref, group_heads, head_dim)
    row_token = lax.broadcasted_iota(jnp.int32, (1, rows), 1) % tokens
    query_pos = token_pos(row_token, pair_at)

    span_k = pl.ds(group_width, head_dim)
    span_v = pl.ds(group_width + head_dim, head_dim)
    cached, spans = [], []
    for k_ref, v_ref, pair in ((k_peer, v_peer, 1 - pair_at), (k_own, v_own, pair_at)):
        for start in range(0, ctx_dev, key_block):
            cached.append((k_ref, v_ref, start, key_block, pair))
    spans.append((recv_ref, pair_at))

    def load_keys(index):
        if index < len(cached):
            k_ref, _, start, size, _ = cached[index]
            return k_ref[start : start + size, :]
        return spans[index - len(cached)][0][:, span_k]

    def load_values(index):
        if index < len(cached):
            _, v_ref, start, size, _ = cached[index]
            return v_ref[start : start + size, :]
        return spans[index - len(cached)][0][:, span_v]

    def place(index):
        if index < len(cached):
            return index * key_block, key_block
        return len(cached) * key_block + (index - len(cached)) * tokens, tokens

    def first_pos(index):
        _, _, start, _, pair = cached[index]
        return pair * ctx_dev + start

    def scores(index, row_at, masked):
        keys = load_keys(index)
        keys = jnp.concatenate([keys, keys], axis=1)
        block = lax.dot_general(
            keys,
            queries[row_at : row_at + row_block],
            (((1,), (1,)), ((), ())),
            preferred_element_type=f32,
        )
        size = block.shape[0]
        pos_q = query_pos[:, row_at : row_at + row_block]
        column = lax.broadcasted_iota(jnp.int32, (size, 1), 0)
        allowed = None
        if index >= len(cached):
            pos_k = token_pos(column, spans[index - len(cached)][1])
            allowed = pos_k <= pos_q
        else:
            pos_k = first_pos(index) + column
        if masked:
            near = (pos_k < sink_len) | (pos_k > pos_q - window_len)
            allowed = near if allowed is None else allowed & near
        if allowed is not None:
            block = jnp.where(allowed, block, NEG_FILL)
        start, _ = place(index)
        score_ref[start : start + size, row_at : row_at + row_block] = block
        return jnp.max(block.reshape(size // 8, 8, row_block), axis=0)

    def weighted(index, row_at, top):
        start, size = place(index)
        block = score_ref[start : start + size, row_at : row_at + row_block]
        weights = jnp.exp2(block - top)
        total = jnp.sum(weights.reshape(size // 8, 8, row_block), axis=0)
        acc = lax.dot_general(
            load_values(index),
            weights.astype(bf16),
            (((0,), (0,)), ((), ())),
            preferred_element_type=f32,
        )
        return total, acc

    blocks = len(cached) + len(spans)
    row_starts = list(range(0, rows, row_block))

    half = len(cached) // 2
    peer_blocks = list(range(half))
    own_blocks = list(range(half, blocks))

    @pl.when(is_retrieval == 1)
    def _():
        running, total, acc = {}, {}, {}

        def first(indices):
            for row_at in row_starts:
                for index in indices:
                    top = scores(index, row_at, False)
                    running[row_at] = jnp.maximum(running[row_at], top) if row_at in running else top

        def second(indices):
            for row_at in row_starts:
                top = jnp.max(running[row_at], axis=0, keepdims=True)
                for index in indices:
                    part_total, part_acc = weighted(index, row_at, top)
                    total[row_at] = total[row_at] + part_total if row_at in total else part_total
                    acc[row_at] = acc[row_at] + part_acc if row_at in acc else part_acc

        first(peer_blocks)
        k_copy.wait()
        v_copy.start()
        first(own_blocks)
        second(peer_blocks)
        v_copy.wait()
        second(own_blocks)
        for row_at in row_starts:
            cols = slice(row_at, row_at + row_block)
            top = jnp.max(running[row_at], axis=0, keepdims=True)
            stat_ref[0:8, cols] = jnp.broadcast_to(top, (8, row_block))
            stat_ref[8:16, cols] = total[row_at]
            acc_ref[:, cols] = acc[row_at]

    @pl.when(is_retrieval != 1)
    def _():
        def needed(index):
            pos = first_pos(index)
            return (pos < sink_len) | (pos + key_block - 1 > context - window_len)

        stat_ref[0:8, :] = jnp.full((8, rows), NEG_FILL, f32)
        stat_ref[8:16, :] = jnp.zeros((8, rows), f32)
        acc_ref[...] = jnp.zeros(acc_ref.shape, f32)

        def first(index):
            for row_at in row_starts:
                cols = slice(row_at, row_at + row_block)
                stat_ref[0:8, cols] = jnp.maximum(stat_ref[0:8, cols], scores(index, row_at, True))

        def second(index):
            for row_at in row_starts:
                cols = slice(row_at, row_at + row_block)
                top = jnp.max(stat_ref[0:8, cols], axis=0, keepdims=True)
                total, acc = weighted(index, row_at, top)
                stat_ref[8:16, cols] += total
                acc_ref[:, cols] += acc

        def each(work, indices):
            for index in indices:
                if index < len(cached):
                    pl.when(needed(index))(functools.partial(work, index))
                else:
                    work(index)

        each(first, peer_blocks)
        k_copy.wait()
        v_copy.start()
        each(first, own_blocks)
        each(second, peer_blocks)
        v_copy.wait()
        each(second, own_blocks)
        top = jnp.max(stat_ref[0:8, :], axis=0, keepdims=True)
        stat_ref[0:8, :] = jnp.broadcast_to(top, (8, rows))


def on_device_pairs(q_span, k_span, v_span, k_cache, v_cache, head_list, retrieval, windows, sinks):
    head_count = lax.axis_size("head")
    tok_rows = q_span.shape[0]
    group_width = q_span.shape[1] // KVH
    head_dim = k_cache.shape[2]
    group_heads = group_width // head_dim
    ctx_dev = k_cache.shape[1]
    tokens = tok_rows * head_count
    rows = tokens * group_heads
    swap = [(0, 1), (1, 0)]
    k_own, v_own = k_cache[0], v_cache[0]
    k_peer = lax.ppermute(k_own, "seq", swap)
    v_peer = lax.ppermute(v_own, "seq", swap)
    joined = jnp.concatenate([q_span, k_span, v_span], axis=1)
    send = pl.pallas_call(
        functools.partial(pack_kernel, group_width=group_width, head_dim=head_dim),
        out_shape=jax.ShapeDtypeStruct((head_count, tok_rows, group_width + 2 * head_dim), jnp.bfloat16),
        in_specs=[SMEM_SPEC, VMEM_SPEC],
        out_specs=VMEM_SPEC,
        compiler_params=pltpu.CompilerParams(vmem_limit_bytes=2**20),
    )(head_list, lax.optimization_barrier(joined))
    recv = lax.all_to_all(send, "head", split_axis=0, concat_axis=0, tiled=True)
    recv = recv.reshape(tokens, group_width + 2 * head_dim)
    peer = lax.ppermute(recv, "seq", swap)
    key_block = math.gcd(ctx_dev, 1024)
    row_block = 256
    keys = 2 * ctx_dev + tokens
    acc, stat = pl.pallas_call(
        functools.partial(
            attend_kernel,
            tok_rows=tok_rows,
            group_heads=group_heads,
            head_dim=head_dim,
            key_block=key_block,
            row_block=row_block,
        ),
        out_shape=(
            jax.ShapeDtypeStruct((head_dim, rows), jnp.float32),
            jax.ShapeDtypeStruct((16, rows), jnp.float32),
        ),
        in_specs=[SMEM_SPEC] * 4 + [VMEM_SPEC] * 3 + [HBM_SPEC] * 2,
        out_specs=(VMEM_SPEC, VMEM_SPEC),
        scratch_shapes=[
            pltpu.VMEM((ctx_dev, head_dim), jnp.bfloat16),
            pltpu.VMEM((ctx_dev, head_dim), jnp.bfloat16),
            pltpu.VMEM((keys, rows), jnp.float32),
            pltpu.SemaphoreType.DMA((2,)),
        ],
        compiler_params=pltpu.CompilerParams(vmem_limit_bytes=51 * 2**20),
    )(head_list, retrieval, windows, sinks, recv, k_peer, v_peer, k_own, v_own)
    result = pl.pallas_call(
        functools.partial(
            span_kernel,
            tok_rows=tok_rows,
            group_heads=group_heads,
            head_dim=head_dim,
            context=2 * ctx_dev,
        ),
        out_shape=jax.ShapeDtypeStruct((tokens, group_width), jnp.bfloat16),
        in_specs=[SMEM_SPEC] * 4 + [VMEM_SPEC] * 4,
        out_specs=VMEM_SPEC,
        compiler_params=pltpu.CompilerParams(vmem_limit_bytes=4 * 2**20),
    )(head_list, retrieval, windows, sinks, recv, peer, acc, stat)
    result = result.reshape(head_count, tok_rows, group_width)
    back = lax.all_to_all(result, "head", split_axis=0, concat_axis=0, tiled=True)
    return pl.pallas_call(
        unpack_kernel,
        out_shape=jax.ShapeDtypeStruct((tok_rows, KVH * group_width), jnp.bfloat16),
        in_specs=[SMEM_SPEC, VMEM_SPEC],
        out_specs=HBM_SPEC,
        scratch_shapes=[pltpu.SemaphoreType.DMA((head_count,))],
        compiler_params=pltpu.CompilerParams(vmem_limit_bytes=2**20),
    )(head_list, back)


def solution(mesh):
    on_device = on_device_pairs if mesh.shape["head"] == KVH else on_device_quarters
    in_specs = (
        P(("rep", "head", "seq"), None),
        P(("rep", "head", "seq"), None),
        P(("rep", "head", "seq"), None),
        P(("rep", "head"), "seq", None),
        P(("rep", "head"), "seq", None),
        P("rep"),
        P("rep"),
        P("rep"),
        P("rep"),
    )
    out_specs = P(("rep", "head", "seq"), None)
    return jax.shard_map(
        on_device, mesh=mesh, in_specs=in_specs, out_specs=out_specs, check_vma=False
    )
```

```python
import functools
import math

import jax
import jax.numpy as jnp
from jax import lax
from jax.experimental import pallas as pl
from jax.experimental.pallas import tpu as pltpu
from jax.sharding import PartitionSpec as P

KVH = 8


NEG_FILL = -1e30


def absorb(
    running,
    query_rows,
    query_pos,
    key_rows,
    value_rows,
    key_pos,
    is_retrieval,
    window_len,
    sink_len,
    score_scale,
):
    top_score, totals, weighted = running
    scores = jnp.dot(query_rows, key_rows.T, preferred_element_type=jnp.float32) * score_scale
    allowed = (key_pos[None, :] <= query_pos[:, None]) & (
        (is_retrieval == 1)
        | (key_pos[None, :] < sink_len)
        | (key_pos[None, :] > query_pos[:, None] - window_len)
    )
    block_top = jnp.max(jnp.where(allowed, scores, NEG_FILL), axis=1)
    new_top = jnp.maximum(top_score, block_top)
    weights = jnp.where(allowed, jnp.exp(scores - new_top[:, None]), 0.0)
    rescale = jnp.exp(top_score - new_top)
    totals = totals * rescale + jnp.sum(weights, axis=1)
    weighted = weighted * rescale[:, None] + jnp.dot(
        weights.astype(jnp.bfloat16), value_rows, preferred_element_type=jnp.float32
    )
    return (new_top, totals, weighted)


def finish_rows(received, spread, head_list, tok_rows, head_dim):
    top_score, totals, weighted = received
    group_heads = top_score.shape[-1]
    top_score = top_score.reshape(KVH, spread, tok_rows, group_heads)
    totals = totals.reshape(KVH, spread, tok_rows, group_heads)
    weighted = weighted.reshape(KVH, spread, tok_rows, group_heads, head_dim)
    overall = jnp.max(top_score, axis=1, keepdims=True)
    factor = jnp.exp(top_score - overall)
    summed = jnp.sum(totals * factor, axis=1)
    combined = jnp.sum(weighted * factor[..., None], axis=1)
    result = combined / summed[..., None]
    matches = (head_list[:, None] == jnp.arange(KVH, dtype=jnp.int32)[None, :]).astype(jnp.int32)
    inverse = jnp.sum(jnp.arange(KVH, dtype=jnp.int32)[:, None] * matches, axis=0)
    by_group = jnp.take(result, inverse, axis=0)
    return (
        by_group.transpose(1, 0, 2, 3)
        .reshape(tok_rows, KVH * group_heads * head_dim)
        .astype(jnp.bfloat16)
    )


def on_device_quarters(q_span, k_span, v_span, k_cache, v_cache, head_list, retrieval, windows, sinks):
    head_count = lax.axis_size("head")
    pair_count = lax.axis_size("seq")
    quarters = head_count // KVH
    tok_rows = q_span.shape[0]
    group_width = q_span.shape[1] // KVH
    head_dim = k_cache.shape[2]
    group_heads = group_width // head_dim
    ctx_dev = k_cache.shape[1]
    total_q = tok_rows * head_count * pair_count
    context = ctx_dev * pair_count * quarters
    head_at = lax.axis_index("head")
    pair_at = lax.axis_index("seq")
    slot_index = head_at // quarters
    quarter = head_at % quarters
    kv_group = jnp.take(head_list, slot_index)
    q_groups = q_span.reshape(tok_rows, KVH, group_width)
    kv_groups = jnp.concatenate(
        [k_span.reshape(tok_rows, KVH, head_dim), v_span.reshape(tok_rows, KVH, head_dim)], axis=2
    )
    targets = jnp.take(head_list, jnp.arange(head_count * pair_count) // pair_count // quarters)
    q_send = jnp.take(q_groups, targets, axis=1)
    kv_send = jnp.take(kv_groups, targets, axis=1)
    q_recv, kv_recv = (
        lax.all_to_all(q_send, ("head", "seq"), split_axis=1, concat_axis=0, tiled=True),
        lax.all_to_all(kv_send, ("head", "seq"), split_axis=1, concat_axis=0, tiled=True),
    )
    queries = q_recv.reshape(total_q, group_width)
    span_kv = kv_recv.reshape(total_q, 2 * head_dim)
    query_rows = queries.reshape(total_q * group_heads, head_dim)
    query_pos = context + jnp.arange(total_q * group_heads, dtype=jnp.int32) // group_heads
    is_retrieval = jnp.take(retrieval, kv_group)
    window_len = jnp.take(windows, kv_group)
    sink_len = jnp.take(sinks, kv_group)
    score_scale = 1.0 / math.sqrt(head_dim)
    row_total = total_q * group_heads
    running = (
        jnp.full((row_total,), NEG_FILL, jnp.float32),
        jnp.zeros((row_total,), jnp.float32),
        jnp.zeros((row_total, head_dim), jnp.float32),
    )
    key_block = min(512, ctx_dev)
    segment = quarter * pair_count + pair_at
    first_key = segment * ctx_dev
    cache_keys = k_cache[0]
    cache_values = v_cache[0]

    def key_step(step_index, state):
        start = step_index * key_block
        key_rows = lax.dynamic_slice_in_dim(cache_keys, start, key_block, 0)
        value_rows = lax.dynamic_slice_in_dim(cache_values, start, key_block, 0)
        key_pos = first_key + start + jnp.arange(key_block, dtype=jnp.int32)
        return absorb(
            state,
            query_rows,
            query_pos,
            key_rows,
            value_rows,
            key_pos,
            is_retrieval,
            window_len,
            sink_len,
            score_scale,
        )

    running = lax.fori_loop(0, ctx_dev // key_block, key_step, running)
    span_piece = total_q // (quarters * pair_count)
    span_start = segment * span_piece
    span_rows = lax.dynamic_slice_in_dim(span_kv, span_start, span_piece, 0)
    span_pos = context + span_start + jnp.arange(span_piece, dtype=jnp.int32)
    top_score, totals, weighted = absorb(
        running,
        query_rows,
        query_pos,
        span_rows[:, :head_dim],
        span_rows[:, head_dim:],
        span_pos,
        is_retrieval,
        window_len,
        sink_len,
        score_scale,
    )
    received = (
        lax.all_to_all(
            top_score.reshape(head_count * pair_count, tok_rows, group_heads),
            ("head", "seq"),
            split_axis=0,
            concat_axis=0,
            tiled=True,
        ),
        lax.all_to_all(
            totals.reshape(head_count * pair_count, tok_rows, group_heads),
            ("head", "seq"),
            split_axis=0,
            concat_axis=0,
            tiled=True,
        ),
        lax.all_to_all(
            weighted.reshape(head_count * pair_count, tok_rows, group_width),
            ("head", "seq"),
            split_axis=0,
            concat_axis=0,
            tiled=True,
        ),
    )
    spread = quarters * pair_count
    return finish_rows(received, spread, head_list, tok_rows, head_dim)


VMEM_SPEC = pl.BlockSpec(memory_space=pltpu.VMEM)
HBM_SPEC = pl.BlockSpec(memory_space=pltpu.HBM)
SMEM_SPEC = pl.BlockSpec(memory_space=pltpu.SMEM)


def pack_kernel(
    head_ref, retrieval_ref, window_ref, sink_ref, in_ref, out_ref, info_ref, *, group_width, head_dim
):
    kv_group = head_ref[lax.axis_index("head")]
    info_ref[0] = retrieval_ref[kv_group]
    info_ref[1] = window_ref[kv_group]
    info_ref[2] = sink_ref[kv_group]
    q_width = KVH * group_width
    q_ref = in_ref.at[:, :q_width]
    k_ref = in_ref.at[:, q_width : q_width + KVH * head_dim]
    v_ref = in_ref.at[:, q_width + KVH * head_dim :]
    for slot in range(out_ref.shape[0]):
        group = head_ref[slot]
        q_start = pl.multiple_of(group * group_width, 128)
        kv_start = pl.multiple_of(group * head_dim, 128)
        out_ref[slot, :, :group_width] = q_ref[:, pl.ds(q_start, group_width)]
        out_ref[slot, :, group_width : group_width + head_dim] = k_ref[:, pl.ds(kv_start, head_dim)]
        out_ref[slot, :, group_width + head_dim :] = v_ref[:, pl.ds(kv_start, head_dim)]


def unpack_kernel(head_ref, in_ref, out_ref, sems):
    width = in_ref.shape[2]
    copies = []
    for slot in range(in_ref.shape[0]):
        start = pl.multiple_of(head_ref[slot] * width, 128)
        copies.append(
            pltpu.make_async_copy(in_ref.at[slot], out_ref.at[:, pl.ds(start, width)], sems.at[slot])
        )
    for copy in copies:
        copy.start()
    for copy in copies:
        copy.wait()


def stack_queries(recv_ref, group_heads, head_dim):
    scale = math.log2(math.e) / math.sqrt(head_dim)
    queries = jnp.concatenate(
        [recv_ref[:, k * head_dim : (k + 1) * head_dim] for k in range(group_heads)], axis=0
    )
    scaled = queries.astype(jnp.float32) * scale
    high = scaled.astype(jnp.bfloat16)
    low = (scaled - high.astype(jnp.float32)).astype(jnp.bfloat16)
    return jnp.concatenate([high, low], axis=1)


def span_kernel(
    info_ref,
    recv_ref,
    peer_ref,
    acc_ref,
    stat_ref,
    out_ref,
    *,
    tok_rows,
    group_heads,
    head_dim,
    context,
):
    f32, bf16 = jnp.float32, jnp.bfloat16
    pair_at = lax.axis_index("seq")
    window_len = jnp.where(info_ref[0] == 1, 2**30, info_ref[1])
    sink_len = info_ref[2]
    tokens = recv_ref.shape[0]
    rows = tokens * group_heads
    group_width = group_heads * head_dim
    queries = stack_queries(recv_ref, group_heads, head_dim)

    def token_pos(index, pair):
        return context + ((index // tok_rows) * 2 + pair) * tok_rows + index % tok_rows

    query_pos = token_pos(lax.broadcasted_iota(jnp.int32, (1, rows), 1) % tokens, pair_at)
    key_pos = token_pos(lax.broadcasted_iota(jnp.int32, (tokens, 1), 0), 1 - pair_at)
    keys = peer_ref[:, group_width : group_width + head_dim]
    values = peer_ref[:, group_width + head_dim : group_width + 2 * head_dim]
    block = lax.dot_general(
        jnp.concatenate([keys, keys], axis=1),
        queries,
        (((1,), (1,)), ((), ())),
        preferred_element_type=f32,
    )
    allowed = (key_pos <= query_pos) & ((key_pos < sink_len) | (key_pos > query_pos - window_len))
    block = jnp.where(allowed, block, NEG_FILL)
    old_top = stat_ref[0:1, :]
    top = jnp.maximum(old_top, jnp.max(block, axis=0, keepdims=True))
    factor = jnp.exp2(old_top - top)
    weights = jnp.exp2(block - top)
    total = jnp.sum(stat_ref[8:16, :], axis=0, keepdims=True) * factor
    total = total + jnp.sum(weights, axis=0, keepdims=True)
    acc = acc_ref[...] * factor + lax.dot_general(
        values, weights.astype(bf16), (((0,), (0,)), ((), ())), preferred_element_type=f32
    )
    result = (acc / total).T.astype(bf16)
    for head in range(group_heads):
        out_ref[:, head * head_dim : (head + 1) * head_dim] = result[head * tokens : (head + 1) * tokens]


def attend_kernel(
    info_ref,
    recv_ref,
    k_peer,
    v_peer,
    k_source,
    v_source,
    acc_ref,
    stat_ref,
    k_own,
    v_own,
    score_ref,
    own_sem,
    *,
    tok_rows,
    group_heads,
    head_dim,
    key_block,
    row_block,
):
    k_copy = pltpu.make_async_copy(k_source, k_own, own_sem.at[0])
    v_copy = pltpu.make_async_copy(v_source, v_own, own_sem.at[1])
    k_copy.start()
    pair_at = lax.axis_index("seq")
    is_retrieval, window_len, sink_len = (info_ref[i] for i in range(3))
    tokens = recv_ref.shape[0]
    rows = tokens * group_heads
    group_width = group_heads * head_dim
    ctx_dev = k_own.shape[0]
    context = 2 * ctx_dev
    f32, bf16 = jnp.float32, jnp.bfloat16
    def token_pos(index, pair):
        return context + ((index // tok_rows) * 2 + pair) * tok_rows + index % tok_rows

    queries = stack_queries(recv_ref, group_heads, head_dim)
    row_token = lax.broadcasted_iota(jnp.int32, (1, rows), 1) % tokens
    query_pos = token_pos(row_token, pair_at)

    span_k = pl.ds(group_width, head_dim)
    span_v = pl.ds(group_width + head_dim, head_dim)
    cached, spans = [], []
    for k_ref, v_ref, pair in ((k_peer, v_peer, 1 - pair_at), (k_own, v_own, pair_at)):
        for start in range(0, ctx_dev, key_block):
            cached.append((k_ref, v_ref, start, key_block, pair))
    spans.append((recv_ref, pair_at))

    def load_keys(index):
        if index < len(cached):
            k_ref, _, start, size, _ = cached[index]
            return k_ref[start : start + size, :]
        return spans[index - len(cached)][0][:, span_k]

    def load_values(index):
        if index < len(cached):
            _, v_ref, start, size, _ = cached[index]
            return v_ref[start : start + size, :]
        return spans[index - len(cached)][0][:, span_v]

    def place(index):
        if index < len(cached):
            return index * key_block, key_block
        return len(cached) * key_block + (index - len(cached)) * tokens, tokens

    def first_pos(index):
        _, _, start, _, pair = cached[index]
        return pair * ctx_dev + start

    def scores(index, row_at, masked):
        keys = load_keys(index)
        keys = jnp.concatenate([keys, keys], axis=1)
        block = lax.dot_general(
            keys,
            queries[row_at : row_at + row_block],
            (((1,), (1,)), ((), ())),
            preferred_element_type=f32,
        )
        size = block.shape[0]
        pos_q = query_pos[:, row_at : row_at + row_block]
        column = lax.broadcasted_iota(jnp.int32, (size, 1), 0)
        allowed = None
        if index >= len(cached):
            pos_k = token_pos(column, spans[index - len(cached)][1])
            allowed = pos_k <= pos_q
        else:
            pos_k = first_pos(index) + column
        if masked:
            near = (pos_k < sink_len) | (pos_k > pos_q - window_len)
            allowed = near if allowed is None else allowed & near
        if allowed is not None:
            block = jnp.where(allowed, block, NEG_FILL)
        start, _ = place(index)
        score_ref[start : start + size, row_at : row_at + row_block] = block
        return jnp.max(block.reshape(size // 8, 8, row_block), axis=0)

    def weighted(index, row_at, top):
        start, size = place(index)
        block = score_ref[start : start + size, row_at : row_at + row_block]
        weights = jnp.exp2(block - top)
        total = jnp.sum(weights.reshape(size // 8, 8, row_block), axis=0)
        acc = lax.dot_general(
            load_values(index),
            weights.astype(bf16),
            (((0,), (0,)), ((), ())),
            preferred_element_type=f32,
        )
        return total, acc

    blocks = len(cached) + len(spans)
    row_starts = list(range(0, rows, row_block))

    half = len(cached) // 2
    peer_blocks = list(range(half))
    own_blocks = list(range(half, blocks))

    @pl.when(is_retrieval == 1)
    def _():
        running, total, acc = {}, {}, {}

        def first(indices):
            for row_at in row_starts:
                for index in indices:
                    top = scores(index, row_at, False)
                    running[row_at] = jnp.maximum(running[row_at], top) if row_at in running else top

        def second(indices):
            for row_at in row_starts:
                top = jnp.max(running[row_at], axis=0, keepdims=True)
                for index in indices:
                    part_total, part_acc = weighted(index, row_at, top)
                    total[row_at] = total[row_at] + part_total if row_at in total else part_total
                    acc[row_at] = acc[row_at] + part_acc if row_at in acc else part_acc

        first(peer_blocks)
        k_copy.wait()
        v_copy.start()
        first(own_blocks)
        second(peer_blocks)
        v_copy.wait()
        second(own_blocks)
        for row_at in row_starts:
            cols = slice(row_at, row_at + row_block)
            top = jnp.max(running[row_at], axis=0, keepdims=True)
            stat_ref[0:8, cols] = jnp.broadcast_to(top, (8, row_block))
            stat_ref[8:16, cols] = total[row_at]
            acc_ref[:, cols] = acc[row_at]

    @pl.when(is_retrieval != 1)
    def _():
        def needed(index):
            pos = first_pos(index)
            return (pos < sink_len) | (pos + key_block - 1 > context - window_len)

        stat_ref[0:8, :] = jnp.full((8, rows), NEG_FILL, f32)
        stat_ref[8:16, :] = jnp.zeros((8, rows), f32)
        acc_ref[...] = jnp.zeros(acc_ref.shape, f32)

        def first(index):
            for row_at in row_starts:
                cols = slice(row_at, row_at + row_block)
                stat_ref[0:8, cols] = jnp.maximum(stat_ref[0:8, cols], scores(index, row_at, True))

        def second(index):
            for row_at in row_starts:
                cols = slice(row_at, row_at + row_block)
                top = jnp.max(stat_ref[0:8, cols], axis=0, keepdims=True)
                total, acc = weighted(index, row_at, top)
                stat_ref[8:16, cols] += total
                acc_ref[:, cols] += acc

        def each(work, indices):
            for index in indices:
                if index < len(cached):
                    pl.when(needed(index))(functools.partial(work, index))
                else:
                    work(index)

        each(first, peer_blocks)
        k_copy.wait()
        v_copy.start()
        each(first, own_blocks)
        each(second, peer_blocks)
        v_copy.wait()
        each(second, own_blocks)
        top = jnp.max(stat_ref[0:8, :], axis=0, keepdims=True)
        stat_ref[0:8, :] = jnp.broadcast_to(top, (8, rows))


def on_device_pairs(q_span, k_span, v_span, k_cache, v_cache, head_list, retrieval, windows, sinks):
    head_count = lax.axis_size("head")
    tok_rows = q_span.shape[0]
    group_width = q_span.shape[1] // KVH
    head_dim = k_cache.shape[2]
    group_heads = group_width // head_dim
    ctx_dev = k_cache.shape[1]
    tokens = tok_rows * head_count
    rows = tokens * group_heads
    swap = [(0, 1), (1, 0)]
    k_own, v_own = k_cache[0], v_cache[0]
    k_peer = lax.ppermute(k_own, "seq", swap)
    v_peer = lax.ppermute(v_own, "seq", swap)
    joined = jnp.concatenate([q_span, k_span, v_span], axis=1)
    send, info = pl.pallas_call(
        functools.partial(pack_kernel, group_width=group_width, head_dim=head_dim),
        out_shape=(
            jax.ShapeDtypeStruct((head_count, tok_rows, group_width + 2 * head_dim), jnp.bfloat16),
            jax.ShapeDtypeStruct((3,), jnp.int32),
        ),
        in_specs=[SMEM_SPEC] * 4 + [VMEM_SPEC],
        out_specs=(VMEM_SPEC, SMEM_SPEC),
        compiler_params=pltpu.CompilerParams(vmem_limit_bytes=2**20),
    )(head_list, retrieval, windows, sinks, lax.optimization_barrier(joined))
    recv = lax.all_to_all(send, "head", split_axis=0, concat_axis=0, tiled=True)
    recv = recv.reshape(tokens, group_width + 2 * head_dim)
    peer = lax.ppermute(recv, "seq", swap)
    key_block = math.gcd(ctx_dev, 1024)
    row_block = 256
    keys = 2 * ctx_dev + tokens
    acc, stat = pl.pallas_call(
        functools.partial(
            attend_kernel,
            tok_rows=tok_rows,
            group_heads=group_heads,
            head_dim=head_dim,
            key_block=key_block,
            row_block=row_block,
        ),
        out_shape=(
            jax.ShapeDtypeStruct((head_dim, rows), jnp.float32),
            jax.ShapeDtypeStruct((16, rows), jnp.float32),
        ),
        in_specs=[SMEM_SPEC] + [VMEM_SPEC] * 3 + [HBM_SPEC] * 2,
        out_specs=(VMEM_SPEC, VMEM_SPEC),
        scratch_shapes=[
            pltpu.VMEM((ctx_dev, head_dim), jnp.bfloat16),
            pltpu.VMEM((ctx_dev, head_dim), jnp.bfloat16),
            pltpu.VMEM((keys, rows), jnp.float32),
            pltpu.SemaphoreType.DMA((2,)),
        ],
        compiler_params=pltpu.CompilerParams(vmem_limit_bytes=51 * 2**20),
    )(info, recv, k_peer, v_peer, k_own, v_own)
    result = pl.pallas_call(
        functools.partial(
            span_kernel,
            tok_rows=tok_rows,
            group_heads=group_heads,
            head_dim=head_dim,
            context=2 * ctx_dev,
        ),
        out_shape=jax.ShapeDtypeStruct((tokens, group_width), jnp.bfloat16),
        in_specs=[SMEM_SPEC] + [VMEM_SPEC] * 4,
        out_specs=VMEM_SPEC,
        compiler_params=pltpu.CompilerParams(vmem_limit_bytes=4 * 2**20),
    )(info, recv, peer, acc, stat)
    result = result.reshape(head_count, tok_rows, group_width)
    back = lax.all_to_all(result, "head", split_axis=0, concat_axis=0, tiled=True)
    return pl.pallas_call(
        unpack_kernel,
        out_shape=jax.ShapeDtypeStruct((tok_rows, KVH * group_width), jnp.bfloat16),
        in_specs=[SMEM_SPEC, VMEM_SPEC],
        out_specs=HBM_SPEC,
        scratch_shapes=[pltpu.SemaphoreType.DMA((head_count,))],
        compiler_params=pltpu.CompilerParams(vmem_limit_bytes=2**20),
    )(head_list, back)


def solution(mesh):
    on_device = on_device_pairs if mesh.shape["head"] == KVH else on_device_quarters
    in_specs = (
        P(("rep", "head", "seq"), None),
        P(("rep", "head", "seq"), None),
        P(("rep", "head", "seq"), None),
        P(("rep", "head"), "seq", None),
        P(("rep", "head"), "seq", None),
        P("rep"),
        P("rep"),
        P("rep"),
        P("rep"),
    )
    out_specs = P(("rep", "head", "seq"), None)
    return jax.shard_map(
        on_device, mesh=mesh, in_specs=in_specs, out_specs=out_specs, check_vma=False
    )
```

```python
import functools
import math

import jax
import jax.numpy as jnp
from jax import lax
from jax.experimental import pallas as pl
from jax.experimental.pallas import tpu as pltpu
from jax.sharding import PartitionSpec as P

KVH = 8


NEG_FILL = -1e30


def absorb(
    running,
    query_rows,
    query_pos,
    key_rows,
    value_rows,
    key_pos,
    is_retrieval,
    window_len,
    sink_len,
    score_scale,
):
    top_score, totals, weighted = running
    scores = jnp.dot(query_rows, key_rows.T, preferred_element_type=jnp.float32) * score_scale
    allowed = (key_pos[None, :] <= query_pos[:, None]) & (
        (is_retrieval == 1)
        | (key_pos[None, :] < sink_len)
        | (key_pos[None, :] > query_pos[:, None] - window_len)
    )
    block_top = jnp.max(jnp.where(allowed, scores, NEG_FILL), axis=1)
    new_top = jnp.maximum(top_score, block_top)
    weights = jnp.where(allowed, jnp.exp(scores - new_top[:, None]), 0.0)
    rescale = jnp.exp(top_score - new_top)
    totals = totals * rescale + jnp.sum(weights, axis=1)
    weighted = weighted * rescale[:, None] + jnp.dot(
        weights.astype(jnp.bfloat16), value_rows, preferred_element_type=jnp.float32
    )
    return (new_top, totals, weighted)


def finish_rows(received, spread, head_list, tok_rows, head_dim):
    top_score, totals, weighted = received
    group_heads = top_score.shape[-1]
    top_score = top_score.reshape(KVH, spread, tok_rows, group_heads)
    totals = totals.reshape(KVH, spread, tok_rows, group_heads)
    weighted = weighted.reshape(KVH, spread, tok_rows, group_heads, head_dim)
    overall = jnp.max(top_score, axis=1, keepdims=True)
    factor = jnp.exp(top_score - overall)
    summed = jnp.sum(totals * factor, axis=1)
    combined = jnp.sum(weighted * factor[..., None], axis=1)
    result = combined / summed[..., None]
    matches = (head_list[:, None] == jnp.arange(KVH, dtype=jnp.int32)[None, :]).astype(jnp.int32)
    inverse = jnp.sum(jnp.arange(KVH, dtype=jnp.int32)[:, None] * matches, axis=0)
    by_group = jnp.take(result, inverse, axis=0)
    return (
        by_group.transpose(1, 0, 2, 3)
        .reshape(tok_rows, KVH * group_heads * head_dim)
        .astype(jnp.bfloat16)
    )


def on_device_quarters(q_span, k_span, v_span, k_cache, v_cache, head_list, retrieval, windows, sinks):
    head_count = lax.axis_size("head")
    pair_count = lax.axis_size("seq")
    quarters = head_count // KVH
    tok_rows = q_span.shape[0]
    group_width = q_span.shape[1] // KVH
    head_dim = k_cache.shape[2]
    group_heads = group_width // head_dim
    ctx_dev = k_cache.shape[1]
    total_q = tok_rows * head_count * pair_count
    context = ctx_dev * pair_count * quarters
    head_at = lax.axis_index("head")
    pair_at = lax.axis_index("seq")
    slot_index = head_at // quarters
    quarter = head_at % quarters
    kv_group = jnp.take(head_list, slot_index)
    q_groups = q_span.reshape(tok_rows, KVH, group_width)
    kv_groups = jnp.concatenate(
        [k_span.reshape(tok_rows, KVH, head_dim), v_span.reshape(tok_rows, KVH, head_dim)], axis=2
    )
    targets = jnp.take(head_list, jnp.arange(head_count * pair_count) // pair_count // quarters)
    q_send = jnp.take(q_groups, targets, axis=1)
    kv_send = jnp.take(kv_groups, targets, axis=1)
    q_recv, kv_recv = (
        lax.all_to_all(q_send, ("head", "seq"), split_axis=1, concat_axis=0, tiled=True),
        lax.all_to_all(kv_send, ("head", "seq"), split_axis=1, concat_axis=0, tiled=True),
    )
    queries = q_recv.reshape(total_q, group_width)
    span_kv = kv_recv.reshape(total_q, 2 * head_dim)
    query_rows = queries.reshape(total_q * group_heads, head_dim)
    query_pos = context + jnp.arange(total_q * group_heads, dtype=jnp.int32) // group_heads
    is_retrieval = jnp.take(retrieval, kv_group)
    window_len = jnp.take(windows, kv_group)
    sink_len = jnp.take(sinks, kv_group)
    score_scale = 1.0 / math.sqrt(head_dim)
    row_total = total_q * group_heads
    running = (
        jnp.full((row_total,), NEG_FILL, jnp.float32),
        jnp.zeros((row_total,), jnp.float32),
        jnp.zeros((row_total, head_dim), jnp.float32),
    )
    key_block = min(512, ctx_dev)
    segment = quarter * pair_count + pair_at
    first_key = segment * ctx_dev
    cache_keys = k_cache[0]
    cache_values = v_cache[0]

    def key_step(step_index, state):
        start = step_index * key_block
        key_rows = lax.dynamic_slice_in_dim(cache_keys, start, key_block, 0)
        value_rows = lax.dynamic_slice_in_dim(cache_values, start, key_block, 0)
        key_pos = first_key + start + jnp.arange(key_block, dtype=jnp.int32)
        return absorb(
            state,
            query_rows,
            query_pos,
            key_rows,
            value_rows,
            key_pos,
            is_retrieval,
            window_len,
            sink_len,
            score_scale,
        )

    running = lax.fori_loop(0, ctx_dev // key_block, key_step, running)
    span_piece = total_q // (quarters * pair_count)
    span_start = segment * span_piece
    span_rows = lax.dynamic_slice_in_dim(span_kv, span_start, span_piece, 0)
    span_pos = context + span_start + jnp.arange(span_piece, dtype=jnp.int32)
    top_score, totals, weighted = absorb(
        running,
        query_rows,
        query_pos,
        span_rows[:, :head_dim],
        span_rows[:, head_dim:],
        span_pos,
        is_retrieval,
        window_len,
        sink_len,
        score_scale,
    )
    received = (
        lax.all_to_all(
            top_score.reshape(head_count * pair_count, tok_rows, group_heads),
            ("head", "seq"),
            split_axis=0,
            concat_axis=0,
            tiled=True,
        ),
        lax.all_to_all(
            totals.reshape(head_count * pair_count, tok_rows, group_heads),
            ("head", "seq"),
            split_axis=0,
            concat_axis=0,
            tiled=True,
        ),
        lax.all_to_all(
            weighted.reshape(head_count * pair_count, tok_rows, group_width),
            ("head", "seq"),
            split_axis=0,
            concat_axis=0,
            tiled=True,
        ),
    )
    spread = quarters * pair_count
    return finish_rows(received, spread, head_list, tok_rows, head_dim)


VMEM_SPEC = pl.BlockSpec(memory_space=pltpu.VMEM)
HBM_SPEC = pl.BlockSpec(memory_space=pltpu.HBM)
SMEM_SPEC = pl.BlockSpec(memory_space=pltpu.SMEM)


def pack_kernel(head_ref, in_ref, out_ref, *, group_width, head_dim):
    q_width = KVH * group_width
    q_ref = in_ref.at[:, :q_width]
    k_ref = in_ref.at[:, q_width : q_width + KVH * head_dim]
    v_ref = in_ref.at[:, q_width + KVH * head_dim :]
    for slot in range(out_ref.shape[0]):
        group = head_ref[slot]
        q_start = pl.multiple_of(group * group_width, 128)
        kv_start = pl.multiple_of(group * head_dim, 128)
        out_ref[slot, :, :group_width] = q_ref[:, pl.ds(q_start, group_width)]
        out_ref[slot, :, group_width : group_width + head_dim] = k_ref[:, pl.ds(kv_start, head_dim)]
        out_ref[slot, :, group_width + head_dim :] = v_ref[:, pl.ds(kv_start, head_dim)]


def unpack_kernel(head_ref, in_ref, out_ref, sems):
    width = in_ref.shape[2]
    copies = []
    for slot in range(in_ref.shape[0]):
        start = pl.multiple_of(head_ref[slot] * width, 128)
        copies.append(
            pltpu.make_async_copy(in_ref.at[slot], out_ref.at[:, pl.ds(start, width)], sems.at[slot])
        )
    for copy in copies:
        copy.start()
    for copy in copies:
        copy.wait()


def look_up(table_ref):
    kv_group = table_ref[lax.axis_index("head")]
    return (table_ref[part * KVH + kv_group] for part in (1, 2, 3))


def stack_queries(recv_ref, group_heads, head_dim):
    scale = math.log2(math.e) / math.sqrt(head_dim)
    queries = jnp.concatenate(
        [recv_ref[:, k * head_dim : (k + 1) * head_dim] for k in range(group_heads)], axis=0
    )
    scaled = queries.astype(jnp.float32) * scale
    high = scaled.astype(jnp.bfloat16)
    low = (scaled - high.astype(jnp.float32)).astype(jnp.bfloat16)
    return jnp.concatenate([high, low], axis=1)


def span_kernel(
    table_ref,
    recv_ref,
    peer_ref,
    acc_ref,
    stat_ref,
    out_ref,
    *,
    tok_rows,
    group_heads,
    head_dim,
    context,
):
    f32, bf16 = jnp.float32, jnp.bfloat16
    pair_at = lax.axis_index("seq")
    is_retrieval, window_len, sink_len = look_up(table_ref)
    window_len = jnp.where(is_retrieval == 1, 2**30, window_len)
    tokens = recv_ref.shape[0]
    rows = tokens * group_heads
    group_width = group_heads * head_dim
    queries = stack_queries(recv_ref, group_heads, head_dim)

    def token_pos(index, pair):
        return context + ((index // tok_rows) * 2 + pair) * tok_rows + index % tok_rows

    query_pos = token_pos(lax.broadcasted_iota(jnp.int32, (1, rows), 1) % tokens, pair_at)
    key_pos = token_pos(lax.broadcasted_iota(jnp.int32, (tokens, 1), 0), 1 - pair_at)
    keys = peer_ref[:, group_width : group_width + head_dim]
    values = peer_ref[:, group_width + head_dim : group_width + 2 * head_dim]
    block = lax.dot_general(
        jnp.concatenate([keys, keys], axis=1),
        queries,
        (((1,), (1,)), ((), ())),
        preferred_element_type=f32,
    )
    allowed = (key_pos <= query_pos) & ((key_pos < sink_len) | (key_pos > query_pos - window_len))
    block = jnp.where(allowed, block, NEG_FILL)
    old_top = stat_ref[0:1, :]
    top = jnp.maximum(old_top, jnp.max(block, axis=0, keepdims=True))
    factor = jnp.exp2(old_top - top)
    weights = jnp.exp2(block - top)
    total = jnp.sum(stat_ref[8:16, :], axis=0, keepdims=True) * factor
    total = total + jnp.sum(weights, axis=0, keepdims=True)
    acc = acc_ref[...] * factor + lax.dot_general(
        values, weights.astype(bf16), (((0,), (0,)), ((), ())), preferred_element_type=f32
    )
    result = (acc / total).T.astype(bf16)
    for head in range(group_heads):
        out_ref[:, head * head_dim : (head + 1) * head_dim] = result[head * tokens : (head + 1) * tokens]


def attend_kernel(
    table_ref,
    recv_ref,
    k_peer,
    v_peer,
    k_source,
    v_source,
    acc_ref,
    stat_ref,
    k_own,
    v_own,
    score_ref,
    own_sem,
    *,
    tok_rows,
    group_heads,
    head_dim,
    key_block,
    row_block,
):
    k_copy = pltpu.make_async_copy(k_source, k_own, own_sem.at[0])
    v_copy = pltpu.make_async_copy(v_source, v_own, own_sem.at[1])
    k_copy.start()
    pair_at = lax.axis_index("seq")
    is_retrieval, window_len, sink_len = look_up(table_ref)
    tokens = recv_ref.shape[0]
    rows = tokens * group_heads
    group_width = group_heads * head_dim
    ctx_dev = k_own.shape[0]
    context = 2 * ctx_dev
    f32, bf16 = jnp.float32, jnp.bfloat16
    def token_pos(index, pair):
        return context + ((index // tok_rows) * 2 + pair) * tok_rows + index % tok_rows

    queries = stack_queries(recv_ref, group_heads, head_dim)
    row_token = lax.broadcasted_iota(jnp.int32, (1, rows), 1) % tokens
    query_pos = token_pos(row_token, pair_at)

    span_k = pl.ds(group_width, head_dim)
    span_v = pl.ds(group_width + head_dim, head_dim)
    cached, spans = [], []
    for k_ref, v_ref, pair in ((k_peer, v_peer, 1 - pair_at), (k_own, v_own, pair_at)):
        for start in range(0, ctx_dev, key_block):
            cached.append((k_ref, v_ref, start, key_block, pair))
    spans.append((recv_ref, pair_at))

    def load_keys(index):
        if index < len(cached):
            k_ref, _, start, size, _ = cached[index]
            return k_ref[start : start + size, :]
        return spans[index - len(cached)][0][:, span_k]

    def load_values(index):
        if index < len(cached):
            _, v_ref, start, size, _ = cached[index]
            return v_ref[start : start + size, :]
        return spans[index - len(cached)][0][:, span_v]

    def place(index):
        if index < len(cached):
            return index * key_block, key_block
        return len(cached) * key_block + (index - len(cached)) * tokens, tokens

    def first_pos(index):
        _, _, start, _, pair = cached[index]
        return pair * ctx_dev + start

    def scores(index, row_at, masked):
        keys = load_keys(index)
        keys = jnp.concatenate([keys, keys], axis=1)
        block = lax.dot_general(
            keys,
            queries[row_at : row_at + row_block],
            (((1,), (1,)), ((), ())),
            preferred_element_type=f32,
        )
        size = block.shape[0]
        pos_q = query_pos[:, row_at : row_at + row_block]
        column = lax.broadcasted_iota(jnp.int32, (size, 1), 0)
        allowed = None
        if index >= len(cached):
            pos_k = token_pos(column, spans[index - len(cached)][1])
            allowed = pos_k <= pos_q
        else:
            pos_k = first_pos(index) + column
        if masked:
            near = (pos_k < sink_len) | (pos_k > pos_q - window_len)
            allowed = near if allowed is None else allowed & near
        if allowed is not None:
            block = jnp.where(allowed, block, NEG_FILL)
        start, _ = place(index)
        score_ref[start : start + size, row_at : row_at + row_block] = block
        return jnp.max(block.reshape(size // 8, 8, row_block), axis=0)

    def weighted(index, row_at, top):
        start, size = place(index)
        block = score_ref[start : start + size, row_at : row_at + row_block]
        weights = jnp.exp2(block - top)
        total = jnp.sum(weights.reshape(size // 8, 8, row_block), axis=0)
        acc = lax.dot_general(
            load_values(index),
            weights.astype(bf16),
            (((0,), (0,)), ((), ())),
            preferred_element_type=f32,
        )
        return total, acc

    blocks = len(cached) + len(spans)
    row_starts = list(range(0, rows, row_block))

    half = len(cached) // 2
    peer_blocks = list(range(half))
    own_blocks = list(range(half, blocks))

    @pl.when(is_retrieval == 1)
    def _():
        running, total, acc = {}, {}, {}

        def first(indices):
            for row_at in row_starts:
                for index in indices:
                    top = scores(index, row_at, False)
                    running[row_at] = jnp.maximum(running[row_at], top) if row_at in running else top

        def second(indices):
            for row_at in row_starts:
                top = jnp.max(running[row_at], axis=0, keepdims=True)
                for index in indices:
                    part_total, part_acc = weighted(index, row_at, top)
                    total[row_at] = total[row_at] + part_total if row_at in total else part_total
                    acc[row_at] = acc[row_at] + part_acc if row_at in acc else part_acc

        first(peer_blocks)
        k_copy.wait()
        v_copy.start()
        first(own_blocks)
        second(peer_blocks)
        v_copy.wait()
        second(own_blocks)
        for row_at in row_starts:
            cols = slice(row_at, row_at + row_block)
            top = jnp.max(running[row_at], axis=0, keepdims=True)
            stat_ref[0:8, cols] = jnp.broadcast_to(top, (8, row_block))
            stat_ref[8:16, cols] = total[row_at]
            acc_ref[:, cols] = acc[row_at]

    @pl.when(is_retrieval != 1)
    def _():
        def needed(index):
            pos = first_pos(index)
            return (pos < sink_len) | (pos + key_block - 1 > context - window_len)

        stat_ref[0:8, :] = jnp.full((8, rows), NEG_FILL, f32)
        stat_ref[8:16, :] = jnp.zeros((8, rows), f32)
        acc_ref[...] = jnp.zeros(acc_ref.shape, f32)

        def first(index):
            for row_at in row_starts:
                cols = slice(row_at, row_at + row_block)
                stat_ref[0:8, cols] = jnp.maximum(stat_ref[0:8, cols], scores(index, row_at, True))

        def second(index):
            for row_at in row_starts:
                cols = slice(row_at, row_at + row_block)
                top = jnp.max(stat_ref[0:8, cols], axis=0, keepdims=True)
                total, acc = weighted(index, row_at, top)
                stat_ref[8:16, cols] += total
                acc_ref[:, cols] += acc

        def each(work, indices):
            for index in indices:
                if index < len(cached):
                    pl.when(needed(index))(functools.partial(work, index))
                else:
                    work(index)

        each(first, peer_blocks)
        k_copy.wait()
        v_copy.start()
        each(first, own_blocks)
        each(second, peer_blocks)
        v_copy.wait()
        each(second, own_blocks)
        top = jnp.max(stat_ref[0:8, :], axis=0, keepdims=True)
        stat_ref[0:8, :] = jnp.broadcast_to(top, (8, rows))


def on_device_pairs(q_span, k_span, v_span, k_cache, v_cache, head_list, retrieval, windows, sinks):
    head_count = lax.axis_size("head")
    tok_rows = q_span.shape[0]
    group_width = q_span.shape[1] // KVH
    head_dim = k_cache.shape[2]
    group_heads = group_width // head_dim
    ctx_dev = k_cache.shape[1]
    tokens = tok_rows * head_count
    rows = tokens * group_heads
    swap = [(0, 1), (1, 0)]
    k_own, v_own = k_cache[0], v_cache[0]
    k_peer = lax.ppermute(k_own, "seq", swap)
    v_peer = lax.ppermute(v_own, "seq", swap)
    joined = jnp.concatenate([q_span, k_span, v_span], axis=1)
    joined, *indices = lax.optimization_barrier((joined, head_list, retrieval, windows, sinks))
    table = jnp.concatenate(indices)
    send = pl.pallas_call(
        functools.partial(pack_kernel, group_width=group_width, head_dim=head_dim),
        out_shape=jax.ShapeDtypeStruct((head_count, tok_rows, group_width + 2 * head_dim), jnp.bfloat16),
        in_specs=[SMEM_SPEC, VMEM_SPEC],
        out_specs=VMEM_SPEC,
        compiler_params=pltpu.CompilerParams(vmem_limit_bytes=2**20),
    )(table, joined)
    recv = lax.all_to_all(send, "head", split_axis=0, concat_axis=0, tiled=True)
    recv = recv.reshape(tokens, group_width + 2 * head_dim)
    peer = lax.ppermute(recv, "seq", swap)
    key_block = math.gcd(ctx_dev, 1024)
    row_block = 256
    keys = 2 * ctx_dev + tokens
    acc, stat = pl.pallas_call(
        functools.partial(
            attend_kernel,
            tok_rows=tok_rows,
            group_heads=group_heads,
            head_dim=head_dim,
            key_block=key_block,
            row_block=row_block,
        ),
        out_shape=(
            jax.ShapeDtypeStruct((head_dim, rows), jnp.float32),
            jax.ShapeDtypeStruct((16, rows), jnp.float32),
        ),
        in_specs=[SMEM_SPEC] + [VMEM_SPEC] * 3 + [HBM_SPEC] * 2,
        out_specs=(VMEM_SPEC, VMEM_SPEC),
        scratch_shapes=[
            pltpu.VMEM((ctx_dev, head_dim), jnp.bfloat16),
            pltpu.VMEM((ctx_dev, head_dim), jnp.bfloat16),
            pltpu.VMEM((keys, rows), jnp.float32),
            pltpu.SemaphoreType.DMA((2,)),
        ],
        compiler_params=pltpu.CompilerParams(vmem_limit_bytes=51 * 2**20),
    )(table, recv, k_peer, v_peer, k_own, v_own)
    result = pl.pallas_call(
        functools.partial(
            span_kernel,
            tok_rows=tok_rows,
            group_heads=group_heads,
            head_dim=head_dim,
            context=2 * ctx_dev,
        ),
        out_shape=jax.ShapeDtypeStruct((tokens, group_width), jnp.bfloat16),
        in_specs=[SMEM_SPEC] + [VMEM_SPEC] * 4,
        out_specs=VMEM_SPEC,
        compiler_params=pltpu.CompilerParams(vmem_limit_bytes=4 * 2**20),
    )(table, recv, peer, acc, stat)
    result = result.reshape(head_count, tok_rows, group_width)
    back = lax.all_to_all(result, "head", split_axis=0, concat_axis=0, tiled=True)
    return pl.pallas_call(
        unpack_kernel,
        out_shape=jax.ShapeDtypeStruct((tok_rows, KVH * group_width), jnp.bfloat16),
        in_specs=[SMEM_SPEC, VMEM_SPEC],
        out_specs=HBM_SPEC,
        scratch_shapes=[pltpu.SemaphoreType.DMA((head_count,))],
        compiler_params=pltpu.CompilerParams(vmem_limit_bytes=2**20),
    )(table, back)


def solution(mesh):
    on_device = on_device_pairs if mesh.shape["head"] == KVH else on_device_quarters
    in_specs = (
        P(("rep", "head", "seq"), None),
        P(("rep", "head", "seq"), None),
        P(("rep", "head", "seq"), None),
        P(("rep", "head"), "seq", None),
        P(("rep", "head"), "seq", None),
        P("rep"),
        P("rep"),
        P("rep"),
        P("rep"),
    )
    out_specs = P(("rep", "head", "seq"), None)
    return jax.shard_map(
        on_device, mesh=mesh, in_specs=in_specs, out_specs=out_specs, check_vma=False
    )
```

```python
import functools
import math

import jax
import jax.numpy as jnp
from jax import lax
from jax.experimental import pallas as pl
from jax.experimental.pallas import tpu as pltpu
from jax.sharding import PartitionSpec as P

KVH = 8


NEG_FILL = -1e30


def absorb(
    running,
    query_rows,
    query_pos,
    key_rows,
    value_rows,
    key_pos,
    is_retrieval,
    window_len,
    sink_len,
    score_scale,
):
    top_score, totals, weighted = running
    scores = jnp.dot(query_rows, key_rows.T, preferred_element_type=jnp.float32) * score_scale
    allowed = (key_pos[None, :] <= query_pos[:, None]) & (
        (is_retrieval == 1)
        | (key_pos[None, :] < sink_len)
        | (key_pos[None, :] > query_pos[:, None] - window_len)
    )
    block_top = jnp.max(jnp.where(allowed, scores, NEG_FILL), axis=1)
    new_top = jnp.maximum(top_score, block_top)
    weights = jnp.where(allowed, jnp.exp(scores - new_top[:, None]), 0.0)
    rescale = jnp.exp(top_score - new_top)
    totals = totals * rescale + jnp.sum(weights, axis=1)
    weighted = weighted * rescale[:, None] + jnp.dot(
        weights.astype(jnp.bfloat16), value_rows, preferred_element_type=jnp.float32
    )
    return (new_top, totals, weighted)


def finish_rows(received, spread, head_list, tok_rows, head_dim):
    top_score, totals, weighted = received
    group_heads = top_score.shape[-1]
    top_score = top_score.reshape(KVH, spread, tok_rows, group_heads)
    totals = totals.reshape(KVH, spread, tok_rows, group_heads)
    weighted = weighted.reshape(KVH, spread, tok_rows, group_heads, head_dim)
    overall = jnp.max(top_score, axis=1, keepdims=True)
    factor = jnp.exp(top_score - overall)
    summed = jnp.sum(totals * factor, axis=1)
    combined = jnp.sum(weighted * factor[..., None], axis=1)
    result = combined / summed[..., None]
    matches = (head_list[:, None] == jnp.arange(KVH, dtype=jnp.int32)[None, :]).astype(jnp.int32)
    inverse = jnp.sum(jnp.arange(KVH, dtype=jnp.int32)[:, None] * matches, axis=0)
    by_group = jnp.take(result, inverse, axis=0)
    return (
        by_group.transpose(1, 0, 2, 3)
        .reshape(tok_rows, KVH * group_heads * head_dim)
        .astype(jnp.bfloat16)
    )


def on_device_quarters(q_span, k_span, v_span, k_cache, v_cache, head_list, retrieval, windows, sinks):
    head_count = lax.axis_size("head")
    pair_count = lax.axis_size("seq")
    quarters = head_count // KVH
    tok_rows = q_span.shape[0]
    group_width = q_span.shape[1] // KVH
    head_dim = k_cache.shape[2]
    group_heads = group_width // head_dim
    ctx_dev = k_cache.shape[1]
    total_q = tok_rows * head_count * pair_count
    context = ctx_dev * pair_count * quarters
    head_at = lax.axis_index("head")
    pair_at = lax.axis_index("seq")
    slot_index = head_at // quarters
    quarter = head_at % quarters
    kv_group = jnp.take(head_list, slot_index)
    q_groups = q_span.reshape(tok_rows, KVH, group_width)
    kv_groups = jnp.concatenate(
        [k_span.reshape(tok_rows, KVH, head_dim), v_span.reshape(tok_rows, KVH, head_dim)], axis=2
    )
    targets = jnp.take(head_list, jnp.arange(head_count * pair_count) // pair_count // quarters)
    q_send = jnp.take(q_groups, targets, axis=1)
    kv_send = jnp.take(kv_groups, targets, axis=1)
    q_recv, kv_recv = (
        lax.all_to_all(q_send, ("head", "seq"), split_axis=1, concat_axis=0, tiled=True),
        lax.all_to_all(kv_send, ("head", "seq"), split_axis=1, concat_axis=0, tiled=True),
    )
    queries = q_recv.reshape(total_q, group_width)
    span_kv = kv_recv.reshape(total_q, 2 * head_dim)
    query_rows = queries.reshape(total_q * group_heads, head_dim)
    query_pos = context + jnp.arange(total_q * group_heads, dtype=jnp.int32) // group_heads
    is_retrieval = jnp.take(retrieval, kv_group)
    window_len = jnp.take(windows, kv_group)
    sink_len = jnp.take(sinks, kv_group)
    score_scale = 1.0 / math.sqrt(head_dim)
    row_total = total_q * group_heads
    running = (
        jnp.full((row_total,), NEG_FILL, jnp.float32),
        jnp.zeros((row_total,), jnp.float32),
        jnp.zeros((row_total, head_dim), jnp.float32),
    )
    key_block = min(512, ctx_dev)
    segment = quarter * pair_count + pair_at
    first_key = segment * ctx_dev
    cache_keys = k_cache[0]
    cache_values = v_cache[0]

    def key_step(step_index, state):
        start = step_index * key_block
        key_rows = lax.dynamic_slice_in_dim(cache_keys, start, key_block, 0)
        value_rows = lax.dynamic_slice_in_dim(cache_values, start, key_block, 0)
        key_pos = first_key + start + jnp.arange(key_block, dtype=jnp.int32)
        return absorb(
            state,
            query_rows,
            query_pos,
            key_rows,
            value_rows,
            key_pos,
            is_retrieval,
            window_len,
            sink_len,
            score_scale,
        )

    running = lax.fori_loop(0, ctx_dev // key_block, key_step, running)
    span_piece = total_q // (quarters * pair_count)
    span_start = segment * span_piece
    span_rows = lax.dynamic_slice_in_dim(span_kv, span_start, span_piece, 0)
    span_pos = context + span_start + jnp.arange(span_piece, dtype=jnp.int32)
    top_score, totals, weighted = absorb(
        running,
        query_rows,
        query_pos,
        span_rows[:, :head_dim],
        span_rows[:, head_dim:],
        span_pos,
        is_retrieval,
        window_len,
        sink_len,
        score_scale,
    )
    received = (
        lax.all_to_all(
            top_score.reshape(head_count * pair_count, tok_rows, group_heads),
            ("head", "seq"),
            split_axis=0,
            concat_axis=0,
            tiled=True,
        ),
        lax.all_to_all(
            totals.reshape(head_count * pair_count, tok_rows, group_heads),
            ("head", "seq"),
            split_axis=0,
            concat_axis=0,
            tiled=True,
        ),
        lax.all_to_all(
            weighted.reshape(head_count * pair_count, tok_rows, group_width),
            ("head", "seq"),
            split_axis=0,
            concat_axis=0,
            tiled=True,
        ),
    )
    spread = quarters * pair_count
    return finish_rows(received, spread, head_list, tok_rows, head_dim)


VMEM_SPEC = pl.BlockSpec(memory_space=pltpu.VMEM)
HBM_SPEC = pl.BlockSpec(memory_space=pltpu.HBM)
SMEM_SPEC = pl.BlockSpec(memory_space=pltpu.SMEM)


def pack_kernel(head_ref, in_ref, out_ref, *, group_width, head_dim):
    q_width = KVH * group_width
    q_ref = in_ref.at[:, :q_width]
    k_ref = in_ref.at[:, q_width : q_width + KVH * head_dim]
    v_ref = in_ref.at[:, q_width + KVH * head_dim :]
    for slot in range(out_ref.shape[0]):
        group = head_ref[slot]
        q_start = pl.multiple_of(group * group_width, 128)
        kv_start = pl.multiple_of(group * head_dim, 128)
        out_ref[slot, :, :group_width] = q_ref[:, pl.ds(q_start, group_width)]
        out_ref[slot, :, group_width : group_width + head_dim] = k_ref[:, pl.ds(kv_start, head_dim)]
        out_ref[slot, :, group_width + head_dim :] = v_ref[:, pl.ds(kv_start, head_dim)]


def unpack_kernel(head_ref, in_ref, out_ref, sems):
    width = in_ref.shape[2]
    copies = []
    for slot in range(in_ref.shape[0]):
        start = pl.multiple_of(head_ref[slot] * width, 128)
        copies.append(
            pltpu.make_async_copy(in_ref.at[slot], out_ref.at[:, pl.ds(start, width)], sems.at[slot])
        )
    for copy in copies:
        copy.start()
    for copy in copies:
        copy.wait()


def look_up(table_ref):
    kv_group = table_ref[lax.axis_index("head")]
    return (table_ref[part * KVH + kv_group] for part in (1, 2, 3))


def stack_queries(recv_ref, group_heads, head_dim):
    scale = math.log2(math.e) / math.sqrt(head_dim)
    queries = jnp.concatenate(
        [recv_ref[:, k * head_dim : (k + 1) * head_dim] for k in range(group_heads)], axis=0
    )
    scaled = queries.astype(jnp.float32) * scale
    high = scaled.astype(jnp.bfloat16)
    low = (scaled - high.astype(jnp.float32)).astype(jnp.bfloat16)
    return jnp.concatenate([high, low], axis=1)


def span_kernel(
    table_ref,
    recv_ref,
    peer_ref,
    acc_ref,
    stat_ref,
    out_ref,
    *,
    tok_rows,
    group_heads,
    head_dim,
    context,
):
    f32, bf16 = jnp.float32, jnp.bfloat16
    pair_at = lax.axis_index("seq")
    is_retrieval, window_len, sink_len = look_up(table_ref)
    window_len = jnp.where(is_retrieval == 1, 2**30, window_len)
    tokens = recv_ref.shape[0]
    rows = tokens * group_heads
    group_width = group_heads * head_dim
    queries = stack_queries(recv_ref, group_heads, head_dim)

    def token_pos(index, pair):
        return context + ((index // tok_rows) * 2 + pair) * tok_rows + index % tok_rows

    query_pos = token_pos(lax.broadcasted_iota(jnp.int32, (1, rows), 1) % tokens, pair_at)
    key_pos = token_pos(lax.broadcasted_iota(jnp.int32, (tokens, 1), 0), 1 - pair_at)
    keys = peer_ref[:, group_width : group_width + head_dim]
    values = peer_ref[:, group_width + head_dim : group_width + 2 * head_dim]
    block = lax.dot_general(
        jnp.concatenate([keys, keys], axis=1),
        queries,
        (((1,), (1,)), ((), ())),
        preferred_element_type=f32,
    )
    allowed = (key_pos <= query_pos) & ((key_pos < sink_len) | (key_pos > query_pos - window_len))
    block = jnp.where(allowed, block, NEG_FILL)
    old_top = stat_ref[0:1, :]
    top = jnp.maximum(old_top, jnp.max(block, axis=0, keepdims=True))
    factor = jnp.exp2(old_top - top)
    weights = jnp.exp2(block - top)
    total = jnp.sum(stat_ref[8:16, :], axis=0, keepdims=True) * factor
    total = total + jnp.sum(weights, axis=0, keepdims=True)
    acc = acc_ref[...] * factor + lax.dot_general(
        values, weights.astype(bf16), (((0,), (0,)), ((), ())), preferred_element_type=f32
    )
    result = (acc / total).T.astype(bf16)
    for head in range(group_heads):
        out_ref[:, head * head_dim : (head + 1) * head_dim] = result[head * tokens : (head + 1) * tokens]


def attend_kernel(
    table_ref,
    recv_ref,
    k_peer,
    v_peer,
    k_source,
    v_source,
    acc_ref,
    stat_ref,
    k_own,
    v_own,
    score_ref,
    own_sem,
    *,
    tok_rows,
    group_heads,
    head_dim,
    key_block,
    row_block,
):

    def own_copies(source, target, which):
        size = source.shape[0] // own_sem.shape[1]
        return [
            pltpu.make_async_copy(
                source.at[pl.ds(chunk * size, size)],
                target.at[pl.ds(chunk * size, size)],
                own_sem.at[which, chunk],
            )
            for chunk in range(own_sem.shape[1])
        ]

    k_copies = own_copies(k_source, k_own, 0)
    v_copies = own_copies(v_source, v_own, 1)
    for copy in k_copies:
        copy.start()

    def end_k_start_v():
        for copy in k_copies:
            copy.wait()
        for copy in v_copies:
            copy.start()

    def end_v():
        for copy in v_copies:
            copy.wait()

    pair_at = lax.axis_index("seq")
    is_retrieval, window_len, sink_len = look_up(table_ref)
    tokens = recv_ref.shape[0]
    rows = tokens * group_heads
    group_width = group_heads * head_dim
    ctx_dev = k_own.shape[0]
    context = 2 * ctx_dev
    f32, bf16 = jnp.float32, jnp.bfloat16
    def token_pos(index, pair):
        return context + ((index // tok_rows) * 2 + pair) * tok_rows + index % tok_rows

    queries = stack_queries(recv_ref, group_heads, head_dim)
    row_token = lax.broadcasted_iota(jnp.int32, (1, rows), 1) % tokens
    query_pos = token_pos(row_token, pair_at)

    span_k = pl.ds(group_width, head_dim)
    span_v = pl.ds(group_width + head_dim, head_dim)
    cached, spans = [], []
    for k_ref, v_ref, pair in ((k_peer, v_peer, 1 - pair_at), (k_own, v_own, pair_at)):
        for start in range(0, ctx_dev, key_block):
            cached.append((k_ref, v_ref, start, key_block, pair))
    spans.append((recv_ref, pair_at))

    def load_keys(index):
        if index < len(cached):
            k_ref, _, start, size, _ = cached[index]
            return k_ref[start : start + size, :]
        return spans[index - len(cached)][0][:, span_k]

    def load_values(index):
        if index < len(cached):
            _, v_ref, start, size, _ = cached[index]
            return v_ref[start : start + size, :]
        return spans[index - len(cached)][0][:, span_v]

    def place(index):
        if index < len(cached):
            return index * key_block, key_block
        return len(cached) * key_block + (index - len(cached)) * tokens, tokens

    def first_pos(index):
        _, _, start, _, pair = cached[index]
        return pair * ctx_dev + start

    def scores(index, row_at, masked):
        keys = load_keys(index)
        keys = jnp.concatenate([keys, keys], axis=1)
        block = lax.dot_general(
            keys,
            queries[row_at : row_at + row_block],
            (((1,), (1,)), ((), ())),
            preferred_element_type=f32,
        )
        size = block.shape[0]
        pos_q = query_pos[:, row_at : row_at + row_block]
        column = lax.broadcasted_iota(jnp.int32, (size, 1), 0)
        allowed = None
        if index >= len(cached):
            pos_k = token_pos(column, spans[index - len(cached)][1])
            allowed = pos_k <= pos_q
        else:
            pos_k = first_pos(index) + column
        if masked:
            near = (pos_k < sink_len) | (pos_k > pos_q - window_len)
            allowed = near if allowed is None else allowed & near
        if allowed is not None:
            block = jnp.where(allowed, block, NEG_FILL)
        start, _ = place(index)
        score_ref[start : start + size, row_at : row_at + row_block] = block
        return jnp.max(block.reshape(size // 8, 8, row_block), axis=0)

    def weighted(index, row_at, top):
        start, size = place(index)
        block = score_ref[start : start + size, row_at : row_at + row_block]
        weights = jnp.exp2(block - top)
        total = jnp.sum(weights.reshape(size // 8, 8, row_block), axis=0)
        acc = lax.dot_general(
            load_values(index),
            weights.astype(bf16),
            (((0,), (0,)), ((), ())),
            preferred_element_type=f32,
        )
        return total, acc

    blocks = len(cached) + len(spans)
    row_starts = list(range(0, rows, row_block))

    half = len(cached) // 2
    peer_blocks = list(range(half))
    own_blocks = list(range(half, blocks))

    @pl.when(is_retrieval == 1)
    def _():
        running, total, acc = {}, {}, {}

        def first(indices):
            for row_at in row_starts:
                for index in indices:
                    top = scores(index, row_at, False)
                    running[row_at] = jnp.maximum(running[row_at], top) if row_at in running else top

        def second(indices):
            for row_at in row_starts:
                top = jnp.max(running[row_at], axis=0, keepdims=True)
                for index in indices:
                    part_total, part_acc = weighted(index, row_at, top)
                    total[row_at] = total[row_at] + part_total if row_at in total else part_total
                    acc[row_at] = acc[row_at] + part_acc if row_at in acc else part_acc

        first(peer_blocks)
        end_k_start_v()
        first(own_blocks)
        second(peer_blocks)
        end_v()
        second(own_blocks)
        for row_at in row_starts:
            cols = slice(row_at, row_at + row_block)
            top = jnp.max(running[row_at], axis=0, keepdims=True)
            stat_ref[0:8, cols] = jnp.broadcast_to(top, (8, row_block))
            stat_ref[8:16, cols] = total[row_at]
            acc_ref[:, cols] = acc[row_at]

    @pl.when(is_retrieval != 1)
    def _():
        def needed(index):
            pos = first_pos(index)
            return (pos < sink_len) | (pos + key_block - 1 > context - window_len)

        stat_ref[0:8, :] = jnp.full((8, rows), NEG_FILL, f32)
        stat_ref[8:16, :] = jnp.zeros((8, rows), f32)
        acc_ref[...] = jnp.zeros(acc_ref.shape, f32)

        def first(index):
            for row_at in row_starts:
                cols = slice(row_at, row_at + row_block)
                stat_ref[0:8, cols] = jnp.maximum(stat_ref[0:8, cols], scores(index, row_at, True))

        def second(index):
            for row_at in row_starts:
                cols = slice(row_at, row_at + row_block)
                top = jnp.max(stat_ref[0:8, cols], axis=0, keepdims=True)
                total, acc = weighted(index, row_at, top)
                stat_ref[8:16, cols] += total
                acc_ref[:, cols] += acc

        def each(work, indices):
            for index in indices:
                if index < len(cached):
                    pl.when(needed(index))(functools.partial(work, index))
                else:
                    work(index)

        each(first, peer_blocks)
        end_k_start_v()
        each(first, own_blocks)
        each(second, peer_blocks)
        end_v()
        each(second, own_blocks)
        top = jnp.max(stat_ref[0:8, :], axis=0, keepdims=True)
        stat_ref[0:8, :] = jnp.broadcast_to(top, (8, rows))


def on_device_pairs(q_span, k_span, v_span, k_cache, v_cache, head_list, retrieval, windows, sinks):
    head_count = lax.axis_size("head")
    tok_rows = q_span.shape[0]
    group_width = q_span.shape[1] // KVH
    head_dim = k_cache.shape[2]
    group_heads = group_width // head_dim
    ctx_dev = k_cache.shape[1]
    tokens = tok_rows * head_count
    rows = tokens * group_heads
    swap = [(0, 1), (1, 0)]
    k_own, v_own = k_cache[0], v_cache[0]
    k_peer = lax.ppermute(k_own, "seq", swap)
    v_peer = lax.ppermute(v_own, "seq", swap)
    joined = jnp.concatenate([q_span, k_span, v_span], axis=1)
    joined, *indices = lax.optimization_barrier((joined, head_list, retrieval, windows, sinks))
    table = jnp.concatenate(indices)
    send = pl.pallas_call(
        functools.partial(pack_kernel, group_width=group_width, head_dim=head_dim),
        out_shape=jax.ShapeDtypeStruct((head_count, tok_rows, group_width + 2 * head_dim), jnp.bfloat16),
        in_specs=[SMEM_SPEC, VMEM_SPEC],
        out_specs=VMEM_SPEC,
        compiler_params=pltpu.CompilerParams(vmem_limit_bytes=2**20),
    )(table, joined)
    recv = lax.all_to_all(send, "head", split_axis=0, concat_axis=0, tiled=True)
    recv = recv.reshape(tokens, group_width + 2 * head_dim)
    peer = lax.ppermute(recv, "seq", swap)
    key_block = math.gcd(ctx_dev, 1024)
    row_block = 256
    keys = 2 * ctx_dev + tokens
    acc, stat = pl.pallas_call(
        functools.partial(
            attend_kernel,
            tok_rows=tok_rows,
            group_heads=group_heads,
            head_dim=head_dim,
            key_block=key_block,
            row_block=row_block,
        ),
        out_shape=(
            jax.ShapeDtypeStruct((head_dim, rows), jnp.float32),
            jax.ShapeDtypeStruct((16, rows), jnp.float32),
        ),
        in_specs=[SMEM_SPEC] + [VMEM_SPEC] * 3 + [HBM_SPEC] * 2,
        out_specs=(VMEM_SPEC, VMEM_SPEC),
        scratch_shapes=[
            pltpu.VMEM((ctx_dev, head_dim), jnp.bfloat16),
            pltpu.VMEM((ctx_dev, head_dim), jnp.bfloat16),
            pltpu.VMEM((keys, rows), jnp.float32),
            pltpu.SemaphoreType.DMA((2, 4)),
        ],
        compiler_params=pltpu.CompilerParams(vmem_limit_bytes=51 * 2**20),
    )(table, recv, k_peer, v_peer, k_own, v_own)
    result = pl.pallas_call(
        functools.partial(
            span_kernel,
            tok_rows=tok_rows,
            group_heads=group_heads,
            head_dim=head_dim,
            context=2 * ctx_dev,
        ),
        out_shape=jax.ShapeDtypeStruct((tokens, group_width), jnp.bfloat16),
        in_specs=[SMEM_SPEC] + [VMEM_SPEC] * 4,
        out_specs=VMEM_SPEC,
        compiler_params=pltpu.CompilerParams(vmem_limit_bytes=4 * 2**20),
    )(table, recv, peer, acc, stat)
    result = result.reshape(head_count, tok_rows, group_width)
    back = lax.all_to_all(result, "head", split_axis=0, concat_axis=0, tiled=True)
    return pl.pallas_call(
        unpack_kernel,
        out_shape=jax.ShapeDtypeStruct((tok_rows, KVH * group_width), jnp.bfloat16),
        in_specs=[SMEM_SPEC, VMEM_SPEC],
        out_specs=HBM_SPEC,
        scratch_shapes=[pltpu.SemaphoreType.DMA((head_count,))],
        compiler_params=pltpu.CompilerParams(vmem_limit_bytes=2**20),
    )(table, back)


def solution(mesh):
    on_device = on_device_pairs if mesh.shape["head"] == KVH else on_device_quarters
    in_specs = (
        P(("rep", "head", "seq"), None),
        P(("rep", "head", "seq"), None),
        P(("rep", "head", "seq"), None),
        P(("rep", "head"), "seq", None),
        P(("rep", "head"), "seq", None),
        P("rep"),
        P("rep"),
        P("rep"),
        P("rep"),
    )
    out_specs = P(("rep", "head", "seq"), None)
    return jax.shard_map(
        on_device, mesh=mesh, in_specs=in_specs, out_specs=out_specs, check_vma=False
    )
```

```python
import functools
import math

import jax
import jax.numpy as jnp
from jax import lax
from jax.experimental import pallas as pl
from jax.experimental.pallas import tpu as pltpu
from jax.sharding import PartitionSpec as P

KVH = 8


NEG_FILL = -1e30


def absorb(
    running,
    query_rows,
    query_pos,
    key_rows,
    value_rows,
    key_pos,
    is_retrieval,
    window_len,
    sink_len,
    score_scale,
):
    top_score, totals, weighted = running
    scores = jnp.dot(query_rows, key_rows.T, preferred_element_type=jnp.float32) * score_scale
    allowed = (key_pos[None, :] <= query_pos[:, None]) & (
        (is_retrieval == 1)
        | (key_pos[None, :] < sink_len)
        | (key_pos[None, :] > query_pos[:, None] - window_len)
    )
    block_top = jnp.max(jnp.where(allowed, scores, NEG_FILL), axis=1)
    new_top = jnp.maximum(top_score, block_top)
    weights = jnp.where(allowed, jnp.exp(scores - new_top[:, None]), 0.0)
    rescale = jnp.exp(top_score - new_top)
    totals = totals * rescale + jnp.sum(weights, axis=1)
    weighted = weighted * rescale[:, None] + jnp.dot(
        weights.astype(jnp.bfloat16), value_rows, preferred_element_type=jnp.float32
    )
    return (new_top, totals, weighted)


def finish_rows(received, spread, head_list, tok_rows, head_dim):
    top_score, totals, weighted = received
    group_heads = top_score.shape[-1]
    top_score = top_score.reshape(KVH, spread, tok_rows, group_heads)
    totals = totals.reshape(KVH, spread, tok_rows, group_heads)
    weighted = weighted.reshape(KVH, spread, tok_rows, group_heads, head_dim)
    overall = jnp.max(top_score, axis=1, keepdims=True)
    factor = jnp.exp(top_score - overall)
    summed = jnp.sum(totals * factor, axis=1)
    combined = jnp.sum(weighted * factor[..., None], axis=1)
    result = combined / summed[..., None]
    matches = (head_list[:, None] == jnp.arange(KVH, dtype=jnp.int32)[None, :]).astype(jnp.int32)
    inverse = jnp.sum(jnp.arange(KVH, dtype=jnp.int32)[:, None] * matches, axis=0)
    by_group = jnp.take(result, inverse, axis=0)
    return (
        by_group.transpose(1, 0, 2, 3)
        .reshape(tok_rows, KVH * group_heads * head_dim)
        .astype(jnp.bfloat16)
    )


def on_device_quarters(q_span, k_span, v_span, k_cache, v_cache, head_list, retrieval, windows, sinks):
    head_count = lax.axis_size("head")
    pair_count = lax.axis_size("seq")
    quarters = head_count // KVH
    tok_rows = q_span.shape[0]
    group_width = q_span.shape[1] // KVH
    head_dim = k_cache.shape[2]
    group_heads = group_width // head_dim
    ctx_dev = k_cache.shape[1]
    total_q = tok_rows * head_count * pair_count
    context = ctx_dev * pair_count * quarters
    head_at = lax.axis_index("head")
    pair_at = lax.axis_index("seq")
    slot_index = head_at // quarters
    quarter = head_at % quarters
    kv_group = jnp.take(head_list, slot_index)
    q_groups = q_span.reshape(tok_rows, KVH, group_width)
    kv_groups = jnp.concatenate(
        [k_span.reshape(tok_rows, KVH, head_dim), v_span.reshape(tok_rows, KVH, head_dim)], axis=2
    )
    targets = jnp.take(head_list, jnp.arange(head_count * pair_count) // pair_count // quarters)
    q_send = jnp.take(q_groups, targets, axis=1)
    kv_send = jnp.take(kv_groups, targets, axis=1)
    q_recv, kv_recv = (
        lax.all_to_all(q_send, ("head", "seq"), split_axis=1, concat_axis=0, tiled=True),
        lax.all_to_all(kv_send, ("head", "seq"), split_axis=1, concat_axis=0, tiled=True),
    )
    queries = q_recv.reshape(total_q, group_width)
    span_kv = kv_recv.reshape(total_q, 2 * head_dim)
    query_rows = queries.reshape(total_q * group_heads, head_dim)
    query_pos = context + jnp.arange(total_q * group_heads, dtype=jnp.int32) // group_heads
    is_retrieval = jnp.take(retrieval, kv_group)
    window_len = jnp.take(windows, kv_group)
    sink_len = jnp.take(sinks, kv_group)
    score_scale = 1.0 / math.sqrt(head_dim)
    row_total = total_q * group_heads
    running = (
        jnp.full((row_total,), NEG_FILL, jnp.float32),
        jnp.zeros((row_total,), jnp.float32),
        jnp.zeros((row_total, head_dim), jnp.float32),
    )
    key_block = min(512, ctx_dev)
    segment = quarter * pair_count + pair_at
    first_key = segment * ctx_dev
    cache_keys = k_cache[0]
    cache_values = v_cache[0]

    def key_step(step_index, state):
        start = step_index * key_block
        key_rows = lax.dynamic_slice_in_dim(cache_keys, start, key_block, 0)
        value_rows = lax.dynamic_slice_in_dim(cache_values, start, key_block, 0)
        key_pos = first_key + start + jnp.arange(key_block, dtype=jnp.int32)
        return absorb(
            state,
            query_rows,
            query_pos,
            key_rows,
            value_rows,
            key_pos,
            is_retrieval,
            window_len,
            sink_len,
            score_scale,
        )

    running = lax.fori_loop(0, ctx_dev // key_block, key_step, running)
    span_piece = total_q // (quarters * pair_count)
    span_start = segment * span_piece
    span_rows = lax.dynamic_slice_in_dim(span_kv, span_start, span_piece, 0)
    span_pos = context + span_start + jnp.arange(span_piece, dtype=jnp.int32)
    top_score, totals, weighted = absorb(
        running,
        query_rows,
        query_pos,
        span_rows[:, :head_dim],
        span_rows[:, head_dim:],
        span_pos,
        is_retrieval,
        window_len,
        sink_len,
        score_scale,
    )
    received = (
        lax.all_to_all(
            top_score.reshape(head_count * pair_count, tok_rows, group_heads),
            ("head", "seq"),
            split_axis=0,
            concat_axis=0,
            tiled=True,
        ),
        lax.all_to_all(
            totals.reshape(head_count * pair_count, tok_rows, group_heads),
            ("head", "seq"),
            split_axis=0,
            concat_axis=0,
            tiled=True,
        ),
        lax.all_to_all(
            weighted.reshape(head_count * pair_count, tok_rows, group_width),
            ("head", "seq"),
            split_axis=0,
            concat_axis=0,
            tiled=True,
        ),
    )
    spread = quarters * pair_count
    return finish_rows(received, spread, head_list, tok_rows, head_dim)


VMEM_SPEC = pl.BlockSpec(memory_space=pltpu.VMEM)
HBM_SPEC = pl.BlockSpec(memory_space=pltpu.HBM)
SMEM_SPEC = pl.BlockSpec(memory_space=pltpu.SMEM)


def pack_kernel(head_ref, in_ref, out_ref, *, group_width, head_dim):
    q_width = KVH * group_width
    q_ref = in_ref.at[:, :q_width]
    k_ref = in_ref.at[:, q_width : q_width + KVH * head_dim]
    v_ref = in_ref.at[:, q_width + KVH * head_dim :]
    for slot in range(out_ref.shape[0]):
        group = head_ref[slot]
        q_start = pl.multiple_of(group * group_width, 128)
        kv_start = pl.multiple_of(group * head_dim, 128)
        out_ref[slot, :, :group_width] = q_ref[:, pl.ds(q_start, group_width)]
        out_ref[slot, :, group_width : group_width + head_dim] = k_ref[:, pl.ds(kv_start, head_dim)]
        out_ref[slot, :, group_width + head_dim :] = v_ref[:, pl.ds(kv_start, head_dim)]


def unpack_kernel(head_ref, in_ref, out_ref, sems):
    width = in_ref.shape[2]
    copies = []
    for slot in range(in_ref.shape[0]):
        start = pl.multiple_of(head_ref[slot] * width, 128)
        copies.append(
            pltpu.make_async_copy(in_ref.at[slot], out_ref.at[:, pl.ds(start, width)], sems.at[slot])
        )
    for copy in copies:
        copy.start()
    for copy in copies:
        copy.wait()


def look_up(table_ref):
    kv_group = table_ref[lax.axis_index("head")]
    return (table_ref[part * KVH + kv_group] for part in (1, 2, 3))


def stack_queries(recv_ref, group_heads, head_dim):
    scale = math.log2(math.e) / math.sqrt(head_dim)
    queries = jnp.concatenate(
        [recv_ref[:, k * head_dim : (k + 1) * head_dim] for k in range(group_heads)], axis=0
    )
    scaled = queries.astype(jnp.float32) * scale
    high = scaled.astype(jnp.bfloat16)
    low = (scaled - high.astype(jnp.float32)).astype(jnp.bfloat16)
    return jnp.concatenate([high, low], axis=1)


def span_kernel(
    table_ref,
    recv_ref,
    peer_ref,
    acc_ref,
    stat_ref,
    out_ref,
    *,
    tok_rows,
    group_heads,
    head_dim,
    context,
):
    f32, bf16 = jnp.float32, jnp.bfloat16
    pair_at = lax.axis_index("seq")
    is_retrieval, window_len, sink_len = look_up(table_ref)
    window_len = jnp.where(is_retrieval == 1, 2**30, window_len)
    tokens = recv_ref.shape[0]
    rows = tokens * group_heads
    group_width = group_heads * head_dim
    queries = stack_queries(recv_ref, group_heads, head_dim)

    def token_pos(index, pair):
        return context + ((index // tok_rows) * 2 + pair) * tok_rows + index % tok_rows

    query_pos = token_pos(lax.broadcasted_iota(jnp.int32, (1, rows), 1) % tokens, pair_at)
    key_pos = token_pos(lax.broadcasted_iota(jnp.int32, (tokens, 1), 0), 1 - pair_at)
    keys = peer_ref[:, group_width : group_width + head_dim]
    values = peer_ref[:, group_width + head_dim : group_width + 2 * head_dim]
    block = lax.dot_general(
        jnp.concatenate([keys, keys], axis=1),
        queries,
        (((1,), (1,)), ((), ())),
        preferred_element_type=f32,
    )
    allowed = (key_pos <= query_pos) & ((key_pos < sink_len) | (key_pos > query_pos - window_len))
    block = jnp.where(allowed, block, NEG_FILL)
    old_top = stat_ref[0:1, :]
    top = jnp.maximum(old_top, jnp.max(block, axis=0, keepdims=True))
    factor = jnp.exp2(old_top - top)
    weights = jnp.exp2(block - top)
    total = jnp.sum(stat_ref[8:16, :], axis=0, keepdims=True) * factor
    total = total + jnp.sum(weights, axis=0, keepdims=True)
    acc = acc_ref[...] * factor + lax.dot_general(
        values, weights.astype(bf16), (((0,), (0,)), ((), ())), preferred_element_type=f32
    )
    result = (acc / total).T.astype(bf16)
    for head in range(group_heads):
        out_ref[:, head * head_dim : (head + 1) * head_dim] = result[head * tokens : (head + 1) * tokens]


def attend_kernel(
    table_ref,
    recv_ref,
    k_peer,
    v_peer,
    k_source,
    v_source,
    acc_ref,
    stat_ref,
    k_own,
    v_own,
    score_ref,
    own_sem,
    *,
    tok_rows,
    group_heads,
    head_dim,
    key_block,
    row_block,
):

    def own_copies(source, target, which):
        size = source.shape[0] // own_sem.shape[1]
        return [
            pltpu.make_async_copy(
                source.at[pl.ds(chunk * size, size)],
                target.at[pl.ds(chunk * size, size)],
                own_sem.at[which, chunk],
            )
            for chunk in range(own_sem.shape[1])
        ]

    k_copies = own_copies(k_source, k_own, 0)
    v_copies = own_copies(v_source, v_own, 1)
    for copy in k_copies:
        copy.start()

    def end_k_start_v():
        for copy in k_copies:
            copy.wait()
        for copy in v_copies:
            copy.start()

    def end_v():
        for copy in v_copies:
            copy.wait()

    pair_at = lax.axis_index("seq")
    is_retrieval, window_len, sink_len = look_up(table_ref)
    tokens = recv_ref.shape[0]
    rows = tokens * group_heads
    group_width = group_heads * head_dim
    ctx_dev = k_own.shape[0]
    context = 2 * ctx_dev
    f32, bf16 = jnp.float32, jnp.bfloat16
    def token_pos(index, pair):
        return context + ((index // tok_rows) * 2 + pair) * tok_rows + index % tok_rows

    queries = stack_queries(recv_ref, group_heads, head_dim)
    row_token = lax.broadcasted_iota(jnp.int32, (1, rows), 1) % tokens
    query_pos = token_pos(row_token, pair_at)

    span_k = pl.ds(group_width, head_dim)
    span_v = pl.ds(group_width + head_dim, head_dim)

    def build(key_block):
        cached, spans = [], []
        for k_ref, v_ref, pair in ((k_peer, v_peer, 1 - pair_at), (k_own, v_own, pair_at)):
            for start in range(0, ctx_dev, key_block):
                cached.append((k_ref, v_ref, start, key_block, pair))
        spans.append((recv_ref, pair_at))

        def load_keys(index):
            if index < len(cached):
                k_ref, _, start, size, _ = cached[index]
                return k_ref[start : start + size, :]
            return spans[index - len(cached)][0][:, span_k]

        def load_values(index):
            if index < len(cached):
                _, v_ref, start, size, _ = cached[index]
                return v_ref[start : start + size, :]
            return spans[index - len(cached)][0][:, span_v]

        def place(index):
            if index < len(cached):
                return index * key_block, key_block
            return len(cached) * key_block + (index - len(cached)) * tokens, tokens

        def first_pos(index):
            _, _, start, _, pair = cached[index]
            return pair * ctx_dev + start

        def scores(index, row_at, masked):
            keys = load_keys(index)
            keys = jnp.concatenate([keys, keys], axis=1)
            block = lax.dot_general(
                keys,
                queries[row_at : row_at + row_block],
                (((1,), (1,)), ((), ())),
                preferred_element_type=f32,
            )
            size = block.shape[0]
            pos_q = query_pos[:, row_at : row_at + row_block]
            column = lax.broadcasted_iota(jnp.int32, (size, 1), 0)
            allowed = None
            if index >= len(cached):
                pos_k = token_pos(column, spans[index - len(cached)][1])
                allowed = pos_k <= pos_q
            else:
                pos_k = first_pos(index) + column
            if masked:
                near = (pos_k < sink_len) | (pos_k > pos_q - window_len)
                allowed = near if allowed is None else allowed & near
            if allowed is not None:
                block = jnp.where(allowed, block, NEG_FILL)
            start, _ = place(index)
            score_ref[start : start + size, row_at : row_at + row_block] = block
            return jnp.max(block.reshape(size // 8, 8, row_block), axis=0)

        def weighted(index, row_at, top):
            start, size = place(index)
            block = score_ref[start : start + size, row_at : row_at + row_block]
            weights = jnp.exp2(block - top)
            total = jnp.sum(weights.reshape(size // 8, 8, row_block), axis=0)
            acc = lax.dot_general(
                load_values(index),
                weights.astype(bf16),
                (((0,), (0,)), ((), ())),
                preferred_element_type=f32,
            )
            return total, acc

        return len(cached), len(spans), first_pos, scores, weighted

    row_starts = list(range(0, rows, row_block))

    @pl.when(is_retrieval == 1)
    def _():
        cached, spans, _, scores, weighted = build(ctx_dev)
        peer_blocks = list(range(cached // 2))
        own_blocks = list(range(cached // 2, cached + spans))
        running, total, acc = {}, {}, {}

        def first(indices):
            for row_at in row_starts:
                for index in indices:
                    top = scores(index, row_at, False)
                    running[row_at] = jnp.maximum(running[row_at], top) if row_at in running else top

        def second(indices):
            for row_at in row_starts:
                top = jnp.max(running[row_at], axis=0, keepdims=True)
                for index in indices:
                    part_total, part_acc = weighted(index, row_at, top)
                    total[row_at] = total[row_at] + part_total if row_at in total else part_total
                    acc[row_at] = acc[row_at] + part_acc if row_at in acc else part_acc

        first(peer_blocks)
        end_k_start_v()
        first(own_blocks)
        second(peer_blocks)
        end_v()
        second(own_blocks)
        for row_at in row_starts:
            cols = slice(row_at, row_at + row_block)
            top = jnp.max(running[row_at], axis=0, keepdims=True)
            stat_ref[0:8, cols] = jnp.broadcast_to(top, (8, row_block))
            stat_ref[8:16, cols] = total[row_at]
            acc_ref[:, cols] = acc[row_at]

    @pl.when(is_retrieval != 1)
    def _():
        cached, spans, first_pos, scores, weighted = build(key_block)
        peer_blocks = list(range(cached // 2))
        own_blocks = list(range(cached // 2, cached + spans))

        def needed(index):
            pos = first_pos(index)
            return (pos < sink_len) | (pos + key_block - 1 > context - window_len)

        stat_ref[0:8, :] = jnp.full((8, rows), NEG_FILL, f32)
        stat_ref[8:16, :] = jnp.zeros((8, rows), f32)
        acc_ref[...] = jnp.zeros(acc_ref.shape, f32)

        def first(index):
            for row_at in row_starts:
                cols = slice(row_at, row_at + row_block)
                stat_ref[0:8, cols] = jnp.maximum(stat_ref[0:8, cols], scores(index, row_at, True))

        def second(index):
            for row_at in row_starts:
                cols = slice(row_at, row_at + row_block)
                top = jnp.max(stat_ref[0:8, cols], axis=0, keepdims=True)
                total, acc = weighted(index, row_at, top)
                stat_ref[8:16, cols] += total
                acc_ref[:, cols] += acc

        def each(work, indices):
            for index in indices:
                if index < cached:
                    pl.when(needed(index))(functools.partial(work, index))
                else:
                    work(index)

        each(first, peer_blocks)
        end_k_start_v()
        each(first, own_blocks)
        each(second, peer_blocks)
        end_v()
        each(second, own_blocks)
        top = jnp.max(stat_ref[0:8, :], axis=0, keepdims=True)
        stat_ref[0:8, :] = jnp.broadcast_to(top, (8, rows))


def on_device_pairs(q_span, k_span, v_span, k_cache, v_cache, head_list, retrieval, windows, sinks):
    head_count = lax.axis_size("head")
    tok_rows = q_span.shape[0]
    group_width = q_span.shape[1] // KVH
    head_dim = k_cache.shape[2]
    group_heads = group_width // head_dim
    ctx_dev = k_cache.shape[1]
    tokens = tok_rows * head_count
    rows = tokens * group_heads
    swap = [(0, 1), (1, 0)]
    k_own, v_own = k_cache[0], v_cache[0]
    k_peer = lax.ppermute(k_own, "seq", swap)
    v_peer = lax.ppermute(v_own, "seq", swap)
    joined = jnp.concatenate([q_span, k_span, v_span], axis=1)
    joined, *indices = lax.optimization_barrier((joined, head_list, retrieval, windows, sinks))
    table = jnp.concatenate(indices)
    send = pl.pallas_call(
        functools.partial(pack_kernel, group_width=group_width, head_dim=head_dim),
        out_shape=jax.ShapeDtypeStruct((head_count, tok_rows, group_width + 2 * head_dim), jnp.bfloat16),
        in_specs=[SMEM_SPEC, VMEM_SPEC],
        out_specs=VMEM_SPEC,
        compiler_params=pltpu.CompilerParams(vmem_limit_bytes=2**20),
    )(table, joined)
    recv = lax.all_to_all(send, "head", split_axis=0, concat_axis=0, tiled=True)
    recv = recv.reshape(tokens, group_width + 2 * head_dim)
    peer = lax.ppermute(recv, "seq", swap)
    key_block = math.gcd(ctx_dev, 1024)
    row_block = 256
    keys = 2 * ctx_dev + tokens
    acc, stat = pl.pallas_call(
        functools.partial(
            attend_kernel,
            tok_rows=tok_rows,
            group_heads=group_heads,
            head_dim=head_dim,
            key_block=key_block,
            row_block=row_block,
        ),
        out_shape=(
            jax.ShapeDtypeStruct((head_dim, rows), jnp.float32),
            jax.ShapeDtypeStruct((16, rows), jnp.float32),
        ),
        in_specs=[SMEM_SPEC] + [VMEM_SPEC] * 3 + [HBM_SPEC] * 2,
        out_specs=(VMEM_SPEC, VMEM_SPEC),
        scratch_shapes=[
            pltpu.VMEM((ctx_dev, head_dim), jnp.bfloat16),
            pltpu.VMEM((ctx_dev, head_dim), jnp.bfloat16),
            pltpu.VMEM((keys, rows), jnp.float32),
            pltpu.SemaphoreType.DMA((2, 4)),
        ],
        compiler_params=pltpu.CompilerParams(vmem_limit_bytes=51 * 2**20),
    )(table, recv, k_peer, v_peer, k_own, v_own)
    result = pl.pallas_call(
        functools.partial(
            span_kernel,
            tok_rows=tok_rows,
            group_heads=group_heads,
            head_dim=head_dim,
            context=2 * ctx_dev,
        ),
        out_shape=jax.ShapeDtypeStruct((tokens, group_width), jnp.bfloat16),
        in_specs=[SMEM_SPEC] + [VMEM_SPEC] * 4,
        out_specs=VMEM_SPEC,
        compiler_params=pltpu.CompilerParams(vmem_limit_bytes=4 * 2**20),
    )(table, recv, peer, acc, stat)
    result = result.reshape(head_count, tok_rows, group_width)
    back = lax.all_to_all(result, "head", split_axis=0, concat_axis=0, tiled=True)
    return pl.pallas_call(
        unpack_kernel,
        out_shape=jax.ShapeDtypeStruct((tok_rows, KVH * group_width), jnp.bfloat16),
        in_specs=[SMEM_SPEC, VMEM_SPEC],
        out_specs=HBM_SPEC,
        scratch_shapes=[pltpu.SemaphoreType.DMA((head_count,))],
        compiler_params=pltpu.CompilerParams(vmem_limit_bytes=2**20),
    )(table, back)


def solution(mesh):
    on_device = on_device_pairs if mesh.shape["head"] == KVH else on_device_quarters
    in_specs = (
        P(("rep", "head", "seq"), None),
        P(("rep", "head", "seq"), None),
        P(("rep", "head", "seq"), None),
        P(("rep", "head"), "seq", None),
        P(("rep", "head"), "seq", None),
        P("rep"),
        P("rep"),
        P("rep"),
        P("rep"),
    )
    out_specs = P(("rep", "head", "seq"), None)
    return jax.shard_map(
        on_device, mesh=mesh, in_specs=in_specs, out_specs=out_specs, check_vma=False
    )
```

```python
import functools
import math

import jax
import jax.numpy as jnp
from jax import lax
from jax.experimental import pallas as pl
from jax.experimental.pallas import tpu as pltpu
from jax.sharding import PartitionSpec as P

KVH = 8


NEG_FILL = -1e30


def absorb(
    running,
    query_rows,
    query_pos,
    key_rows,
    value_rows,
    key_pos,
    is_retrieval,
    window_len,
    sink_len,
    score_scale,
):
    top_score, totals, weighted = running
    scores = jnp.dot(query_rows, key_rows.T, preferred_element_type=jnp.float32) * score_scale
    allowed = (key_pos[None, :] <= query_pos[:, None]) & (
        (is_retrieval == 1)
        | (key_pos[None, :] < sink_len)
        | (key_pos[None, :] > query_pos[:, None] - window_len)
    )
    block_top = jnp.max(jnp.where(allowed, scores, NEG_FILL), axis=1)
    new_top = jnp.maximum(top_score, block_top)
    weights = jnp.where(allowed, jnp.exp(scores - new_top[:, None]), 0.0)
    rescale = jnp.exp(top_score - new_top)
    totals = totals * rescale + jnp.sum(weights, axis=1)
    weighted = weighted * rescale[:, None] + jnp.dot(
        weights.astype(jnp.bfloat16), value_rows, preferred_element_type=jnp.float32
    )
    return (new_top, totals, weighted)


def finish_rows(received, spread, head_list, tok_rows, head_dim):
    top_score, totals, weighted = received
    group_heads = top_score.shape[-1]
    top_score = top_score.reshape(KVH, spread, tok_rows, group_heads)
    totals = totals.reshape(KVH, spread, tok_rows, group_heads)
    weighted = weighted.reshape(KVH, spread, tok_rows, group_heads, head_dim)
    overall = jnp.max(top_score, axis=1, keepdims=True)
    factor = jnp.exp(top_score - overall)
    summed = jnp.sum(totals * factor, axis=1)
    combined = jnp.sum(weighted * factor[..., None], axis=1)
    result = combined / summed[..., None]
    matches = (head_list[:, None] == jnp.arange(KVH, dtype=jnp.int32)[None, :]).astype(jnp.int32)
    inverse = jnp.sum(jnp.arange(KVH, dtype=jnp.int32)[:, None] * matches, axis=0)
    by_group = jnp.take(result, inverse, axis=0)
    return (
        by_group.transpose(1, 0, 2, 3)
        .reshape(tok_rows, KVH * group_heads * head_dim)
        .astype(jnp.bfloat16)
    )


def on_device_quarters(q_span, k_span, v_span, k_cache, v_cache, head_list, retrieval, windows, sinks):
    head_count = lax.axis_size("head")
    pair_count = lax.axis_size("seq")
    quarters = head_count // KVH
    tok_rows = q_span.shape[0]
    group_width = q_span.shape[1] // KVH
    head_dim = k_cache.shape[2]
    group_heads = group_width // head_dim
    ctx_dev = k_cache.shape[1]
    total_q = tok_rows * head_count * pair_count
    context = ctx_dev * pair_count * quarters
    head_at = lax.axis_index("head")
    pair_at = lax.axis_index("seq")
    slot_index = head_at // quarters
    quarter = head_at % quarters
    kv_group = jnp.take(head_list, slot_index)
    q_groups = q_span.reshape(tok_rows, KVH, group_width)
    kv_groups = jnp.concatenate(
        [k_span.reshape(tok_rows, KVH, head_dim), v_span.reshape(tok_rows, KVH, head_dim)], axis=2
    )
    targets = jnp.take(head_list, jnp.arange(head_count * pair_count) // pair_count // quarters)
    q_send = jnp.take(q_groups, targets, axis=1)
    kv_send = jnp.take(kv_groups, targets, axis=1)
    q_recv, kv_recv = (
        lax.all_to_all(q_send, ("head", "seq"), split_axis=1, concat_axis=0, tiled=True),
        lax.all_to_all(kv_send, ("head", "seq"), split_axis=1, concat_axis=0, tiled=True),
    )
    queries = q_recv.reshape(total_q, group_width)
    span_kv = kv_recv.reshape(total_q, 2 * head_dim)
    query_rows = queries.reshape(total_q * group_heads, head_dim)
    query_pos = context + jnp.arange(total_q * group_heads, dtype=jnp.int32) // group_heads
    is_retrieval = jnp.take(retrieval, kv_group)
    window_len = jnp.take(windows, kv_group)
    sink_len = jnp.take(sinks, kv_group)
    score_scale = 1.0 / math.sqrt(head_dim)
    row_total = total_q * group_heads
    running = (
        jnp.full((row_total,), NEG_FILL, jnp.float32),
        jnp.zeros((row_total,), jnp.float32),
        jnp.zeros((row_total, head_dim), jnp.float32),
    )
    key_block = min(512, ctx_dev)
    segment = quarter * pair_count + pair_at
    first_key = segment * ctx_dev
    cache_keys = k_cache[0]
    cache_values = v_cache[0]

    def key_step(step_index, state):
        start = step_index * key_block
        key_rows = lax.dynamic_slice_in_dim(cache_keys, start, key_block, 0)
        value_rows = lax.dynamic_slice_in_dim(cache_values, start, key_block, 0)
        key_pos = first_key + start + jnp.arange(key_block, dtype=jnp.int32)
        return absorb(
            state,
            query_rows,
            query_pos,
            key_rows,
            value_rows,
            key_pos,
            is_retrieval,
            window_len,
            sink_len,
            score_scale,
        )

    running = lax.fori_loop(0, ctx_dev // key_block, key_step, running)
    span_piece = total_q // (quarters * pair_count)
    span_start = segment * span_piece
    span_rows = lax.dynamic_slice_in_dim(span_kv, span_start, span_piece, 0)
    span_pos = context + span_start + jnp.arange(span_piece, dtype=jnp.int32)
    top_score, totals, weighted = absorb(
        running,
        query_rows,
        query_pos,
        span_rows[:, :head_dim],
        span_rows[:, head_dim:],
        span_pos,
        is_retrieval,
        window_len,
        sink_len,
        score_scale,
    )
    received = (
        lax.all_to_all(
            top_score.reshape(head_count * pair_count, tok_rows, group_heads),
            ("head", "seq"),
            split_axis=0,
            concat_axis=0,
            tiled=True,
        ),
        lax.all_to_all(
            totals.reshape(head_count * pair_count, tok_rows, group_heads),
            ("head", "seq"),
            split_axis=0,
            concat_axis=0,
            tiled=True,
        ),
        lax.all_to_all(
            weighted.reshape(head_count * pair_count, tok_rows, group_width),
            ("head", "seq"),
            split_axis=0,
            concat_axis=0,
            tiled=True,
        ),
    )
    spread = quarters * pair_count
    return finish_rows(received, spread, head_list, tok_rows, head_dim)


VMEM_SPEC = pl.BlockSpec(memory_space=pltpu.VMEM)
HBM_SPEC = pl.BlockSpec(memory_space=pltpu.HBM)
SMEM_SPEC = pl.BlockSpec(memory_space=pltpu.SMEM)


def pack_kernel(head_ref, in_ref, out_ref, *, group_width, head_dim):
    q_width = KVH * group_width
    q_ref = in_ref.at[:, :q_width]
    k_ref = in_ref.at[:, q_width : q_width + KVH * head_dim]
    v_ref = in_ref.at[:, q_width + KVH * head_dim :]
    for slot in range(out_ref.shape[0]):
        group = head_ref[slot]
        q_start = pl.multiple_of(group * group_width, 128)
        kv_start = pl.multiple_of(group * head_dim, 128)
        out_ref[slot, :, :group_width] = q_ref[:, pl.ds(q_start, group_width)]
        out_ref[slot, :, group_width : group_width + head_dim] = k_ref[:, pl.ds(kv_start, head_dim)]
        out_ref[slot, :, group_width + head_dim :] = v_ref[:, pl.ds(kv_start, head_dim)]


def unpack_kernel(head_ref, in_ref, out_ref, sems):
    width = in_ref.shape[2]
    copies = []
    for slot in range(in_ref.shape[0]):
        start = pl.multiple_of(head_ref[slot] * width, 128)
        copies.append(
            pltpu.make_async_copy(in_ref.at[slot], out_ref.at[:, pl.ds(start, width)], sems.at[slot])
        )
    for copy in copies:
        copy.start()
    for copy in copies:
        copy.wait()


def look_up(table_ref):
    kv_group = table_ref[lax.axis_index("head")]
    return (table_ref[part * KVH + kv_group] for part in (1, 2, 3))


def stack_queries(recv_ref, group_heads, head_dim):
    scale = math.log2(math.e) / math.sqrt(head_dim)
    queries = jnp.concatenate(
        [recv_ref[:, k * head_dim : (k + 1) * head_dim] for k in range(group_heads)], axis=0
    )
    scaled = queries.astype(jnp.float32) * scale
    high = scaled.astype(jnp.bfloat16)
    low = (scaled - high.astype(jnp.float32)).astype(jnp.bfloat16)
    return jnp.concatenate([high, low], axis=1)


def span_kernel(
    table_ref,
    recv_ref,
    peer_ref,
    acc_ref,
    stat_ref,
    out_ref,
    *,
    tok_rows,
    group_heads,
    head_dim,
    context,
):
    f32, bf16 = jnp.float32, jnp.bfloat16
    pair_at = lax.axis_index("seq")
    is_retrieval, window_len, sink_len = look_up(table_ref)
    window_len = jnp.where(is_retrieval == 1, 2**30, window_len)
    tokens = recv_ref.shape[0]
    rows = tokens * group_heads
    group_width = group_heads * head_dim
    queries = stack_queries(recv_ref, group_heads, head_dim)

    def token_pos(index, pair):
        return context + ((index // tok_rows) * 2 + pair) * tok_rows + index % tok_rows

    query_pos = token_pos(lax.broadcasted_iota(jnp.int32, (1, rows), 1) % tokens, pair_at)
    key_pos = token_pos(lax.broadcasted_iota(jnp.int32, (tokens, 1), 0), 1 - pair_at)
    keys = peer_ref[:, group_width : group_width + head_dim]
    values = peer_ref[:, group_width + head_dim : group_width + 2 * head_dim]
    block = lax.dot_general(
        jnp.concatenate([keys, keys], axis=1),
        queries,
        (((1,), (1,)), ((), ())),
        preferred_element_type=f32,
    )
    allowed = (key_pos <= query_pos) & ((key_pos < sink_len) | (key_pos > query_pos - window_len))
    block = jnp.where(allowed, block, NEG_FILL)
    old_top = stat_ref[0:1, :]
    top = jnp.maximum(old_top, jnp.max(block, axis=0, keepdims=True))
    factor = jnp.exp2(old_top - top)
    weights = jnp.exp2(block - top)
    total = jnp.sum(stat_ref[8:16, :], axis=0, keepdims=True) * factor
    total = total + jnp.sum(weights, axis=0, keepdims=True)
    acc = acc_ref[...] * factor + lax.dot_general(
        values, weights.astype(bf16), (((0,), (0,)), ((), ())), preferred_element_type=f32
    )
    result = (acc / total).T.astype(bf16)
    for head in range(group_heads):
        out_ref[:, head * head_dim : (head + 1) * head_dim] = result[head * tokens : (head + 1) * tokens]


def attend_kernel(
    table_ref,
    recv_ref,
    k_peer,
    v_peer,
    k_source,
    v_source,
    acc_ref,
    stat_ref,
    k_own,
    v_own,
    score_ref,
    own_sem,
    *,
    tok_rows,
    group_heads,
    head_dim,
    key_block,
    row_block,
):

    def own_copies(source, target, which):
        size = source.shape[0] // own_sem.shape[1]
        return [
            pltpu.make_async_copy(
                source.at[pl.ds(chunk * size, size)],
                target.at[pl.ds(chunk * size, size)],
                own_sem.at[which, chunk],
            )
            for chunk in range(own_sem.shape[1])
        ]

    k_copies = own_copies(k_source, k_own, 0)
    v_copies = own_copies(v_source, v_own, 1)
    for copy in k_copies:
        copy.start()

    def end_k_start_v():
        for copy in k_copies:
            copy.wait()
        for copy in v_copies:
            copy.start()

    def end_v():
        for copy in v_copies:
            copy.wait()

    pair_at = lax.axis_index("seq")
    is_retrieval, window_len, sink_len = look_up(table_ref)
    tokens = recv_ref.shape[0]
    rows = tokens * group_heads
    group_width = group_heads * head_dim
    ctx_dev = k_own.shape[0]
    context = 2 * ctx_dev
    f32, bf16 = jnp.float32, jnp.bfloat16
    def token_pos(index, pair):
        return context + ((index // tok_rows) * 2 + pair) * tok_rows + index % tok_rows

    queries = stack_queries(recv_ref, group_heads, head_dim)
    row_token = lax.broadcasted_iota(jnp.int32, (1, rows), 1) % tokens
    query_pos = token_pos(row_token, pair_at)

    span_k = pl.ds(group_width, head_dim)
    span_v = pl.ds(group_width + head_dim, head_dim)

    def build(key_block):
        cached, spans = [], []
        for k_ref, v_ref, pair in ((k_peer, v_peer, 1 - pair_at), (k_own, v_own, pair_at)):
            for start in range(0, ctx_dev, key_block):
                cached.append((k_ref, v_ref, start, key_block, pair))
        spans.append((recv_ref, pair_at))

        def load_keys(index):
            if index < len(cached):
                k_ref, _, start, size, _ = cached[index]
                return k_ref[start : start + size, :]
            return spans[index - len(cached)][0][:, span_k]

        def load_values(index):
            if index < len(cached):
                _, v_ref, start, size, _ = cached[index]
                return v_ref[start : start + size, :]
            return spans[index - len(cached)][0][:, span_v]

        def place(index):
            if index < len(cached):
                return index * key_block, key_block
            return len(cached) * key_block + (index - len(cached)) * tokens, tokens

        def first_pos(index):
            _, _, start, _, pair = cached[index]
            return pair * ctx_dev + start

        def scores(index, row_at, masked):
            keys = load_keys(index)
            keys = jnp.concatenate([keys, keys], axis=1)
            block = lax.dot_general(
                keys,
                queries[row_at : row_at + row_block],
                (((1,), (1,)), ((), ())),
                preferred_element_type=f32,
            )
            size = block.shape[0]
            pos_q = query_pos[:, row_at : row_at + row_block]
            column = lax.broadcasted_iota(jnp.int32, (size, 1), 0)
            allowed = None
            if index >= len(cached):
                pos_k = token_pos(column, spans[index - len(cached)][1])
                allowed = pos_k <= pos_q
            else:
                pos_k = first_pos(index) + column
            if masked:
                near = (pos_k < sink_len) | (pos_k > pos_q - window_len)
                allowed = near if allowed is None else allowed & near
            if allowed is not None:
                block = jnp.where(allowed, block, NEG_FILL)
            start, _ = place(index)
            score_ref[start : start + size, row_at : row_at + row_block] = block
            return jnp.max(block.reshape(size // 8, 8, row_block), axis=0)

        def weighted(index, row_at, top):
            start, size = place(index)
            block = score_ref[start : start + size, row_at : row_at + row_block]
            weights = jnp.exp2(block - top)
            total = jnp.sum(weights.reshape(size // 8, 8, row_block), axis=0)
            acc = lax.dot_general(
                load_values(index),
                weights.astype(bf16),
                (((0,), (0,)), ((), ())),
                preferred_element_type=f32,
            )
            return total, acc

        return len(cached), len(spans), first_pos, scores, weighted

    row_starts = list(range(0, rows, row_block))

    @pl.when(is_retrieval == 1)
    def _():
        cached, spans, _, scores, weighted = build(math.gcd(ctx_dev, 512))
        peer_blocks = list(range(cached // 2))
        own_blocks = list(range(cached // 2, cached + spans))
        running, total, acc = {}, {}, {}

        def first(indices):
            for row_at in row_starts:
                for index in indices:
                    top = scores(index, row_at, False)
                    running[row_at] = jnp.maximum(running[row_at], top) if row_at in running else top

        def second(indices):
            for row_at in row_starts:
                top = jnp.max(running[row_at], axis=0, keepdims=True)
                for index in indices:
                    part_total, part_acc = weighted(index, row_at, top)
                    total[row_at] = total[row_at] + part_total if row_at in total else part_total
                    acc[row_at] = acc[row_at] + part_acc if row_at in acc else part_acc

        first(peer_blocks)
        end_k_start_v()
        first(own_blocks)
        second(peer_blocks)
        end_v()
        second(own_blocks)
        for row_at in row_starts:
            cols = slice(row_at, row_at + row_block)
            top = jnp.max(running[row_at], axis=0, keepdims=True)
            stat_ref[0:8, cols] = jnp.broadcast_to(top, (8, row_block))
            stat_ref[8:16, cols] = total[row_at]
            acc_ref[:, cols] = acc[row_at]

    @pl.when(is_retrieval != 1)
    def _():
        cached, spans, first_pos, scores, weighted = build(key_block)
        peer_blocks = list(range(cached // 2))
        own_blocks = list(range(cached // 2, cached + spans))

        def needed(index):
            pos = first_pos(index)
            return (pos < sink_len) | (pos + key_block - 1 > context - window_len)

        stat_ref[0:8, :] = jnp.full((8, rows), NEG_FILL, f32)
        stat_ref[8:16, :] = jnp.zeros((8, rows), f32)
        acc_ref[...] = jnp.zeros(acc_ref.shape, f32)

        def first(index):
            for row_at in row_starts:
                cols = slice(row_at, row_at + row_block)
                stat_ref[0:8, cols] = jnp.maximum(stat_ref[0:8, cols], scores(index, row_at, True))

        def second(index):
            for row_at in row_starts:
                cols = slice(row_at, row_at + row_block)
                top = jnp.max(stat_ref[0:8, cols], axis=0, keepdims=True)
                total, acc = weighted(index, row_at, top)
                stat_ref[8:16, cols] += total
                acc_ref[:, cols] += acc

        def each(work, indices):
            for index in indices:
                if index < cached:
                    pl.when(needed(index))(functools.partial(work, index))
                else:
                    work(index)

        each(first, peer_blocks)
        end_k_start_v()
        each(first, own_blocks)
        each(second, peer_blocks)
        end_v()
        each(second, own_blocks)
        top = jnp.max(stat_ref[0:8, :], axis=0, keepdims=True)
        stat_ref[0:8, :] = jnp.broadcast_to(top, (8, rows))


def on_device_pairs(q_span, k_span, v_span, k_cache, v_cache, head_list, retrieval, windows, sinks):
    head_count = lax.axis_size("head")
    tok_rows = q_span.shape[0]
    group_width = q_span.shape[1] // KVH
    head_dim = k_cache.shape[2]
    group_heads = group_width // head_dim
    ctx_dev = k_cache.shape[1]
    tokens = tok_rows * head_count
    rows = tokens * group_heads
    swap = [(0, 1), (1, 0)]
    k_own, v_own = k_cache[0], v_cache[0]
    k_peer = lax.ppermute(k_own, "seq", swap)
    v_peer = lax.ppermute(v_own, "seq", swap)
    joined = jnp.concatenate([q_span, k_span, v_span], axis=1)
    joined, *indices = lax.optimization_barrier((joined, head_list, retrieval, windows, sinks))
    table = jnp.concatenate(indices)
    send = pl.pallas_call(
        functools.partial(pack_kernel, group_width=group_width, head_dim=head_dim),
        out_shape=jax.ShapeDtypeStruct((head_count, tok_rows, group_width + 2 * head_dim), jnp.bfloat16),
        in_specs=[SMEM_SPEC, VMEM_SPEC],
        out_specs=VMEM_SPEC,
        compiler_params=pltpu.CompilerParams(vmem_limit_bytes=2**20),
    )(table, joined)
    recv = lax.all_to_all(send, "head", split_axis=0, concat_axis=0, tiled=True)
    recv = recv.reshape(tokens, group_width + 2 * head_dim)
    peer = lax.ppermute(recv, "seq", swap)
    key_block = math.gcd(ctx_dev, 1024)
    row_block = 256
    keys = 2 * ctx_dev + tokens
    acc, stat = pl.pallas_call(
        functools.partial(
            attend_kernel,
            tok_rows=tok_rows,
            group_heads=group_heads,
            head_dim=head_dim,
            key_block=key_block,
            row_block=row_block,
        ),
        out_shape=(
            jax.ShapeDtypeStruct((head_dim, rows), jnp.float32),
            jax.ShapeDtypeStruct((16, rows), jnp.float32),
        ),
        in_specs=[SMEM_SPEC] + [VMEM_SPEC] * 3 + [HBM_SPEC] * 2,
        out_specs=(VMEM_SPEC, VMEM_SPEC),
        scratch_shapes=[
            pltpu.VMEM((ctx_dev, head_dim), jnp.bfloat16),
            pltpu.VMEM((ctx_dev, head_dim), jnp.bfloat16),
            pltpu.VMEM((keys, rows), jnp.float32),
            pltpu.SemaphoreType.DMA((2, 4)),
        ],
        compiler_params=pltpu.CompilerParams(vmem_limit_bytes=51 * 2**20),
    )(table, recv, k_peer, v_peer, k_own, v_own)
    result = pl.pallas_call(
        functools.partial(
            span_kernel,
            tok_rows=tok_rows,
            group_heads=group_heads,
            head_dim=head_dim,
            context=2 * ctx_dev,
        ),
        out_shape=jax.ShapeDtypeStruct((tokens, group_width), jnp.bfloat16),
        in_specs=[SMEM_SPEC] + [VMEM_SPEC] * 4,
        out_specs=VMEM_SPEC,
        compiler_params=pltpu.CompilerParams(vmem_limit_bytes=4 * 2**20),
    )(table, recv, peer, acc, stat)
    result = result.reshape(head_count, tok_rows, group_width)
    back = lax.all_to_all(result, "head", split_axis=0, concat_axis=0, tiled=True)
    return pl.pallas_call(
        unpack_kernel,
        out_shape=jax.ShapeDtypeStruct((tok_rows, KVH * group_width), jnp.bfloat16),
        in_specs=[SMEM_SPEC, VMEM_SPEC],
        out_specs=HBM_SPEC,
        scratch_shapes=[pltpu.SemaphoreType.DMA((head_count,))],
        compiler_params=pltpu.CompilerParams(vmem_limit_bytes=2**20),
    )(table, back)


def solution(mesh):
    on_device = on_device_pairs if mesh.shape["head"] == KVH else on_device_quarters
    in_specs = (
        P(("rep", "head", "seq"), None),
        P(("rep", "head", "seq"), None),
        P(("rep", "head", "seq"), None),
        P(("rep", "head"), "seq", None),
        P(("rep", "head"), "seq", None),
        P("rep"),
        P("rep"),
        P("rep"),
        P("rep"),
    )
    out_specs = P(("rep", "head", "seq"), None)
    return jax.shard_map(
        on_device, mesh=mesh, in_specs=in_specs, out_specs=out_specs, check_vma=False
    )
```

```python
import functools
import math

import jax
import jax.numpy as jnp
from jax import lax
from jax.experimental import pallas as pl
from jax.experimental.pallas import tpu as pltpu
from jax.sharding import PartitionSpec as P

KVH = 8


NEG_FILL = -1e30


def absorb(
    running,
    query_rows,
    query_pos,
    key_rows,
    value_rows,
    key_pos,
    is_retrieval,
    window_len,
    sink_len,
    score_scale,
):
    top_score, totals, weighted = running
    scores = jnp.dot(query_rows, key_rows.T, preferred_element_type=jnp.float32) * score_scale
    allowed = (key_pos[None, :] <= query_pos[:, None]) & (
        (is_retrieval == 1)
        | (key_pos[None, :] < sink_len)
        | (key_pos[None, :] > query_pos[:, None] - window_len)
    )
    block_top = jnp.max(jnp.where(allowed, scores, NEG_FILL), axis=1)
    new_top = jnp.maximum(top_score, block_top)
    weights = jnp.where(allowed, jnp.exp(scores - new_top[:, None]), 0.0)
    rescale = jnp.exp(top_score - new_top)
    totals = totals * rescale + jnp.sum(weights, axis=1)
    weighted = weighted * rescale[:, None] + jnp.dot(
        weights.astype(jnp.bfloat16), value_rows, preferred_element_type=jnp.float32
    )
    return (new_top, totals, weighted)


def finish_rows(received, spread, head_list, tok_rows, head_dim):
    top_score, totals, weighted = received
    group_heads = top_score.shape[-1]
    top_score = top_score.reshape(KVH, spread, tok_rows, group_heads)
    totals = totals.reshape(KVH, spread, tok_rows, group_heads)
    weighted = weighted.reshape(KVH, spread, tok_rows, group_heads, head_dim)
    overall = jnp.max(top_score, axis=1, keepdims=True)
    factor = jnp.exp(top_score - overall)
    summed = jnp.sum(totals * factor, axis=1)
    combined = jnp.sum(weighted * factor[..., None], axis=1)
    result = combined / summed[..., None]
    matches = (head_list[:, None] == jnp.arange(KVH, dtype=jnp.int32)[None, :]).astype(jnp.int32)
    inverse = jnp.sum(jnp.arange(KVH, dtype=jnp.int32)[:, None] * matches, axis=0)
    by_group = jnp.take(result, inverse, axis=0)
    return (
        by_group.transpose(1, 0, 2, 3)
        .reshape(tok_rows, KVH * group_heads * head_dim)
        .astype(jnp.bfloat16)
    )


def on_device_quarters(q_span, k_span, v_span, k_cache, v_cache, head_list, retrieval, windows, sinks):
    head_count = lax.axis_size("head")
    pair_count = lax.axis_size("seq")
    quarters = head_count // KVH
    tok_rows = q_span.shape[0]
    group_width = q_span.shape[1] // KVH
    head_dim = k_cache.shape[2]
    group_heads = group_width // head_dim
    ctx_dev = k_cache.shape[1]
    total_q = tok_rows * head_count * pair_count
    context = ctx_dev * pair_count * quarters
    head_at = lax.axis_index("head")
    pair_at = lax.axis_index("seq")
    slot_index = head_at // quarters
    quarter = head_at % quarters
    kv_group = jnp.take(head_list, slot_index)
    q_groups = q_span.reshape(tok_rows, KVH, group_width)
    kv_groups = jnp.concatenate(
        [k_span.reshape(tok_rows, KVH, head_dim), v_span.reshape(tok_rows, KVH, head_dim)], axis=2
    )
    targets = jnp.take(head_list, jnp.arange(head_count * pair_count) // pair_count // quarters)
    q_send = jnp.take(q_groups, targets, axis=1)
    kv_send = jnp.take(kv_groups, targets, axis=1)
    q_recv, kv_recv = (
        lax.all_to_all(q_send, ("head", "seq"), split_axis=1, concat_axis=0, tiled=True),
        lax.all_to_all(kv_send, ("head", "seq"), split_axis=1, concat_axis=0, tiled=True),
    )
    queries = q_recv.reshape(total_q, group_width)
    span_kv = kv_recv.reshape(total_q, 2 * head_dim)
    query_rows = queries.reshape(total_q * group_heads, head_dim)
    query_pos = context + jnp.arange(total_q * group_heads, dtype=jnp.int32) // group_heads
    is_retrieval = jnp.take(retrieval, kv_group)
    window_len = jnp.take(windows, kv_group)
    sink_len = jnp.take(sinks, kv_group)
    score_scale = 1.0 / math.sqrt(head_dim)
    row_total = total_q * group_heads
    running = (
        jnp.full((row_total,), NEG_FILL, jnp.float32),
        jnp.zeros((row_total,), jnp.float32),
        jnp.zeros((row_total, head_dim), jnp.float32),
    )
    key_block = min(512, ctx_dev)
    segment = quarter * pair_count + pair_at
    first_key = segment * ctx_dev
    cache_keys = k_cache[0]
    cache_values = v_cache[0]

    def key_step(step_index, state):
        start = step_index * key_block
        key_rows = lax.dynamic_slice_in_dim(cache_keys, start, key_block, 0)
        value_rows = lax.dynamic_slice_in_dim(cache_values, start, key_block, 0)
        key_pos = first_key + start + jnp.arange(key_block, dtype=jnp.int32)
        return absorb(
            state,
            query_rows,
            query_pos,
            key_rows,
            value_rows,
            key_pos,
            is_retrieval,
            window_len,
            sink_len,
            score_scale,
        )

    running = lax.fori_loop(0, ctx_dev // key_block, key_step, running)
    span_piece = total_q // (quarters * pair_count)
    span_start = segment * span_piece
    span_rows = lax.dynamic_slice_in_dim(span_kv, span_start, span_piece, 0)
    span_pos = context + span_start + jnp.arange(span_piece, dtype=jnp.int32)
    top_score, totals, weighted = absorb(
        running,
        query_rows,
        query_pos,
        span_rows[:, :head_dim],
        span_rows[:, head_dim:],
        span_pos,
        is_retrieval,
        window_len,
        sink_len,
        score_scale,
    )
    received = (
        lax.all_to_all(
            top_score.reshape(head_count * pair_count, tok_rows, group_heads),
            ("head", "seq"),
            split_axis=0,
            concat_axis=0,
            tiled=True,
        ),
        lax.all_to_all(
            totals.reshape(head_count * pair_count, tok_rows, group_heads),
            ("head", "seq"),
            split_axis=0,
            concat_axis=0,
            tiled=True,
        ),
        lax.all_to_all(
            weighted.reshape(head_count * pair_count, tok_rows, group_width),
            ("head", "seq"),
            split_axis=0,
            concat_axis=0,
            tiled=True,
        ),
    )
    spread = quarters * pair_count
    return finish_rows(received, spread, head_list, tok_rows, head_dim)


VMEM_SPEC = pl.BlockSpec(memory_space=pltpu.VMEM)
HBM_SPEC = pl.BlockSpec(memory_space=pltpu.HBM)
SMEM_SPEC = pl.BlockSpec(memory_space=pltpu.SMEM)


def pack_kernel(head_ref, in_ref, out_ref, *, group_width, head_dim):
    q_width = KVH * group_width
    q_ref = in_ref.at[:, :q_width]
    k_ref = in_ref.at[:, q_width : q_width + KVH * head_dim]
    v_ref = in_ref.at[:, q_width + KVH * head_dim :]
    for slot in range(out_ref.shape[0]):
        group = head_ref[slot]
        q_start = pl.multiple_of(group * group_width, 128)
        kv_start = pl.multiple_of(group * head_dim, 128)
        out_ref[slot, :, :group_width] = q_ref[:, pl.ds(q_start, group_width)]
        out_ref[slot, :, group_width : group_width + head_dim] = k_ref[:, pl.ds(kv_start, head_dim)]
        out_ref[slot, :, group_width + head_dim :] = v_ref[:, pl.ds(kv_start, head_dim)]


def unpack_kernel(head_ref, in_ref, out_ref, sems):
    width = in_ref.shape[2]
    copies = []
    for slot in range(in_ref.shape[0]):
        start = pl.multiple_of(head_ref[slot] * width, 128)
        copies.append(
            pltpu.make_async_copy(in_ref.at[slot], out_ref.at[:, pl.ds(start, width)], sems.at[slot])
        )
    for copy in copies:
        copy.start()
    for copy in copies:
        copy.wait()


def look_up(table_ref):
    kv_group = table_ref[lax.axis_index("head")]
    return (table_ref[part * KVH + kv_group] for part in (1, 2, 3))


def stack_queries(recv_ref, group_heads, head_dim):
    scale = math.log2(math.e) / math.sqrt(head_dim)
    queries = jnp.concatenate(
        [recv_ref[:, k * head_dim : (k + 1) * head_dim] for k in range(group_heads)], axis=0
    )
    scaled = queries.astype(jnp.float32) * scale
    high = scaled.astype(jnp.bfloat16)
    low = (scaled - high.astype(jnp.float32)).astype(jnp.bfloat16)
    return jnp.concatenate([high, low], axis=1)


def span_kernel(
    table_ref,
    recv_ref,
    peer_ref,
    acc_ref,
    stat_ref,
    out_ref,
    *,
    tok_rows,
    group_heads,
    head_dim,
    context,
):
    f32, bf16 = jnp.float32, jnp.bfloat16
    pair_at = lax.axis_index("seq")
    is_retrieval, window_len, sink_len = look_up(table_ref)
    window_len = jnp.where(is_retrieval == 1, 2**30, window_len)
    tokens = recv_ref.shape[0]
    rows = tokens * group_heads
    group_width = group_heads * head_dim
    queries = stack_queries(recv_ref, group_heads, head_dim)

    def token_pos(index, pair):
        return context + ((index // tok_rows) * 2 + pair) * tok_rows + index % tok_rows

    query_pos = token_pos(lax.broadcasted_iota(jnp.int32, (1, rows), 1) % tokens, pair_at)
    key_pos = token_pos(lax.broadcasted_iota(jnp.int32, (tokens, 1), 0), 1 - pair_at)
    keys = peer_ref[:, group_width : group_width + head_dim]
    values = peer_ref[:, group_width + head_dim : group_width + 2 * head_dim]
    block = lax.dot_general(
        jnp.concatenate([keys, keys], axis=1),
        queries,
        (((1,), (1,)), ((), ())),
        preferred_element_type=f32,
    )
    allowed = (key_pos <= query_pos) & ((key_pos < sink_len) | (key_pos > query_pos - window_len))
    block = jnp.where(allowed, block, NEG_FILL)
    old_top = stat_ref[0:1, :]
    top = jnp.maximum(old_top, jnp.max(block, axis=0, keepdims=True))
    factor = jnp.exp2(old_top - top)
    weights = jnp.exp2(block - top)
    total = jnp.sum(stat_ref[8:16, :], axis=0, keepdims=True) * factor
    total = total + jnp.sum(weights, axis=0, keepdims=True)
    acc = acc_ref[...] * factor + lax.dot_general(
        values, weights.astype(bf16), (((0,), (0,)), ((), ())), preferred_element_type=f32
    )
    result = (acc / total).T.astype(bf16)
    for head in range(group_heads):
        out_ref[:, head * head_dim : (head + 1) * head_dim] = result[head * tokens : (head + 1) * tokens]


def attend_kernel(
    table_ref,
    recv_ref,
    k_peer,
    v_peer,
    k_source,
    v_source,
    acc_ref,
    stat_ref,
    k_own,
    v_own,
    score_ref,
    own_sem,
    *,
    tok_rows,
    group_heads,
    head_dim,
    key_block,
    row_block,
):

    def own_copies(source, target, which):
        size = source.shape[0] // own_sem.shape[1]
        return [
            pltpu.make_async_copy(
                source.at[pl.ds(chunk * size, size)],
                target.at[pl.ds(chunk * size, size)],
                own_sem.at[which, chunk],
            )
            for chunk in range(own_sem.shape[1])
        ]

    k_copies = own_copies(k_source, k_own, 0)
    v_copies = own_copies(v_source, v_own, 1)
    for copy in k_copies:
        copy.start()

    def end_k_start_v():
        for copy in k_copies:
            copy.wait()
        for copy in v_copies:
            copy.start()

    def end_v():
        for copy in v_copies:
            copy.wait()

    pair_at = lax.axis_index("seq")
    is_retrieval, window_len, sink_len = look_up(table_ref)
    tokens = recv_ref.shape[0]
    rows = tokens * group_heads
    group_width = group_heads * head_dim
    ctx_dev = k_own.shape[0]
    context = 2 * ctx_dev
    f32, bf16 = jnp.float32, jnp.bfloat16
    def token_pos(index, pair):
        return context + ((index // tok_rows) * 2 + pair) * tok_rows + index % tok_rows

    queries = stack_queries(recv_ref, group_heads, head_dim)
    row_token = lax.broadcasted_iota(jnp.int32, (1, rows), 1) % tokens
    query_pos = token_pos(row_token, pair_at)

    span_k = pl.ds(group_width, head_dim)
    span_v = pl.ds(group_width + head_dim, head_dim)

    def build(key_block):
        cached, spans = [], []
        for k_ref, v_ref, pair in ((k_peer, v_peer, 1 - pair_at), (k_own, v_own, pair_at)):
            for start in range(0, ctx_dev, key_block):
                cached.append((k_ref, v_ref, start, key_block, pair))
        spans.append((recv_ref, pair_at))

        def load_keys(index):
            if index < len(cached):
                k_ref, _, start, size, _ = cached[index]
                return k_ref[start : start + size, :]
            return spans[index - len(cached)][0][:, span_k]

        def load_values(index):
            if index < len(cached):
                _, v_ref, start, size, _ = cached[index]
                return v_ref[start : start + size, :]
            return spans[index - len(cached)][0][:, span_v]

        def place(index):
            if index < len(cached):
                return index * key_block, key_block
            return len(cached) * key_block + (index - len(cached)) * tokens, tokens

        def first_pos(index):
            _, _, start, _, pair = cached[index]
            return pair * ctx_dev + start

        def scores(index, row_at, masked):
            keys = load_keys(index)
            keys = jnp.concatenate([keys, keys], axis=1)
            block = lax.dot_general(
                keys,
                queries[row_at : row_at + row_block],
                (((1,), (1,)), ((), ())),
                preferred_element_type=f32,
            )
            size = block.shape[0]
            pos_q = query_pos[:, row_at : row_at + row_block]
            column = lax.broadcasted_iota(jnp.int32, (size, 1), 0)
            allowed = None
            if index >= len(cached):
                pos_k = token_pos(column, spans[index - len(cached)][1])
                allowed = pos_k <= pos_q
            else:
                pos_k = first_pos(index) + column
            if masked:
                near = (pos_k < sink_len) | (pos_k > pos_q - window_len)
                allowed = near if allowed is None else allowed & near
            if allowed is not None:
                block = jnp.where(allowed, block, NEG_FILL)
            start, _ = place(index)
            score_ref[start : start + size, row_at : row_at + row_block] = block
            return jnp.max(block.reshape(size // 8, 8, row_block), axis=0)

        def weighted(index, row_at, top):
            start, size = place(index)
            block = score_ref[start : start + size, row_at : row_at + row_block]
            weights = jnp.exp2(block - top)
            total = jnp.sum(weights.reshape(size // 8, 8, row_block), axis=0)
            acc = lax.dot_general(
                load_values(index),
                weights.astype(bf16),
                (((0,), (0,)), ((), ())),
                preferred_element_type=f32,
            )
            return total, acc

        return len(cached), len(spans), first_pos, scores, weighted

    row_starts = list(range(0, rows, row_block))

    @pl.when(is_retrieval == 1)
    def _():
        cached, spans, _, scores, weighted = build(math.gcd(ctx_dev, 512))
        peer_blocks = list(range(cached // 2))
        own_blocks = list(range(cached // 2, cached + spans))
        running, total, acc = {}, {}, {}

        def first(indices):
            for row_at in row_starts:
                for index in indices:
                    top = scores(index, row_at, False)
                    running[row_at] = jnp.maximum(running[row_at], top) if row_at in running else top

        def second(indices):
            for row_at in row_starts:
                top = jnp.max(running[row_at], axis=0, keepdims=True)
                for index in indices:
                    part_total, part_acc = weighted(index, row_at, top)
                    total[row_at] = total[row_at] + part_total if row_at in total else part_total
                    acc[row_at] = acc[row_at] + part_acc if row_at in acc else part_acc

        first(peer_blocks)
        end_k_start_v()
        first(own_blocks)
        second(peer_blocks)
        end_v()
        second(own_blocks)
        for row_at in row_starts:
            cols = slice(row_at, row_at + row_block)
            top = jnp.max(running[row_at], axis=0, keepdims=True)
            stat_ref[0:8, cols] = jnp.broadcast_to(top, (8, row_block))
            stat_ref[8:16, cols] = total[row_at]
            acc_ref[:, cols] = acc[row_at]

    @pl.when(is_retrieval != 1)
    def _():
        cached, spans, first_pos, scores, weighted = build(key_block)
        peer_blocks = list(range(cached // 2))
        own_blocks = list(range(cached // 2, cached + spans))

        def needed(index):
            pos = first_pos(index)
            return (pos < sink_len) | (pos + key_block - 1 > context - window_len)

        stat_ref[0:8, :] = jnp.full((8, rows), NEG_FILL, f32)
        stat_ref[8:16, :] = jnp.zeros((8, rows), f32)
        acc_ref[...] = jnp.zeros(acc_ref.shape, f32)

        def first(index):
            for row_at in row_starts:
                cols = slice(row_at, row_at + row_block)
                stat_ref[0:8, cols] = jnp.maximum(stat_ref[0:8, cols], scores(index, row_at, True))

        def second(index):
            for row_at in row_starts:
                cols = slice(row_at, row_at + row_block)
                top = jnp.max(stat_ref[0:8, cols], axis=0, keepdims=True)
                total, acc = weighted(index, row_at, top)
                stat_ref[8:16, cols] += total
                acc_ref[:, cols] += acc

        def each(work, indices):
            for index in indices:
                if index < cached:
                    pl.when(needed(index))(functools.partial(work, index))
                else:
                    work(index)

        each(first, peer_blocks)
        end_k_start_v()
        each(first, own_blocks)
        each(second, peer_blocks)
        end_v()
        each(second, own_blocks)
        top = jnp.max(stat_ref[0:8, :], axis=0, keepdims=True)
        stat_ref[0:8, :] = jnp.broadcast_to(top, (8, rows))


def on_device_pairs(q_span, k_span, v_span, k_cache, v_cache, head_list, retrieval, windows, sinks):
    head_count = lax.axis_size("head")
    tok_rows = q_span.shape[0]
    group_width = q_span.shape[1] // KVH
    head_dim = k_cache.shape[2]
    group_heads = group_width // head_dim
    ctx_dev = k_cache.shape[1]
    tokens = tok_rows * head_count
    rows = tokens * group_heads
    swap = [(0, 1), (1, 0)]
    k_own, v_own = k_cache[0], v_cache[0]
    k_peer = lax.ppermute(k_own, "seq", swap)
    v_peer = lax.ppermute(v_own, "seq", swap)
    joined = jnp.concatenate([q_span, k_span, v_span], axis=1)
    joined, *indices = lax.optimization_barrier((joined, head_list, retrieval, windows, sinks))
    table = jnp.concatenate(indices)
    send = pl.pallas_call(
        functools.partial(pack_kernel, group_width=group_width, head_dim=head_dim),
        out_shape=jax.ShapeDtypeStruct((head_count, tok_rows, group_width + 2 * head_dim), jnp.bfloat16),
        in_specs=[SMEM_SPEC, VMEM_SPEC],
        out_specs=VMEM_SPEC,
        compiler_params=pltpu.CompilerParams(vmem_limit_bytes=2**20),
    )(table, joined)
    recv = lax.all_to_all(send, "head", split_axis=0, concat_axis=0, tiled=True)
    recv = recv.reshape(tokens, group_width + 2 * head_dim)
    peer = lax.ppermute(recv, "seq", swap)
    key_block = math.gcd(ctx_dev, 1024)
    row_block = rows
    keys = 2 * ctx_dev + tokens
    acc, stat = pl.pallas_call(
        functools.partial(
            attend_kernel,
            tok_rows=tok_rows,
            group_heads=group_heads,
            head_dim=head_dim,
            key_block=key_block,
            row_block=row_block,
        ),
        out_shape=(
            jax.ShapeDtypeStruct((head_dim, rows), jnp.float32),
            jax.ShapeDtypeStruct((16, rows), jnp.float32),
        ),
        in_specs=[SMEM_SPEC] + [VMEM_SPEC] * 3 + [HBM_SPEC] * 2,
        out_specs=(VMEM_SPEC, VMEM_SPEC),
        scratch_shapes=[
            pltpu.VMEM((ctx_dev, head_dim), jnp.bfloat16),
            pltpu.VMEM((ctx_dev, head_dim), jnp.bfloat16),
            pltpu.VMEM((keys, rows), jnp.float32),
            pltpu.SemaphoreType.DMA((2, 4)),
        ],
        compiler_params=pltpu.CompilerParams(vmem_limit_bytes=51 * 2**20),
    )(table, recv, k_peer, v_peer, k_own, v_own)
    result = pl.pallas_call(
        functools.partial(
            span_kernel,
            tok_rows=tok_rows,
            group_heads=group_heads,
            head_dim=head_dim,
            context=2 * ctx_dev,
        ),
        out_shape=jax.ShapeDtypeStruct((tokens, group_width), jnp.bfloat16),
        in_specs=[SMEM_SPEC] + [VMEM_SPEC] * 4,
        out_specs=VMEM_SPEC,
        compiler_params=pltpu.CompilerParams(vmem_limit_bytes=4 * 2**20),
    )(table, recv, peer, acc, stat)
    result = result.reshape(head_count, tok_rows, group_width)
    back = lax.all_to_all(result, "head", split_axis=0, concat_axis=0, tiled=True)
    return pl.pallas_call(
        unpack_kernel,
        out_shape=jax.ShapeDtypeStruct((tok_rows, KVH * group_width), jnp.bfloat16),
        in_specs=[SMEM_SPEC, VMEM_SPEC],
        out_specs=HBM_SPEC,
        scratch_shapes=[pltpu.SemaphoreType.DMA((head_count,))],
        compiler_params=pltpu.CompilerParams(vmem_limit_bytes=2**20),
    )(table, back)


def solution(mesh):
    on_device = on_device_pairs if mesh.shape["head"] == KVH else on_device_quarters
    in_specs = (
        P(("rep", "head", "seq"), None),
        P(("rep", "head", "seq"), None),
        P(("rep", "head", "seq"), None),
        P(("rep", "head"), "seq", None),
        P(("rep", "head"), "seq", None),
        P("rep"),
        P("rep"),
        P("rep"),
        P("rep"),
    )
    out_specs = P(("rep", "head", "seq"), None)
    return jax.shard_map(
        on_device, mesh=mesh, in_specs=in_specs, out_specs=out_specs, check_vma=False
    )
```

```python
import functools
import math

import jax
import jax.numpy as jnp
from jax import lax
from jax.experimental import pallas as pl
from jax.experimental.pallas import tpu as pltpu
from jax.sharding import PartitionSpec as P

KVH = 8


NEG_FILL = -1e30


def absorb(
    running,
    query_rows,
    query_pos,
    key_rows,
    value_rows,
    key_pos,
    is_retrieval,
    window_len,
    sink_len,
    score_scale,
):
    top_score, totals, weighted = running
    scores = jnp.dot(query_rows, key_rows.T, preferred_element_type=jnp.float32) * score_scale
    allowed = (key_pos[None, :] <= query_pos[:, None]) & (
        (is_retrieval == 1)
        | (key_pos[None, :] < sink_len)
        | (key_pos[None, :] > query_pos[:, None] - window_len)
    )
    block_top = jnp.max(jnp.where(allowed, scores, NEG_FILL), axis=1)
    new_top = jnp.maximum(top_score, block_top)
    weights = jnp.where(allowed, jnp.exp(scores - new_top[:, None]), 0.0)
    rescale = jnp.exp(top_score - new_top)
    totals = totals * rescale + jnp.sum(weights, axis=1)
    weighted = weighted * rescale[:, None] + jnp.dot(
        weights.astype(jnp.bfloat16), value_rows, preferred_element_type=jnp.float32
    )
    return (new_top, totals, weighted)


def finish_rows(received, spread, head_list, tok_rows, head_dim):
    top_score, totals, weighted = received
    group_heads = top_score.shape[-1]
    top_score = top_score.reshape(KVH, spread, tok_rows, group_heads)
    totals = totals.reshape(KVH, spread, tok_rows, group_heads)
    weighted = weighted.reshape(KVH, spread, tok_rows, group_heads, head_dim)
    overall = jnp.max(top_score, axis=1, keepdims=True)
    factor = jnp.exp(top_score - overall)
    summed = jnp.sum(totals * factor, axis=1)
    combined = jnp.sum(weighted * factor[..., None], axis=1)
    result = combined / summed[..., None]
    matches = (head_list[:, None] == jnp.arange(KVH, dtype=jnp.int32)[None, :]).astype(jnp.int32)
    inverse = jnp.sum(jnp.arange(KVH, dtype=jnp.int32)[:, None] * matches, axis=0)
    by_group = jnp.take(result, inverse, axis=0)
    return (
        by_group.transpose(1, 0, 2, 3)
        .reshape(tok_rows, KVH * group_heads * head_dim)
        .astype(jnp.bfloat16)
    )


def on_device_quarters(q_span, k_span, v_span, k_cache, v_cache, head_list, retrieval, windows, sinks):
    head_count = lax.axis_size("head")
    pair_count = lax.axis_size("seq")
    quarters = head_count // KVH
    tok_rows = q_span.shape[0]
    group_width = q_span.shape[1] // KVH
    head_dim = k_cache.shape[2]
    group_heads = group_width // head_dim
    ctx_dev = k_cache.shape[1]
    total_q = tok_rows * head_count * pair_count
    context = ctx_dev * pair_count * quarters
    head_at = lax.axis_index("head")
    pair_at = lax.axis_index("seq")
    slot_index = head_at // quarters
    quarter = head_at % quarters
    kv_group = jnp.take(head_list, slot_index)
    q_groups = q_span.reshape(tok_rows, KVH, group_width)
    kv_groups = jnp.concatenate(
        [k_span.reshape(tok_rows, KVH, head_dim), v_span.reshape(tok_rows, KVH, head_dim)], axis=2
    )
    targets = jnp.take(head_list, jnp.arange(head_count * pair_count) // pair_count // quarters)
    q_send = jnp.take(q_groups, targets, axis=1)
    kv_send = jnp.take(kv_groups, targets, axis=1)
    q_recv, kv_recv = (
        lax.all_to_all(q_send, ("head", "seq"), split_axis=1, concat_axis=0, tiled=True),
        lax.all_to_all(kv_send, ("head", "seq"), split_axis=1, concat_axis=0, tiled=True),
    )
    queries = q_recv.reshape(total_q, group_width)
    span_kv = kv_recv.reshape(total_q, 2 * head_dim)
    query_rows = queries.reshape(total_q * group_heads, head_dim)
    query_pos = context + jnp.arange(total_q * group_heads, dtype=jnp.int32) // group_heads
    is_retrieval = jnp.take(retrieval, kv_group)
    window_len = jnp.take(windows, kv_group)
    sink_len = jnp.take(sinks, kv_group)
    score_scale = 1.0 / math.sqrt(head_dim)
    row_total = total_q * group_heads
    running = (
        jnp.full((row_total,), NEG_FILL, jnp.float32),
        jnp.zeros((row_total,), jnp.float32),
        jnp.zeros((row_total, head_dim), jnp.float32),
    )
    key_block = min(512, ctx_dev)
    segment = quarter * pair_count + pair_at
    first_key = segment * ctx_dev
    cache_keys = k_cache[0]
    cache_values = v_cache[0]

    def key_step(step_index, state):
        start = step_index * key_block
        key_rows = lax.dynamic_slice_in_dim(cache_keys, start, key_block, 0)
        value_rows = lax.dynamic_slice_in_dim(cache_values, start, key_block, 0)
        key_pos = first_key + start + jnp.arange(key_block, dtype=jnp.int32)
        return absorb(
            state,
            query_rows,
            query_pos,
            key_rows,
            value_rows,
            key_pos,
            is_retrieval,
            window_len,
            sink_len,
            score_scale,
        )

    running = lax.fori_loop(0, ctx_dev // key_block, key_step, running)
    span_piece = total_q // (quarters * pair_count)
    span_start = segment * span_piece
    span_rows = lax.dynamic_slice_in_dim(span_kv, span_start, span_piece, 0)
    span_pos = context + span_start + jnp.arange(span_piece, dtype=jnp.int32)
    top_score, totals, weighted = absorb(
        running,
        query_rows,
        query_pos,
        span_rows[:, :head_dim],
        span_rows[:, head_dim:],
        span_pos,
        is_retrieval,
        window_len,
        sink_len,
        score_scale,
    )
    received = (
        lax.all_to_all(
            top_score.reshape(head_count * pair_count, tok_rows, group_heads),
            ("head", "seq"),
            split_axis=0,
            concat_axis=0,
            tiled=True,
        ),
        lax.all_to_all(
            totals.reshape(head_count * pair_count, tok_rows, group_heads),
            ("head", "seq"),
            split_axis=0,
            concat_axis=0,
            tiled=True,
        ),
        lax.all_to_all(
            weighted.reshape(head_count * pair_count, tok_rows, group_width),
            ("head", "seq"),
            split_axis=0,
            concat_axis=0,
            tiled=True,
        ),
    )
    spread = quarters * pair_count
    return finish_rows(received, spread, head_list, tok_rows, head_dim)


VMEM_SPEC = pl.BlockSpec(memory_space=pltpu.VMEM)
HBM_SPEC = pl.BlockSpec(memory_space=pltpu.HBM)
SMEM_SPEC = pl.BlockSpec(memory_space=pltpu.SMEM)


def pack_kernel(head_ref, in_ref, out_ref, *, group_width, head_dim):
    q_width = KVH * group_width
    q_ref = in_ref.at[:, :q_width]
    k_ref = in_ref.at[:, q_width : q_width + KVH * head_dim]
    v_ref = in_ref.at[:, q_width + KVH * head_dim :]
    for slot in range(out_ref.shape[0]):
        group = head_ref[slot]
        q_start = pl.multiple_of(group * group_width, 128)
        kv_start = pl.multiple_of(group * head_dim, 128)
        out_ref[slot, :, :group_width] = q_ref[:, pl.ds(q_start, group_width)]
        out_ref[slot, :, group_width : group_width + head_dim] = k_ref[:, pl.ds(kv_start, head_dim)]
        out_ref[slot, :, group_width + head_dim :] = v_ref[:, pl.ds(kv_start, head_dim)]


def unpack_kernel(head_ref, in_ref, out_ref, sems):
    width = in_ref.shape[2]
    copies = []
    for slot in range(in_ref.shape[0]):
        start = pl.multiple_of(head_ref[slot] * width, 128)
        copies.append(
            pltpu.make_async_copy(in_ref.at[slot], out_ref.at[:, pl.ds(start, width)], sems.at[slot])
        )
    for copy in copies:
        copy.start()
    for copy in copies:
        copy.wait()


def look_up(table_ref):
    kv_group = table_ref[lax.axis_index("head")]
    return (table_ref[part * KVH + kv_group] for part in (1, 2, 3))


def stack_queries(recv_ref, group_heads, head_dim):
    scale = math.log2(math.e) / math.sqrt(head_dim)
    queries = jnp.concatenate(
        [recv_ref[:, k * head_dim : (k + 1) * head_dim] for k in range(group_heads)], axis=0
    )
    scaled = queries.astype(jnp.float32) * scale
    high = scaled.astype(jnp.bfloat16)
    low = (scaled - high.astype(jnp.float32)).astype(jnp.bfloat16)
    return jnp.concatenate([high, low], axis=1)


def span_kernel(
    table_ref,
    recv_ref,
    peer_ref,
    acc_ref,
    stat_ref,
    out_ref,
    *,
    tok_rows,
    group_heads,
    head_dim,
    context,
):
    f32, bf16 = jnp.float32, jnp.bfloat16
    pair_at = lax.axis_index("seq")
    is_retrieval, window_len, sink_len = look_up(table_ref)
    window_len = jnp.where(is_retrieval == 1, 2**30, window_len)
    tokens = recv_ref.shape[0]
    rows = tokens * group_heads
    group_width = group_heads * head_dim
    queries = stack_queries(recv_ref, group_heads, head_dim)

    def token_pos(index, pair):
        return context + ((index // tok_rows) * 2 + pair) * tok_rows + index % tok_rows

    query_pos = token_pos(lax.broadcasted_iota(jnp.int32, (1, rows), 1) % tokens, pair_at)
    key_pos = token_pos(lax.broadcasted_iota(jnp.int32, (tokens, 1), 0), 1 - pair_at)
    keys = peer_ref[:, group_width : group_width + head_dim]
    values = peer_ref[:, group_width + head_dim : group_width + 2 * head_dim]
    block = lax.dot_general(
        jnp.concatenate([keys, keys], axis=1),
        queries,
        (((1,), (1,)), ((), ())),
        preferred_element_type=f32,
    )
    allowed = (key_pos <= query_pos) & ((key_pos < sink_len) | (key_pos > query_pos - window_len))
    block = jnp.where(allowed, block, NEG_FILL)
    old_top = stat_ref[0:1, :]
    top = jnp.maximum(old_top, jnp.max(block, axis=0, keepdims=True))
    factor = jnp.exp2(old_top - top)
    weights = jnp.exp2(block - top)
    total = jnp.sum(stat_ref[8:16, :], axis=0, keepdims=True) * factor
    total = total + jnp.sum(weights, axis=0, keepdims=True)
    acc = acc_ref[...] * factor + lax.dot_general(
        values, weights.astype(bf16), (((0,), (0,)), ((), ())), preferred_element_type=f32
    )
    result = (acc / total).T.astype(bf16)
    for head in range(group_heads):
        out_ref[:, head * head_dim : (head + 1) * head_dim] = result[head * tokens : (head + 1) * tokens]


def attend_kernel(
    table_ref,
    recv_ref,
    k_peer,
    v_peer,
    k_source,
    v_source,
    acc_ref,
    stat_ref,
    k_own,
    v_own,
    score_ref,
    own_sem,
    *,
    tok_rows,
    group_heads,
    head_dim,
    key_block,
    row_block,
):

    def own_copies(source, target, which):
        size = source.shape[0] // own_sem.shape[1]
        return [
            pltpu.make_async_copy(
                source.at[pl.ds(chunk * size, size)],
                target.at[pl.ds(chunk * size, size)],
                own_sem.at[which, chunk],
            )
            for chunk in range(own_sem.shape[1])
        ]

    k_copies = own_copies(k_source, k_own, 0)
    v_copies = own_copies(v_source, v_own, 1)
    for copy in k_copies:
        copy.start()

    def end_k_start_v():
        for copy in k_copies:
            copy.wait()
        for copy in v_copies:
            copy.start()

    def end_v():
        for copy in v_copies:
            copy.wait()

    pair_at = lax.axis_index("seq")
    is_retrieval, window_len, sink_len = look_up(table_ref)
    tokens = recv_ref.shape[0]
    rows = tokens * group_heads
    group_width = group_heads * head_dim
    ctx_dev = k_own.shape[0]
    context = 2 * ctx_dev
    f32, bf16 = jnp.float32, jnp.bfloat16
    def token_pos(index, pair):
        return context + ((index // tok_rows) * 2 + pair) * tok_rows + index % tok_rows

    queries = stack_queries(recv_ref, group_heads, head_dim)
    row_token = lax.broadcasted_iota(jnp.int32, (1, rows), 1) % tokens
    query_pos = token_pos(row_token, pair_at)

    span_k = pl.ds(group_width, head_dim)
    span_v = pl.ds(group_width + head_dim, head_dim)

    def build(key_block):
        cached, spans = [], []
        for k_ref, v_ref, pair in ((k_peer, v_peer, 1 - pair_at), (k_own, v_own, pair_at)):
            for start in range(0, ctx_dev, key_block):
                cached.append((k_ref, v_ref, start, key_block, pair))
        spans.append((recv_ref, pair_at))

        def load_keys(index):
            if index < len(cached):
                k_ref, _, start, size, _ = cached[index]
                return k_ref[start : start + size, :]
            return spans[index - len(cached)][0][:, span_k]

        def load_values(index):
            if index < len(cached):
                _, v_ref, start, size, _ = cached[index]
                return v_ref[start : start + size, :]
            return spans[index - len(cached)][0][:, span_v]

        def place(index):
            if index < len(cached):
                return index * key_block, key_block
            return len(cached) * key_block + (index - len(cached)) * tokens, tokens

        def first_pos(index):
            _, _, start, _, pair = cached[index]
            return pair * ctx_dev + start

        def scores(index, row_at, masked):
            keys = load_keys(index)
            keys = jnp.concatenate([keys, keys], axis=1)
            block = lax.dot_general(
                keys,
                queries[row_at : row_at + row_block],
                (((1,), (1,)), ((), ())),
                preferred_element_type=f32,
            )
            size = block.shape[0]
            pos_q = query_pos[:, row_at : row_at + row_block]
            column = lax.broadcasted_iota(jnp.int32, (size, 1), 0)
            allowed = None
            if index >= len(cached):
                pos_k = token_pos(column, spans[index - len(cached)][1])
                allowed = pos_k <= pos_q
            else:
                pos_k = first_pos(index) + column
            if masked:
                near = (pos_k < sink_len) | (pos_k > pos_q - window_len)
                allowed = near if allowed is None else allowed & near
            if allowed is not None:
                block = jnp.where(allowed, block, NEG_FILL)
            start, _ = place(index)
            score_ref[start : start + size, row_at : row_at + row_block] = block
            return jnp.max(block.reshape(size // 8, 8, row_block), axis=0)

        def weighted(index, row_at, top):
            start, size = place(index)
            block = score_ref[start : start + size, row_at : row_at + row_block]
            weights = jnp.exp2(block - top)
            total = jnp.sum(weights.reshape(size // 8, 8, row_block), axis=0)
            acc = lax.dot_general(
                load_values(index),
                weights.astype(bf16),
                (((0,), (0,)), ((), ())),
                preferred_element_type=f32,
            )
            return total, acc

        return len(cached), len(spans), first_pos, scores, weighted

    row_starts = list(range(0, rows, row_block))

    @pl.when(is_retrieval == 1)
    def _():
        cached, spans, _, scores, weighted = build(math.gcd(ctx_dev, 512))
        peer_blocks = list(range(cached // 2))
        own_blocks = list(range(cached // 2, cached + spans))
        running, total, acc = {}, {}, {}

        def first(indices):
            for row_at in row_starts:
                for index in indices:
                    top = scores(index, row_at, False)
                    running[row_at] = jnp.maximum(running[row_at], top) if row_at in running else top

        def second(indices):
            for row_at in row_starts:
                top = jnp.max(running[row_at], axis=0, keepdims=True)
                for index in indices:
                    part_total, part_acc = weighted(index, row_at, top)
                    total[row_at] = total[row_at] + part_total if row_at in total else part_total
                    acc[row_at] = acc[row_at] + part_acc if row_at in acc else part_acc

        first(peer_blocks)
        end_k_start_v()
        first(own_blocks)
        second(peer_blocks)
        end_v()
        second(own_blocks)
        for row_at in row_starts:
            cols = slice(row_at, row_at + row_block)
            top = jnp.max(running[row_at], axis=0, keepdims=True)
            stat_ref[0:8, cols] = jnp.broadcast_to(top, (8, row_block))
            stat_ref[8:16, cols] = total[row_at]
            acc_ref[:, cols] = acc[row_at]

    @pl.when(is_retrieval != 1)
    def _():
        cached, spans, first_pos, scores, weighted = build(key_block)
        peer_blocks = list(range(cached // 2))
        own_blocks = list(range(cached // 2, cached + spans))

        def needed(index):
            pos = first_pos(index)
            return (pos < sink_len) | (pos + key_block - 1 > context - window_len)

        stat_ref[0:8, :] = jnp.full((8, rows), NEG_FILL, f32)
        stat_ref[8:16, :] = jnp.zeros((8, rows), f32)
        acc_ref[...] = jnp.zeros(acc_ref.shape, f32)

        def first(index):
            for row_at in row_starts:
                cols = slice(row_at, row_at + row_block)
                stat_ref[0:8, cols] = jnp.maximum(stat_ref[0:8, cols], scores(index, row_at, True))

        def second(index):
            for row_at in row_starts:
                cols = slice(row_at, row_at + row_block)
                top = jnp.max(stat_ref[0:8, cols], axis=0, keepdims=True)
                total, acc = weighted(index, row_at, top)
                stat_ref[8:16, cols] += total
                acc_ref[:, cols] += acc

        def each(work, indices):
            for index in indices:
                if index < cached:
                    pl.when(needed(index))(functools.partial(work, index))
                else:
                    work(index)

        each(first, peer_blocks)
        end_k_start_v()
        each(first, own_blocks)
        each(second, peer_blocks)
        end_v()
        each(second, own_blocks)
        top = jnp.max(stat_ref[0:8, :], axis=0, keepdims=True)
        stat_ref[0:8, :] = jnp.broadcast_to(top, (8, rows))


def on_device_pairs(q_span, k_span, v_span, k_cache, v_cache, head_list, retrieval, windows, sinks):
    head_count = lax.axis_size("head")
    tok_rows = q_span.shape[0]
    group_width = q_span.shape[1] // KVH
    head_dim = k_cache.shape[2]
    group_heads = group_width // head_dim
    ctx_dev = k_cache.shape[1]
    tokens = tok_rows * head_count
    rows = tokens * group_heads
    swap = [(0, 1), (1, 0)]
    k_own, v_own = k_cache[0], v_cache[0]
    k_peer = lax.ppermute(k_own, "seq", swap)
    v_peer = lax.ppermute(v_own, "seq", swap)
    joined = jnp.concatenate([q_span, k_span, v_span], axis=1)
    joined, *indices = lax.optimization_barrier((joined, head_list, retrieval, windows, sinks))
    table = jnp.concatenate(indices)
    send = pl.pallas_call(
        functools.partial(pack_kernel, group_width=group_width, head_dim=head_dim),
        out_shape=jax.ShapeDtypeStruct((head_count, tok_rows, group_width + 2 * head_dim), jnp.bfloat16),
        in_specs=[SMEM_SPEC, VMEM_SPEC],
        out_specs=VMEM_SPEC,
        compiler_params=pltpu.CompilerParams(vmem_limit_bytes=2**20),
    )(table, joined)
    recv = lax.all_to_all(send, "head", split_axis=0, concat_axis=0, tiled=True)
    recv = recv.reshape(tokens, group_width + 2 * head_dim)
    peer = lax.ppermute(recv, "seq", swap)
    key_block = math.gcd(ctx_dev, 512)
    row_block = 256
    keys = 2 * ctx_dev + tokens
    acc, stat = pl.pallas_call(
        functools.partial(
            attend_kernel,
            tok_rows=tok_rows,
            group_heads=group_heads,
            head_dim=head_dim,
            key_block=key_block,
            row_block=row_block,
        ),
        out_shape=(
            jax.ShapeDtypeStruct((head_dim, rows), jnp.float32),
            jax.ShapeDtypeStruct((16, rows), jnp.float32),
        ),
        in_specs=[SMEM_SPEC] + [VMEM_SPEC] * 3 + [HBM_SPEC] * 2,
        out_specs=(VMEM_SPEC, VMEM_SPEC),
        scratch_shapes=[
            pltpu.VMEM((ctx_dev, head_dim), jnp.bfloat16),
            pltpu.VMEM((ctx_dev, head_dim), jnp.bfloat16),
            pltpu.VMEM((keys, rows), jnp.float32),
            pltpu.SemaphoreType.DMA((2, 4)),
        ],
        compiler_params=pltpu.CompilerParams(vmem_limit_bytes=51 * 2**20),
    )(table, recv, k_peer, v_peer, k_own, v_own)
    result = pl.pallas_call(
        functools.partial(
            span_kernel,
            tok_rows=tok_rows,
            group_heads=group_heads,
            head_dim=head_dim,
            context=2 * ctx_dev,
        ),
        out_shape=jax.ShapeDtypeStruct((tokens, group_width), jnp.bfloat16),
        in_specs=[SMEM_SPEC] + [VMEM_SPEC] * 4,
        out_specs=VMEM_SPEC,
        compiler_params=pltpu.CompilerParams(vmem_limit_bytes=4 * 2**20),
    )(table, recv, peer, acc, stat)
    result = result.reshape(head_count, tok_rows, group_width)
    back = lax.all_to_all(result, "head", split_axis=0, concat_axis=0, tiled=True)
    return pl.pallas_call(
        unpack_kernel,
        out_shape=jax.ShapeDtypeStruct((tok_rows, KVH * group_width), jnp.bfloat16),
        in_specs=[SMEM_SPEC, VMEM_SPEC],
        out_specs=HBM_SPEC,
        scratch_shapes=[pltpu.SemaphoreType.DMA((head_count,))],
        compiler_params=pltpu.CompilerParams(vmem_limit_bytes=2**20),
    )(table, back)


def solution(mesh):
    on_device = on_device_pairs if mesh.shape["head"] == KVH else on_device_quarters
    in_specs = (
        P(("rep", "head", "seq"), None),
        P(("rep", "head", "seq"), None),
        P(("rep", "head", "seq"), None),
        P(("rep", "head"), "seq", None),
        P(("rep", "head"), "seq", None),
        P("rep"),
        P("rep"),
        P("rep"),
        P("rep"),
    )
    out_specs = P(("rep", "head", "seq"), None)
    return jax.shard_map(
        on_device, mesh=mesh, in_specs=in_specs, out_specs=out_specs, check_vma=False
    )
```
